32 devices in a mesh: group: 2 (over x), replica: 16 (over z, y, core).
Axes of the slice: x: 2, y: 2, z: 4, core: 2. Of those that a mesh axis runs over, the one named last changes fastest.
Arguments:
- block_in: bfloat16 [16, 1024, 1024], P('replica', 'group'), may hold values from -6 to 6
- attn_gain: bfloat16 [1024], P('group'), may hold values from 0.5 to 1.5
- query_weight: bfloat16 [1024, 1024], P('group'), may hold values from -0.25 to 0.25
- key_weight: bfloat16 [1024, 512], P('group'), may hold values from -0.25 to 0.25
- value_weight: bfloat16 [1024, 512], P('group'), may hold values from -0.1875 to 0.1875
- out_weight: bfloat16 [1024, 1024], P('group'), may hold values from -1.5 to 1.5
- ffn_gain: bfloat16 [1024], P('group'), may hold values from 0.5 to 1.5
- router_weight: bfloat16 [1024, 16], P('group'), may hold values from -0.09375 to 0.09375
- expert_in: bfloat16 [16, 1024, 1024], P('group'), may hold values from -0.1875 to 0.1875
- expert_out: bfloat16 [16, 1024, 512], P('group'), may hold values from -1.5 to 1.5
- routes: int32 [16, 1024, 8], P('replica', 'group'), may hold values from 0 to 15, all different within a row; in each aligned block of 512 rows (0 to 511, 512 to 1023, ..., all dimensions but the last counted through in order) at most 384 rows name the same one
- prefix: int32 [16], P('replica'), may hold values from 102 to 512, as said below
- cotangent: bfloat16 [16, 1024, 1024], P('replica', 'group'), may hold values from -6 to 6
Outputs:
- block_out: bfloat16 [16, 1024, 1024], P('replica', 'group')
- input_grad: float32 [16, 1024, 1024], P('replica', 'group')
- attn_gain_grad: float32 [1024], P(('group', 'replica'))
- query_grad: float32 [1024, 1024], P(('group', 'replica'))
- key_grad: float32 [1024, 512], P(('group', 'replica'))
- value_grad: float32 [1024, 512], P(('group', 'replica'))
- out_grad: float32 [1024, 1024], P(None, ('group', 'replica'))
- ffn_gain_grad: float32 [1024], P(('group', 'replica'))
- router_grad: float32 [1024, 16], P(('group', 'replica'))
- expert_in_grad: float32 [16, 1024, 1024], P(None, ('group', 'replica'))
- expert_out_grad: float32 [16, 1024, 512], P(None, ('group', 'replica'))
The draws below stay inside these ranges and needn't reach their ends.
Inputs may be any that keep to these rules, and one draw needn't show every extreme that they name: `routes`: each token names 8 different experts. Among the 512 tokens of one sequence block no expert is named more than 384 times, and in every draw some expert is named exactly 384 times by some block. Some sequence has a prefix of exactly 512.
All inputs are finite; a program needn't handle non-finite values.
Results may differ from the reference program's by a relative error of at most 0.017.
The reference program's roundings to bfloat16 on the way count: a program that leaves them out, or rounds other values in their place, can miss the bound.
Values may be sent and summed in bfloat16 or wider, within the bound.
No kernel may reach another device: no remote copies, remote signals or barrier semaphores. Data moves between devices by JAX's collectives and lax.ppermute only.
A program may use at most 448 MiB of HBM per device.

```python
import math
import jax
import jax.numpy as jnp
import numpy as np
from jax import lax

D = 1024
HEADS = 16
KV_HEADS = 8
HEAD = 64
FF = 512
TOP = 8
EXPERTS = 16
TOK_DEV = 512
LENGTH = 1024
SEQS = 16
CAP = 384
N_GROUP = 2


def draw_prefix(key, part):
    first_key, second_key = jax.random.split(key)
    lengths = jax.random.randint(first_key, (SEQS,), LENGTH // 10, LENGTH // 2 + 1)
    chosen = jax.random.randint(second_key, (), 0, SEQS)
    return jnp.where(jnp.arange(SEQS) == chosen, LENGTH // 2, lengths).astype(jnp.int32)


def strengthened(result, rng, source, target, parts, factor):
    owner, partner = [(jnp.arange(result.shape[position]) // (result.shape[position] // parts)).reshape([-1 if axis == position else 1 for axis in range(result.ndim)]) for position in (source, target)]
    chosen = jax.random.permutation(rng, parts)[partner]
    strong = (owner == chosen) | (owner == (partner + parts // 2) % parts)
    return jnp.where(strong, factor * result, result)


def steps_of(key, extent, cuts, smallest, top_value):
    level = 1.0
    for position, blocks in cuts:
        heights = jax.random.uniform(jax.random.fold_in(jax.random.fold_in(key, 6), position), (blocks,), jnp.float32, smallest / len(cuts), top_value / len(cuts))
        level = level * jnp.repeat(jnp.exp(heights), extent[position] // blocks).reshape((-1,) + (1,) * (len(extent) - 1 - position))
    return level


def routed_block(key, own, number, rows, number_of, top, limit, lean):
    order = jax.random.permutation(key, number_of)
    heavy_load, common = load_shares(number_of, rows * top, limit, lean, True), load_shares(number_of, rows * top, limit, lean, False)
    places = jnp.arange(number_of)

    def named(tallies, turn):
        used = int((tallies > 0).sum())
        fixed = max(1, used // 4)
        passed = fixed + (places - fixed + turn * (used - fixed)) % max(1, number_of - fixed)
        return jnp.zeros((number_of,), jnp.int32).at[order[jnp.where(places < fixed, places, passed)]].set(jnp.asarray(tallies, jnp.int32))

    tallies = jnp.where(number % 4 == 0, named(heavy_load, number // 4), named(common, number - number // 4 - 1))
    mixed = jax.random.permutation(jax.random.fold_in(own, 3), number_of)
    source_of, sink = mixed[0:number_of // 2 * 2:2], mixed[1:number_of // 2 * 2:2]
    slack = jnp.minimum(tallies[source_of] - 1, limit - tallies[sink]) // 2
    slack = jnp.where((source_of == order[0]) | (sink == order[0]) | (tallies[sink] == 0), 0, jnp.maximum(slack, 0))
    passed = jax.random.randint(jax.random.fold_in(own, 4), (number_of // 2,), 0, 1 << 20) % (slack + 1)
    tallies = tallies.at[source_of].add(-passed).at[sink].add(passed)
    labels = jnp.searchsorted(jnp.cumsum(tallies), jnp.arange(rows * top), side="right").astype(jnp.int32)
    listing = labels.reshape(top, rows).T
    listing = listing[jax.random.permutation(jax.random.fold_in(own, 1), rows)]
    turn = jax.random.randint(jax.random.fold_in(own, 2), (rows, 1), 0, top)
    return jnp.take_along_axis(listing, (jnp.arange(top)[None, :] + turn) % top, axis=1)


def load_shares(count, total, limit, slope, full):
    loads = [(1 << 20) // math.isqrt(grade ** slope) + 1 for grade in range(1, count + 1)]
    largest = limit if full else min(limit, max(-(-total // count), total * loads[0] // sum(loads)))
    least = 1 if total - largest >= count - 1 else 0
    counts, spare = [largest] + [least] * (count - 1), total - largest - least * (count - 1)
    while spare > 0:
        candidates = [i for i in range(1, count) if counts[i] < largest] or [i for i in range(1, count) if counts[i] < limit]
        pool, left = sum([loads[i] for i in candidates]), spare
        for i in candidates:
            addition = min(limit - counts[i], max(1, left * loads[i] // pool), spare)
            counts[i] = counts[i] + addition
            spare = spare - addition
    return np.array(counts)


def centred(own_key, shape, spread, bound, cuts=(), kind=jnp.bfloat16):
    values = jax.random.normal(own_key, shape, jnp.float32) * spread
    if len(cuts) > 0:
        values = steps_of(own_key, shape, cuts, -0.22, 0.18) * values
    return jnp.clip(values, min=-bound, max=bound).astype(kind)


def bell_draw_with(rng, extent, spread, reach, cuts, heavy, held_as=jnp.bfloat16):
    array = spread * jax.random.normal(rng, extent, jnp.float32)
    if cuts:
        array = array * steps_of(rng, extent, cuts, -0.22, 0.18)
    return jnp.clip(strengthened(array, jax.random.fold_in(rng, 3), *heavy), -reach, reach).astype(held_as)


def setup_inputs(seed: int = 0) -> dict:
    splits = jax.random.split(jax.random.key(seed), 14)
    block_in = centred(splits[0], (SEQS, LENGTH, D), 1.0, 6.0, ((0, 16), (1, 2)))
    attn_gain = jnp.clip(1.0 + 0.1 * jax.random.normal(splits[1], (D,), jnp.float32), 0.5, 1.5).astype(jnp.bfloat16)
    query_weight = centred(splits[2], (D, HEADS * HEAD), (D // 2) ** -0.5, 0.25, ((0, 2),))
    key_weight = centred(splits[3], (D, KV_HEADS * HEAD), (D // 2) ** -0.5, 0.25, ((0, 2),))
    value_weight = centred(splits[4], (D, KV_HEADS * HEAD), D ** -0.5, 0.1875, ((0, 2),))
    out_weight = centred(splits[5], (HEADS * HEAD, D), (HEADS * HEAD // 64) ** -0.5, 1.5, ((0, 2),))
    ffn_gain = jnp.clip(1.0 + 0.1 * jax.random.normal(splits[6], (D,), jnp.float32), 0.5, 1.5).astype(jnp.bfloat16)
    router_weight = centred(splits[7], (D, EXPERTS), (4 * D) ** -0.5, 0.09375, ((0, 2),))
    expert_in = centred(splits[8], (EXPERTS, D, 2 * FF), D ** -0.5, 0.1875, ((0, 2),))
    expert_out = centred(splits[9], (EXPERTS, D, FF), (FF // 32) ** -0.5, 1.5, ((0, 2),))
    routes_keys = jax.random.split(jax.random.fold_in(splits[10], 1), SEQS * LENGTH // TOK_DEV)
    routes_turns = jax.random.permutation(jax.random.fold_in(splits[10], 3), SEQS * LENGTH // TOK_DEV)
    routes = jax.vmap(lambda own, number: routed_block(jax.random.fold_in(splits[10], 2), own, number, TOK_DEV, EXPERTS, TOP, CAP, 2))(routes_keys, routes_turns).reshape((SEQS, LENGTH, TOP))
    prefix = draw_prefix(jax.random.fold_in(splits[13], 71), 0)
    cotangent = bell_draw_with(splits[12], (SEQS, LENGTH, D), 1.0, 6.0, ((0, 16), (1, 2)), (0, 2, 16, 2.0))
    return {"block_in": block_in, "attn_gain": attn_gain, "query_weight": query_weight, "key_weight": key_weight, "value_weight": value_weight, "out_weight": out_weight, "ffn_gain": ffn_gain, "router_weight": router_weight, "expert_in": expert_in, "expert_out": expert_out, "routes": routes, "prefix": prefix, "cotangent": cotangent}


EPSILON = 1e-06
THETA_BASE = 10000.0
MASKED = -1e+30
HIGHEST = lax.Precision.HIGHEST

@jax.custom_vjp
def low(v):
    return lax.optimization_barrier(v.astype(jnp.bfloat16)).astype(jnp.float32)

@jax.custom_vjp
def low_back(v):
    return v

def low_keep(v):
    return (low(v), None)

def low_pass(kept, grad):
    return (grad,)

def back_keep(v):
    return (v, None)

def back_low(kept, grad):
    return (low(grad),)
low.defvjp(low_keep, low_pass)
low_back.defvjp(back_keep, back_low)

def normalize(values, gain):
    return values * lax.rsqrt(lax.optimization_barrier(jnp.mean(values * values, -1, keepdims=True)) + EPSILON) * gain

def rotate(values, positions):
    half_head = HEAD // 2
    frequency = THETA_BASE ** (-jnp.arange(half_head, dtype=jnp.float32) * 2.0 / HEAD)
    angles = positions.astype(jnp.float32)[:, None] * frequency[None, :]
    cosine = jnp.cos(angles)[:, None, :]
    sine_table = jnp.sin(angles)[:, None, :]
    first_half = values[..., :half_head]
    second_half = values[..., half_head:]
    return jnp.concatenate([first_half * cosine - second_half * sine_table, second_half * cosine + first_half * sine_table], -1)

def attend(queries, keys, values, prefix_len):
    rows_block = min(LENGTH, 512)
    groups = HEADS // KV_HEADS
    key_positions = jnp.arange(LENGTH, dtype=jnp.int32)
    score_scale = 1.0 / math.sqrt(HEAD)

    def one_block(block_index):
        row_start = (block_index * rows_block).astype(jnp.int32)
        query_block = lax.dynamic_slice_in_dim(queries, row_start, rows_block, 0).reshape(rows_block, KV_HEADS, groups, HEAD)
        query_pos = row_start + jnp.arange(rows_block, dtype=jnp.int32)
        scores = jnp.einsum('qkgd,jkd->kgqj', query_block, keys, precision=HIGHEST) * score_scale
        visible = (key_positions[None, :] <= query_pos[:, None]) | (key_positions[None, :] < prefix_len)
        scores = low_back(jnp.where(visible, scores, MASKED))
        probability = jax.nn.softmax(scores, -1)
        attended = jnp.einsum('kgqj,jkd->qkgd', low(probability), values, precision=HIGHEST)
        return attended.reshape(rows_block, HEADS * HEAD)
    blocks = lax.map(jax.checkpoint(one_block), jnp.arange(LENGTH // rows_block, dtype=jnp.int32))
    return blocks.reshape(LENGTH, HEADS * HEAD)

def experts(rows, gate_probs, token_routes, expert_in, expert_out):
    expert_ids = jnp.arange(EXPERTS, dtype=jnp.int32)
    member = (token_routes[:, :, None] == expert_ids[None, None, :]).astype(jnp.int32)
    per_token = lax.optimization_barrier(jnp.sum(member, 1)).astype(jnp.int32)
    before = (jnp.cumsum(per_token, 0) - per_token).astype(jnp.int32)
    slot_index = lax.optimization_barrier(jnp.sum(member * before[:, None, :], 2)).astype(jnp.int32)
    flat_slot = (token_routes * CAP + slot_index).reshape(-1).astype(jnp.int32)
    token_ids = jnp.repeat(jnp.arange(TOK_DEV, dtype=jnp.int32), TOP)
    source = jnp.zeros((EXPERTS * CAP,), jnp.int32).at[flat_slot].set(token_ids)
    filled = jnp.zeros((EXPERTS * CAP,), jnp.float32).at[flat_slot].set(1.0)
    buffer = (rows[source] * filled[:, None]).reshape(EXPERTS, CAP, D)
    gate_up = low_back(jnp.einsum('ecd,edf->ecf', buffer, expert_in, precision=HIGHEST))
    hidden = low(jax.nn.silu(gate_up[..., :FF]) * gate_up[..., FF:])
    outputs = low_back(jnp.einsum('ecf,edf->ecd', hidden, expert_out, precision=HIGHEST))
    picked = outputs.reshape(EXPERTS * CAP, D)[flat_slot].reshape(TOK_DEV, TOP, D)
    return lax.optimization_barrier(jnp.sum(gate_probs[:, :, None] * picked, 1))

def block_forward(inputs, attn_gain, query_weight, key_weight, value_weight, out_weight, ffn_gain, router_weight, expert_in, expert_out, token_routes, prefix_len):
    positions = jnp.arange(LENGTH, dtype=jnp.int32)
    normed_attn = low(normalize(inputs, attn_gain))
    query_pre = low_back(jnp.dot(normed_attn, query_weight, precision=HIGHEST)).reshape(LENGTH, HEADS, HEAD)
    key_pre = low_back(jnp.dot(normed_attn, key_weight, precision=HIGHEST)).reshape(LENGTH, KV_HEADS, HEAD)
    queries = low(rotate(query_pre, positions))
    keys = low(rotate(key_pre, positions))
    values = low(low_back(jnp.dot(normed_attn, value_weight, precision=HIGHEST))).reshape(LENGTH, KV_HEADS, HEAD)
    attended = low(low_back(attend(queries, keys, values, prefix_len)))
    residual = inputs + low_back(jnp.dot(attended, out_weight, precision=HIGHEST))
    normed_ffn = low(normalize(residual, ffn_gain))
    logits = jnp.dot(normed_ffn, router_weight, precision=HIGHEST)
    gate_probs = jax.nn.softmax(jnp.take_along_axis(logits, token_routes, 1), -1)
    halves = jax.vmap(experts, in_axes=(0, 0, 0, None, None))(normed_ffn.reshape(N_GROUP, TOK_DEV, D), gate_probs.reshape(N_GROUP, TOK_DEV, TOP), token_routes.reshape(N_GROUP, TOK_DEV, TOP), expert_in, expert_out)
    return residual + halves.reshape(LENGTH, D)

def reference(block_in, attn_gain, query_weight, key_weight, value_weight, out_weight, ffn_gain, router_weight, expert_in, expert_out, routes, prefix, cotangent):
    weights = (attn_gain.astype(jnp.float32), query_weight.astype(jnp.float32), key_weight.astype(jnp.float32), value_weight.astype(jnp.float32), out_weight.astype(jnp.float32), ffn_gain.astype(jnp.float32), router_weight.astype(jnp.float32), expert_in.astype(jnp.float32), expert_out.astype(jnp.float32))

    def one_sequence(totals, batch_items):
        sequence, token_routes, prefix_len, grad_seq = batch_items

        def forward(inputs, *params):
            return block_forward(inputs, *params, token_routes, prefix_len)
        output, pullback = jax.vjp(forward, sequence.astype(jnp.float32), *weights)
        gradients = pullback(grad_seq.astype(jnp.float32))
        new_totals = tuple((running + fresh_grad for running, fresh_grad in zip(totals, gradients[1:])))
        return (new_totals, (output.astype(jnp.bfloat16), gradients[0]))
    empty_sums = tuple((jnp.zeros(weight.shape, jnp.float32) for weight in weights))
    totals, (block_out, input_grad) = lax.scan(one_sequence, empty_sums, (block_in, routes, prefix, cotangent))
    return (block_out, input_grad, totals[0], totals[1], totals[2], totals[3], totals[4], totals[5], totals[6], totals[7], totals[8])
```

```python
import functools
import math

import jax
import jax.numpy as jnp
import numpy as np
from jax import lax
from jax.experimental import pallas as pl
from jax.experimental.pallas import tpu as pltpu
from jax.sharding import PartitionSpec as P

HEADS = 16
KV_HEADS = 8
HEAD = 64
FF = 512
TOP = 8
EXPERTS = 16

EPSILON = 1e-06
THETA_BASE = 10000.0
MASKED = -1e30
HIGHEST = lax.Precision.HIGHEST
F32 = jnp.float32
BF16 = jnp.bfloat16
MIB = 1 << 20


def nn(left, right):
    return lax.dot_general(left, right, (((1,), (0,)), ((), ())), preferred_element_type=F32)


def nt(left, right):
    return lax.dot_general(left, right, (((1,), (1,)), ((), ())), preferred_element_type=F32)


def params(limit=48, **more):
    return pltpu.CompilerParams(vmem_limit_bytes=limit * MIB, **more)


def whole(shape):
    return pl.BlockSpec(shape, lambda *_: (0,) * len(shape), pipeline_mode=pl.Buffered(1))


SCALAR = pl.BlockSpec(memory_space=pltpu.SMEM)


def half_lanes(ref, which, half):
    return ref[:, pl.ds(pl.multiple_of(which * half, half), half)]


def swap_halves(tile):
    lane = lax.broadcasted_iota(jnp.int32, tile.shape, 1) % HEAD
    return jnp.where(
        lane < HEAD // 2, pltpu.roll(tile, 128 - HEAD // 2, 1), pltpu.roll(tile, HEAD // 2, 1)
    )


def rotated(values, cosine, sine, sign):
    tiles = []
    for start in range(0, values.shape[1], 128):
        tile = values[:, start : start + 128]
        tiles.append(tile * cosine + swap_halves(tile) * (sine * sign))
    return tiles[0] if len(tiles) == 1 else jnp.concatenate(tiles, 1)


def project_kernel(g_ref, x_ref, gain_ref, wq0, wq1, wk0, wk1, wv0, wv1, cos_ref, sin_ref,
                   n_ref, q_ref, k_ref, v_ref):
    half = x_ref.shape[1] // 2
    g = g_ref[0]

    @pl.when(pl.program_id(0) == 0)
    def _():
        x = x_ref[...].astype(F32)
        scale = lax.rsqrt(jnp.mean(x * x, -1, keepdims=True) + EPSILON)
        n_ref[...] = (x * scale * gain_ref[...]).astype(BF16)

    own = half_lanes(n_ref, g, half)
    other = half_lanes(n_ref, 1 - g, half)
    cosine, sine = cos_ref[...], sin_ref[...]
    q = rotated(nn(own, wq0[...]) + nn(other, wq1[...]), cosine, sine, 1.0)
    q_ref[...] = q.astype(BF16) * jnp.asarray(1.0 / math.sqrt(HEAD), BF16)
    k = rotated(nn(own, wk0[...]) + nn(other, wk1[...]), cosine, sine, 1.0)
    k_ref[...] = k.astype(BF16)
    v_ref[...] = (nn(own, wv0[...]) + nn(other, wv1[...])).astype(BF16)


def project(g, x, gain, wq, wk, wv, cosine, sine):
    tokens, width = x.shape
    steps = 4
    qb, kb = wq[0].shape[1] // steps, wk[0].shape[1] // steps
    half = width // 2
    w_spec = lambda n: pl.BlockSpec((half, n), lambda i: (0, i))
    o_spec = lambda n: pl.BlockSpec((tokens, n), lambda i: (0, i))
    return pl.pallas_call(
        project_kernel,
        grid=(steps,),
        in_specs=[SCALAR, whole((tokens, width)), whole((1, width)),
                  w_spec(qb), w_spec(qb), w_spec(kb), w_spec(kb), w_spec(kb), w_spec(kb),
                  whole((tokens, 128)), whole((tokens, 128))],
        out_specs=[pl.BlockSpec((tokens, width), lambda i: (0, 0)), o_spec(qb), o_spec(kb), o_spec(kb)],
        out_shape=[jax.ShapeDtypeStruct((tokens, width), BF16),
                   jax.ShapeDtypeStruct((tokens, wq[0].shape[1]), BF16),
                   jax.ShapeDtypeStruct((tokens, wk[0].shape[1]), BF16),
                   jax.ShapeDtypeStruct((tokens, wv[0].shape[1]), BF16)],
        compiler_params=params(),
        cost_estimate=pl.CostEstimate(flops=2 * tokens * width * 2048, bytes_accessed=8 * MIB, transcendentals=0),
        name="project",
    )(g, x, gain, *wq, *wk, *wv, cosine, sine)


def lane_half(shape, which):
    lane = lax.broadcasted_iota(jnp.int32, shape, 1)
    return ((lane // HEAD) % 2 == which).astype(F32)


def doubled(tile, which):
    kept = tile.astype(F32) * lane_half(tile.shape, which)
    return kept + pltpu.roll(kept, HEAD, 1)


def fill_bias(bias, prefix_ref, g):
    shape = bias.shape
    key = lax.broadcasted_iota(jnp.int32, shape, 0)
    query = lax.broadcasted_iota(jnp.int32, shape, 1)
    seen = (key <= query) | (key + g * shape[0] < prefix_ref[0])
    bias[...] = jnp.where(seen, 0.0, MASKED)


def attend_kernel(g_ref, prefix_ref, q_ref, k0_ref, v0_ref, k1_ref, v1_ref, o_ref, lse_ref, bias):
    g = g_ref[0]
    which = pl.program_id(0) % 2

    @pl.when(pl.program_id(0) == 0)
    def _():
        fill_bias(bias, prefix_ref, g)

    def run(blocks):
        q = q_ref[...].astype(F32)
        keys = [doubled(k[...], which).astype(BF16) for k, _ in blocks]
        values = [doubled(v[...], which).T[:HEAD].astype(BF16) for _, v in blocks]
        outs = []
        for a in range(2):
            qa = (q * lane_half(q.shape, a)).astype(BF16)
            scores = [nt(k, qa) for k in keys]
            scores[0] = scores[0] + bias[...]
            peak = functools.reduce(jnp.maximum, [jnp.max(s, 0, keepdims=True) for s in scores])
            weights = [jnp.exp(s - peak) for s in scores]
            total = sum(jnp.sum(w, 0, keepdims=True) for w in weights)
            out = sum(nn(v, w.astype(BF16)) for v, w in zip(values, weights))
            outs.append(out * (1.0 / total))
            lse_ref[0, a : a + 1, :] = peak + jnp.log(total)
        o_ref[...] = jnp.concatenate(outs, 0).T.astype(BF16)

    @pl.when(g == 0)
    def _():
        run([(k0_ref, v0_ref)])

    @pl.when(g != 0)
    def _():
        run([(k0_ref, v0_ref), (k1_ref, v1_ref)])


def attend(g, prefix, q, k0, v0, k1, v1):
    tokens = q.shape[0]
    kv = pl.BlockSpec((tokens, 128), lambda i: (0, i // 2))
    qs = pl.BlockSpec((tokens, 128), lambda i: (0, i))
    return pl.pallas_call(
        attend_kernel,
        grid=(KV_HEADS,),
        in_specs=[SCALAR, SCALAR, qs, kv, kv, kv, kv],
        out_specs=[qs, pl.BlockSpec((1, 8, tokens), lambda i: (i, 0, 0))],
        out_shape=[jax.ShapeDtypeStruct(q.shape, BF16), jax.ShapeDtypeStruct((KV_HEADS, 8, tokens), F32)],
        scratch_shapes=[pltpu.VMEM((tokens, tokens), F32)],
        compiler_params=params(),
        cost_estimate=pl.CostEstimate(flops=16 * tokens * tokens * 2 * 256 * 4, bytes_accessed=5 * MIB,
                                      transcendentals=16 * tokens * tokens * 2),
        name="attend",
    )(g, prefix, q, k0, v0, k1, v1)


def attend_back_kernel(g_ref, prefix_ref, q_ref, k0_ref, v0_ref, k1_ref, v1_ref, do_ref, lse_ref,
                       cos_ref, sin_ref, dq_ref, dk0_ref, dv0_ref, dk1_ref, dv1_ref, bias):
    g = g_ref[0]
    which = pl.program_id(0) % 2

    @pl.when(pl.program_id(0) == 0)
    def _():
        fill_bias(bias, prefix_ref, g)

    def run(blocks):
        q = q_ref[...].astype(F32)
        do = do_ref[...].astype(F32)
        keys = [doubled(b[0][...], which) for b in blocks]
        keys_t = [k.T[:HEAD].astype(BF16) for k in keys]
        keys = [k.astype(BF16) for k in keys]
        values = [doubled(b[1][...], which).astype(BF16) for b in blocks]
        dks = [0.0 for _ in blocks]
        dvs = [0.0 for _ in blocks]
        dqs = []
        for a in range(2):
            half = lane_half(q.shape, a)
            qa = (q * half).astype(BF16)
            doa = (do * half).astype(BF16)
            lse = lse_ref[0, a : a + 1, :]
            scores = [nt(k, qa) for k in keys]
            scores[0] = scores[0] + bias[...]
            probs = [jnp.exp(s - lse) for s in scores]
            dps = [nt(v, doa) for v in values]
            delta = sum(jnp.sum(p * dp, 0, keepdims=True) for p, dp in zip(probs, dps))
            dq = 0.0
            for n in range(len(blocks)):
                ds = (probs[n] * (dps[n] - delta)).astype(BF16)
                dvs[n] = dvs[n] + nn(probs[n].astype(BF16), doa)
                dks[n] = dks[n] + nn(ds, qa)
                dq = dq + nn(keys_t[n], ds)
            dqs.append(dq)
        dq = jnp.concatenate(dqs, 0).T * (1.0 / math.sqrt(HEAD))
        dq_ref[...] = rotated(dq, cos_ref[...], sin_ref[...], -1.0).astype(BF16)
        for n, (_, _, dk_ref, dv_ref) in enumerate(blocks):
            for grad, ref in ((dks[n], dk_ref), (dvs[n], dv_ref)):
                both = grad + pltpu.roll(grad, HEAD, 1)
                part = both * lane_half(both.shape, which)

                @pl.when(which == 0)
                def _():
                    ref[...] = part.astype(ref.dtype)

                @pl.when(which != 0)
                def _():
                    ref[...] = (ref[...].astype(F32) + part).astype(ref.dtype)

    own = (k0_ref, v0_ref, dk0_ref, dv0_ref)
    earlier = (k1_ref, v1_ref, dk1_ref, dv1_ref)

    @pl.when(g == 0)
    def _():
        run([own])
        dk1_ref[...] = jnp.zeros_like(dk1_ref)
        dv1_ref[...] = jnp.zeros_like(dv1_ref)

    @pl.when(g != 0)
    def _():
        run([own, earlier])


def attend_back(g, prefix, q, k0, v0, k1, v1, do, lse, cosine, sine):
    tokens = q.shape[0]
    kv = pl.BlockSpec((tokens, 128), lambda i: (0, i // 2))
    qs = pl.BlockSpec((tokens, 128), lambda i: (0, i))
    return pl.pallas_call(
        attend_back_kernel,
        grid=(KV_HEADS,),
        in_specs=[SCALAR, SCALAR, qs, kv, kv, kv, kv, qs,
                  pl.BlockSpec((1, 8, tokens), lambda i: (i, 0, 0)),
                  whole((tokens, 128)), whole((tokens, 128))],
        out_specs=[qs, kv, kv, kv, kv],
        out_shape=[jax.ShapeDtypeStruct(q.shape, BF16),
                   jax.ShapeDtypeStruct(k0.shape, F32), jax.ShapeDtypeStruct(k0.shape, F32),
                   jax.ShapeDtypeStruct(k0.shape, BF16), jax.ShapeDtypeStruct(k0.shape, BF16)],
        scratch_shapes=[pltpu.VMEM((tokens, tokens), F32)],
        compiler_params=params(),
        cost_estimate=pl.CostEstimate(flops=16 * tokens * tokens * 2 * 256 * 10, bytes_accessed=8 * MIB,
                                      transcendentals=16 * tokens * tokens * 2),
        name="attend_back",
    )(g, prefix, q, k0, v0, k1, v1, do, lse, cosine, sine)


def output_kernel(g_ref, a_ref, wo0, wo1, x_ref, gain_ref, res_ref, n_ref):
    half = a_ref.shape[1] // 2
    g = g_ref[0]
    res = x_ref[...].astype(F32) + (
        nn(half_lanes(a_ref, g, half), wo0[...]) + nn(half_lanes(a_ref, 1 - g, half), wo1[...]))
    res_ref[...] = res
    scale = lax.rsqrt(jnp.mean(res * res, -1, keepdims=True) + EPSILON)
    n_ref[...] = (res * scale * gain_ref[...]).astype(BF16)


def output(g, attended, wo, x, gain):
    tokens, width = x.shape
    rows = 256
    row = pl.BlockSpec((rows, width), lambda i: (i, 0))
    return pl.pallas_call(
        output_kernel,
        grid=(tokens // rows,),
        in_specs=[SCALAR, row, whole(wo[0].shape), whole(wo[1].shape), row, whole((1, width))],
        out_specs=[row, row],
        out_shape=[jax.ShapeDtypeStruct((tokens, width), F32), jax.ShapeDtypeStruct((tokens, width), BF16)],
        compiler_params=params(),
        cost_estimate=pl.CostEstimate(flops=2 * tokens * width * width, bytes_accessed=7 * MIB, transcendentals=0),
        name="output",
    )(g, attended, *wo, x, gain)


def gates_of(rows, router_t, member):
    logits = jnp.where(member > 0.0, nt(rows, router_t), MASKED)
    peak = jnp.max(logits, -1, keepdims=True)
    weights = jnp.where(member > 0.0, jnp.exp(logits - peak), 0.0)
    return weights / jnp.sum(weights, -1, keepdims=True)


def experts_kernel(g_ref, x0, x1, xt0, xt1, c0, c1, ct0, ct1, m0, m1, router_ref, win, wout,
                   keep_ref, send_ref, grad0_ref, back_ref, sum0_ref, sum1_ref, p0_ref, gg0_ref,
                   p_scr, gg_scr, hid_scr, dgu_scr, grad1, sum1):
    e = pl.program_id(0)
    last = pl.num_programs(0) - 1
    tokens, width = x0.shape
    column = g_ref[0] * pl.num_programs(0) + e

    @pl.when(e == 0)
    def _():
        router = router_ref[...]
        p_scr[0:tokens] = gates_of(x0[...], router, m0[...])
        p_scr[tokens:] = gates_of(x1[...], router, m1[...])
        p0_ref[...] = p_scr[0:tokens]
        gg_scr[...] = jnp.zeros_like(gg_scr)

    def tile(x_ref, c_ref, grad_ref, sum_ref, base, start, rows):
        at = pl.ds(start, rows)
        to = pl.ds(base + start, rows)
        probs = p_scr[to]
        mine = lax.broadcasted_iota(jnp.int32, probs.shape, 1) == column
        p = jnp.sum(jnp.where(mine, probs, 0.0), 1, keepdims=True)
        gate_up = nn(x_ref[at], win[0])
        back = nn(c_ref[at], wout[0])
        gate, up = gate_up[:, :FF], gate_up[:, FF:]
        sig = 1.0 / (1.0 + jnp.exp(-gate))
        act = gate * sig
        hid = act * up
        gg = jnp.sum(hid * back, 1, keepdims=True)
        gg_scr[to] = jnp.where(mine, gg, gg_scr[to])
        back = back * p
        dgate = back * up * (sig * (1.0 + gate * (1.0 - sig)))
        dup = back * act
        hid_low = (hid * p).astype(BF16)
        dgu = jnp.concatenate([dgate, dup], 1).astype(BF16)
        hid_scr[to] = hid_low
        dgu_scr[to] = dgu
        add = nt(hid_low, wout[0])
        grad = nt(dgu, win[0])

        @pl.when(e == 0)
        def _():
            sum_ref[at] = add
            grad_ref[at] = grad

        @pl.when(e != 0)
        def _():
            sum_ref[at] += add
            grad_ref[at] += grad

    rows = 256

    @pl.loop(0, tokens // rows)
    def _(i):
        tile(x0, c0, grad0_ref, sum0_ref, 0, pl.multiple_of(i * rows, rows), rows)

    @pl.loop(0, tokens // rows)
    def _(i):
        tile(x1, c1, grad1, sum1, tokens, pl.multiple_of(i * rows, rows), rows)

    block = 256
    for out, base in ((keep_ref, 0), (send_ref, width // 2)):

        @pl.loop(0, width // 2 // block)
        def _(i, out=out, base=base):
            at = pl.ds(pl.multiple_of(base + i * block, block), block)
            to = pl.ds(pl.multiple_of(i * block, block), block)
            win_grad = nn(xt0[at], dgu_scr[0:tokens]) + nn(xt1[at], dgu_scr[tokens:])
            out[0, to, 0 : 2 * FF] = win_grad.astype(BF16)
            wout_grad = nn(ct0[at], hid_scr[0:tokens]) + nn(ct1[at], hid_scr[tokens:])
            out[0, to, 2 * FF :] = wout_grad.astype(BF16)

    @pl.when(e == last)
    def _():
        back_ref[:, 0:width] = grad1[...].astype(BF16)
        back_ref[:, width:] = gg_scr[tokens:].astype(BF16)
        sum1_ref[...] = sum1[...].astype(BF16)
        gg0_ref[...] = gg_scr[0:tokens]


def experts(g, x, xt, c, ct, member, router_t, win, wout):
    tokens, width = x[0].shape
    count = win.shape[0]
    cols = 3 * FF
    full = whole((tokens, width))
    full_t = whole((width, tokens))
    small = whole((tokens, EXPERTS))
    shape = jax.ShapeDtypeStruct
    const = lambda s: pl.BlockSpec(s, lambda i: (0, 0))
    half = pl.BlockSpec((1, width // 2, cols), lambda i: (i, 0, 0))
    return pl.pallas_call(
        experts_kernel,
        grid=(count,),
        in_specs=[SCALAR, full, full, full_t, full_t, full, full, full_t, full_t, small, small,
                  whole((EXPERTS, width)),
                  pl.BlockSpec((1, width, 2 * FF), lambda i: (i, 0, 0)),
                  pl.BlockSpec((1, width, FF), lambda i: (i, 0, 0))],
        out_specs=[half, half, const((tokens, width)), const((tokens, width + EXPERTS)),
                   const((tokens, width)), const((tokens, width)), const((tokens, EXPERTS)),
                   const((tokens, EXPERTS))],
        out_shape=[shape((count, width // 2, cols), BF16), shape((count, width // 2, cols), BF16),
                   shape((tokens, width), F32), shape((tokens, width + EXPERTS), BF16),
                   shape((tokens, width), F32), shape((tokens, width), BF16),
                   shape((tokens, EXPERTS), F32), shape((tokens, EXPERTS), F32)],
        scratch_shapes=[pltpu.VMEM((2 * tokens, EXPERTS), F32), pltpu.VMEM((2 * tokens, EXPERTS), F32),
                        pltpu.VMEM((2 * tokens, FF), BF16), pltpu.VMEM((2 * tokens, 2 * FF), BF16),
                        pltpu.VMEM((tokens, width), F32), pltpu.VMEM((tokens, width), F32)],
        compiler_params=params(60),
        cost_estimate=pl.CostEstimate(flops=2 * tokens * count * width * FF * 18, bytes_accessed=70 * MIB,
                                      transcendentals=2 * tokens * count * FF),
        name="experts",
    )(g, *x, *xt, *c, *ct, *member, router_t, win, wout)


def middle_kernel(g_ref, c_ref, grad_ref, back_ref, gg_ref, p_ref, router_ref, res_ref, gain_ref, wo0, wo1,
                  dres_ref, low_ref, da_ref, dl_ref):
    width = c_ref.shape[1]
    half = width // 2
    g = g_ref[0]
    p = p_ref[...]
    gg = gg_ref[...] + back_ref[:, width:].astype(F32)
    dlogits = p * (gg - jnp.sum(p * gg, 1, keepdims=True))
    dl_ref[...] = dlogits
    grad = grad_ref[...] + back_ref[:, :width].astype(F32) + lax.dot_general(
        dlogits, router_ref[...].astype(F32), (((1,), (0,)), ((), ())), precision=HIGHEST,
        preferred_element_type=F32)
    res = res_ref[...]
    scale = lax.rsqrt(jnp.mean(res * res, -1, keepdims=True) + EPSILON)
    w = grad * gain_ref[...]
    dres = c_ref[...].astype(F32) + (scale * w - res * (scale * scale * scale)
                                     * jnp.mean(w * res, -1, keepdims=True))
    dres_ref[...] = dres
    low = dres.astype(BF16)
    low_ref[...] = low
    da_ref[:, pl.ds(pl.multiple_of(g * half, half), half)] = nt(low, wo0[...]).astype(BF16)
    da_ref[:, pl.ds(pl.multiple_of((1 - g) * half, half), half)] = nt(low, wo1[...]).astype(BF16)


def middle(g, c, grad, back, gg, p, router_t, res, gain, wo):
    tokens, width = c.shape
    rows = 256
    row = lambda n: pl.BlockSpec((rows, n), lambda i: (i, 0))
    shape = jax.ShapeDtypeStruct
    return pl.pallas_call(
        middle_kernel,
        grid=(tokens // rows,),
        in_specs=[SCALAR, row(width), row(width), row(width + EXPERTS), row(EXPERTS), row(EXPERTS),
                  whole((EXPERTS, width)), row(width), whole((1, width)), whole(wo[0].shape), whole(wo[1].shape)],
        out_specs=[row(width), row(width), row(width), row(EXPERTS)],
        out_shape=[shape((tokens, width), F32), shape((tokens, width), BF16), shape((tokens, width), BF16),
                   shape((tokens, EXPERTS), F32)],
        compiler_params=params(),
        cost_estimate=pl.CostEstimate(flops=2 * tokens * width * width, bytes_accessed=14 * MIB, transcendentals=0),
        name="middle",
    )(g, c, grad, back, gg, p, router_t, res, gain, *wo)


def weight_kernel(xt_ref, dq_ref, dk0, dk1, dv0, dv1, cos_ref, sin_ref, keep_ref, send_ref, dk_ref, dv_ref):
    half = keep_ref.shape[0]
    dq = dq_ref[...]
    dk = rotated(dk0[...] + dk1[...].astype(F32), cos_ref[...], sin_ref[...], -1.0).astype(BF16)
    dv = (dv0[...] + dv1[...].astype(F32)).astype(BF16)
    dk_ref[...] = dk
    dv_ref[...] = dv
    qb, kb = dq.shape[1], dk.shape[1]
    for ref, base in ((keep_ref, 0), (send_ref, half)):
        rows = xt_ref[base : base + half]
        ref[:, 0:qb] = nn(rows, dq).astype(BF16)
        ref[:, qb : qb + kb] = nn(rows, dk).astype(BF16)
        ref[:, qb + kb :] = nn(rows, dv).astype(BF16)


def weight_grads(xt, dq, dk, dv, cosine, sine):
    width, tokens = xt.shape
    steps = 4
    qb, kb = dq.shape[1] // steps, dk[0].shape[1] // steps
    col = lambda n: pl.BlockSpec((tokens, n), lambda i: (0, i))
    out = pl.BlockSpec((width // 2, qb + 2 * kb), lambda i: (0, i))
    shape = jax.ShapeDtypeStruct
    total = steps * (qb + 2 * kb)
    return pl.pallas_call(
        weight_kernel,
        grid=(steps,),
        in_specs=[whole((width, tokens)), col(qb), col(kb), col(kb), col(kb), col(kb),
                  whole((tokens, 128)), whole((tokens, 128))],
        out_specs=[out, out, col(kb), col(kb)],
        out_shape=[shape((width // 2, total), BF16), shape((width // 2, total), BF16),
                   shape(dk[0].shape, BF16), shape(dv[0].shape, BF16)],
        compiler_params=params(),
        cost_estimate=pl.CostEstimate(flops=2 * tokens * width * total, bytes_accessed=10 * MIB, transcendentals=0),
        name="weight_grads",
    )(xt, dq, *dk, *dv, cosine, sine)


def input_kernel(g_ref, dq_ref, dk_ref, dv_ref, wq0, wq1, wk0, wk1, wv0, wv1, x_ref, gain_ref, dres_ref,
                 out_ref, grad):
    half = x_ref.shape[1] // 2
    g = g_ref[0]
    dq, dk, dv = dq_ref[...], dk_ref[...], dv_ref[...]
    grad[:, pl.ds(pl.multiple_of(g * half, half), half)] = (
        nt(dq, wq0[...]) + nt(dk, wk0[...]) + nt(dv, wv0[...]))
    grad[:, pl.ds(pl.multiple_of((1 - g) * half, half), half)] = (
        nt(dq, wq1[...]) + nt(dk, wk1[...]) + nt(dv, wv1[...]))
    x = x_ref[...].astype(F32)
    scale = lax.rsqrt(jnp.mean(x * x, -1, keepdims=True) + EPSILON)
    w = grad[...] * gain_ref[...]
    out_ref[...] = dres_ref[...] + (scale * w - x * (scale * scale * scale) * jnp.mean(w * x, -1, keepdims=True))


def input_grads(g, dq, dk, dv, wq, wk, wv, x, gain, dres):
    tokens, width = x.shape
    rows = 256
    row = lambda a: pl.BlockSpec((rows, a.shape[1]), lambda i: (i, 0))
    weights = (*wq, *wk, *wv)
    return pl.pallas_call(
        input_kernel,
        grid=(tokens // rows,),
        in_specs=[SCALAR, row(dq), row(dk), row(dv), *(whole(w.shape) for w in weights), row(x),
                  whole((1, width)), row(dres)],
        out_specs=row(dres),
        out_shape=jax.ShapeDtypeStruct((tokens, width), F32),
        scratch_shapes=[pltpu.VMEM((rows, width), F32)],
        compiler_params=params(),
        cost_estimate=pl.CostEstimate(flops=2 * tokens * width * 2048, bytes_accessed=12 * MIB, transcendentals=0),
        name="input_grads",
    )(g, dq, dk, dv, *weights, x, gain, dres)


def exchange(value, bit):
    if bit == "group":
        return lax.ppermute(value, "group", [(0, 1), (1, 0)])
    count = lax.axis_size("replica")
    return lax.ppermute(value, "replica", [(i, i ^ (1 << bit)) for i in range(count)])


def halving(parts, axes, order):
    axes = list(axes)
    for bit, dim in order:
        at = axes.index(dim)
        take = lambda which: sum(lax.index_in_dim(p, which, at, False).astype(F32) for p in parts)
        received = exchange(take(1).astype(BF16), bit)
        parts = [lax.index_in_dim(p, 0, at, False) for p in parts] + [received]
        axes.pop(at)
    return sum(p.astype(F32) for p in parts)


def on_device(
    block_in, attn_gain, query_weight, key_weight, value_weight, out_weight, ffn_gain, router_weight,
    expert_in, expert_out, routes, prefix, cotangent,
):
    replicas = lax.axis_size("replica")
    bits = replicas.bit_length() - 1
    tokens, width = block_in.shape[1:]
    half = width // 2
    chunk = half // replicas
    group, replica = lax.axis_index("group"), lax.axis_index("replica")
    g = group.astype(jnp.int32).reshape(1)
    x, cot = block_in[0], cotangent[0]
    swap = lambda v: exchange(v, "group")

    def ordered(own, other, axis):
        return jnp.where(group == 0, jnp.concatenate([own, other], axis), jnp.concatenate([other, own], axis))

    wq = (query_weight, swap(query_weight))
    wk = (key_weight, swap(key_weight))
    wv = (value_weight, swap(value_weight))
    expert_ids = jnp.arange(EXPERTS, dtype=jnp.int32)
    member = (routes[0][:, None, :] == expert_ids[None, :, None]).any(-1)
    small = jnp.concatenate(
        [attn_gain[None], ffn_gain[None], router_weight.T, member.astype(BF16).T], 0)
    small_other = swap(small)
    vectors = ordered(small[: 2 + EXPERTS], small_other[: 2 + EXPERTS], 1)
    gain_attn, gain_ffn = vectors[0:1].astype(F32), vectors[1:2].astype(F32)
    router_t = vectors[2:]
    member = (member.astype(F32), small_other[2 + EXPERTS :].T.astype(F32))
    wo_send, cot_send, *_ = lax.optimization_barrier((out_weight, cot, wq[1], wk[1], wv[1]))
    wo = (out_weight, swap(wo_send))
    cots = (cot, swap(cot_send))

    positions = group * tokens + jnp.arange(tokens, dtype=jnp.int32)
    frequency = THETA_BASE ** (-jnp.arange(HEAD // 2, dtype=F32) * 2.0 / HEAD)
    angles = positions.astype(F32)[:, None] * frequency[None, :]
    cosine = jnp.tile(jnp.cos(angles), (1, 4))
    sine = jnp.sin(angles)
    sine = jnp.concatenate([-sine, sine, -sine, sine], 1)

    place = np.arange(width)
    blocks, inner = place // chunk, place % chunk
    reverse = np.zeros_like(blocks)
    for b in range(bits):
        reverse |= ((blocks >> 1 >> (bits - 1 - b)) & 1) << b
    feature = ((jnp.asarray(blocks & 1, jnp.int32) ^ group) * half
               + (jnp.asarray(reverse, jnp.int32) ^ replica) * chunk + jnp.asarray(inner, jnp.int32))
    order = (feature[:, None] == jnp.arange(width, dtype=jnp.int32)[None, :]).astype(BF16)
    reorder = lambda a: nt(order, a).astype(BF16)

    normed_attn, q, k, v = project(g, x, gain_attn, wq, wk, wv, cosine, sine)
    to_later = lambda a: lax.ppermute(a, "group", [(0, 1)])
    to_earlier = lambda a: lax.ppermute(a, "group", [(1, 0)])
    k1, v1 = to_later(k), to_later(v)
    attended, lse = attend(g, prefix, q, k, v, k1, v1)
    residual, normed_ffn = output(g, attended, wo, x, gain_ffn)
    normed = (normed_ffn, swap(normed_ffn))
    normed_t = (reorder(normed[0]), reorder(normed[1]))
    cots_t = (reorder(cots[0]), reorder(cots[1]))
    keep, send, grad_own, back, sum_own, sum_other, gates, gg = experts(
        g, normed, normed_t, cots, cots_t, member, router_t, expert_in, expert_out)

    back = swap(back)
    grad_res, grad_low, grad_att, grad_logits = middle(
        g, cot, grad_own, back, gg, gates, router_t, residual, gain_ffn, wo)
    block_out = (residual + sum_own + swap(sum_other).astype(F32)).astype(BF16)
    dq, dk0, dv0, dk1, dv1 = attend_back(g, prefix, q, k, v, k1, v1, grad_att, lse, cosine, sine)
    dk = (dk0, to_earlier(dk1))
    dv = (dv0, to_earlier(dv1))
    attn_keep, attn_send, dk_low, dv_low = weight_grads(reorder(normed_attn), dq, dk, dv, cosine, sine)
    input_grad = input_grads(g, dq, dk_low, dv_low, wq, wk, wv, x, gain_attn, grad_res)

    dims = [*range(1, bits), "group"]
    shape = (2,) * bits + (chunk,)
    received = exchange(send, 0)
    two = max(1, keep.shape[0] // 4)
    summed = []
    for first in range(0, keep.shape[0], two):
        stages = list(range(1, bits))
        if first + two >= keep.shape[0] and bits > 2:
            stages[0], stages[1] = stages[1], stages[0]
        parts = [p[first : first + two].reshape(two, *shape, 3 * FF) for p in (keep, received)]
        summed.append(halving(parts, ["e", *dims], [(b, b) for b in stages]))
    summed = jnp.concatenate(summed, 0)
    rows = lambda owner: lax.dynamic_slice_in_dim(expert_in, owner * half + replica * chunk, chunk, 1).astype(F32)
    gain_parts = [jnp.sum(summed[:, n, :, : 2 * FF] * rows(owner), (0, 2)) for n, owner in ((0, group), (1, 1 - group))]
    other_experts = swap(summed[:, 1].astype(BF16)).astype(F32)
    gain_other = swap(jnp.broadcast_to(gain_parts[1][:, None], (chunk, 128)))[:, 0]
    expert_grads = ordered(summed[:, 0], other_experts, 0)

    def sum_rows(keep, send, orders):
        received = exchange(send, 0)
        total = keep.shape[1]
        cut = total // 128 // len(orders) * 128
        outs = []
        for n, stages in enumerate(orders):
            first, end = n * cut, total if n == len(orders) - 1 else (n + 1) * cut
            parts = [p[:, first:end].reshape(*shape, end - first) for p in (keep, received)]
            outs.append(halving(parts, dims, [(b, b) for b in stages]))
        return jnp.concatenate(outs, 1)

    later = list(range(1, bits))
    turned = later[1:2] + later[0:1] + later[2:]
    orders = [["group", *later], [*later, "group"], [*turned, "group"]]
    out_t = jnp.concatenate(
        [nn(reorder(grad_low), attended).astype(BF16), nn(normed_t[0], grad_logits.astype(BF16)).astype(BF16)], 1)
    out_sum = sum_rows(out_t[:half], out_t[half:], orders)
    attn_sum = sum_rows(attn_keep, attn_send, orders)

    out_grad = out_sum[:, :width].T
    router_grad = out_sum[:, width:]
    qb, kb = HEADS * HEAD // 4, KV_HEADS * HEAD // 4
    attn_sum = attn_sum.reshape(chunk, 4, qb + 2 * kb)
    query_grad = attn_sum[:, :, :qb].reshape(chunk, -1)
    key_grad = attn_sum[:, :, qb : qb + kb].reshape(chunk, -1)
    value_grad = attn_sum[:, :, qb + kb :].reshape(chunk, -1)

    mine = lambda a: lax.dynamic_slice_in_dim(a, replica * chunk, chunk, 0).astype(F32)
    attn_gain_grad = (
        jnp.sum(mine(query_weight) * query_grad, 1) + jnp.sum(mine(key_weight) * key_grad, 1)
        + jnp.sum(mine(value_weight) * value_grad, 1)) / mine(attn_gain)
    ffn_gain_grad = (
        gain_parts[0] + gain_other + jnp.sum(mine(router_weight) * router_grad, 1)) / mine(ffn_gain)
    return (
        block_out[None], input_grad[None], attn_gain_grad, query_grad, key_grad, value_grad, out_grad,
        ffn_gain_grad, router_grad, expert_grads[:, :, : 2 * FF], expert_grads[:, :, 2 * FF :],
    )


def solution(mesh):
    placed = (
        P("replica", "group", None),
        P("group"),
        P("group", None),
        P("group", None),
        P("group", None),
        P("group", None),
        P("group"),
        P("group", None),
        P("group", None, None),
        P("group", None, None),
        P("replica", "group", None),
        P("replica"),
        P("replica", "group", None),
    )
    both = ("group", "replica")
    return jax.shard_map(
        on_device,
        mesh=mesh,
        in_specs=placed,
        out_specs=(
            P("replica", "group", None),
            P("replica", "group", None),
            P(both),
            P(both, None),
            P(both, None),
            P(both, None),
            P(None, both),
            P(both),
            P(both, None),
            P(None, both, None),
            P(None, both, None),
        ),
        check_vma=False,
    )
```

```python
import functools
import math

import jax
import jax.numpy as jnp
import numpy as np
from jax import lax
from jax.experimental import pallas as pl
from jax.experimental.pallas import tpu as pltpu
from jax.sharding import PartitionSpec as P

HEADS = 16
KV_HEADS = 8
HEAD = 64
FF = 512
TOP = 8
EXPERTS = 16

EPSILON = 1e-06
THETA_BASE = 10000.0
MASKED = -1e30
HIGHEST = lax.Precision.HIGHEST
F32 = jnp.float32
BF16 = jnp.bfloat16
MIB = 1 << 20


def nn(left, right):
    return lax.dot_general(left, right, (((1,), (0,)), ((), ())), preferred_element_type=F32)


def nt(left, right):
    return lax.dot_general(left, right, (((1,), (1,)), ((), ())), preferred_element_type=F32)


def params(limit=24):
    return pltpu.CompilerParams(vmem_limit_bytes=limit * MIB)


def cost(microseconds):
    return pl.CostEstimate(flops=int(microseconds * 0.9e9), bytes_accessed=int(microseconds * 1e5), transcendentals=0)


def whole(shape):
    return pl.BlockSpec(shape, lambda *_: (0,) * len(shape), pipeline_mode=pl.Buffered(1))


SCALAR = pl.BlockSpec(memory_space=pltpu.SMEM)

FOLLOWED = []


def pallas(kernel, *, in_specs, out_shape, **more):
    def call(*args):
        tokens, count = list(FOLLOWED), len(in_specs)

        def body(*refs):
            kernel(*refs[:count], *refs[count + len(tokens) :])

        out = pl.pallas_call(
            body,
            in_specs=[*in_specs, *[pl.BlockSpec(memory_space=pl.ANY)] * len(tokens)],
            out_shape=out_shape,
            **more,
        )(*args, *tokens)
        FOLLOWED[:] = [min(jax.tree.leaves(out), key=lambda a: a.size)]
        return out

    return call
LANES = 128


def pieces(where_ref, width):
    g, core = where_ref[0], where_ref[1]
    half, quarter = width // 2, width // 4
    other = (1 - g) * half
    at = lambda start, size: pl.ds(pl.multiple_of(start, size), size)
    return (at(g * half, half), at(other + core * quarter, quarter), at(other + (1 - core) * quarter, quarter))


def project_rows(ref, where_ref, weights):
    cols = pieces(where_ref, ref.shape[1])
    return sum(nn(ref[:, c], w[...]) for c, w in zip(cols, weights))


def swap_halves(tile):
    lane = lax.broadcasted_iota(jnp.int32, tile.shape, 1) % HEAD
    return jnp.where(
        lane < HEAD // 2, pltpu.roll(tile, 128 - HEAD // 2, 1), pltpu.roll(tile, HEAD // 2, 1)
    )


def rotated(values, cosine, sine, sign):
    tiles = []
    for start in range(0, values.shape[1], 128):
        tile = values[:, start : start + 128]
        tiles.append(tile * cosine + swap_halves(tile) * (sine * sign))
    return tiles[0] if len(tiles) == 1 else jnp.concatenate(tiles, 1)


def project_kernel(where_ref, x_ref, gain_ref, wq0, wq1, wq2, wk0, wk1, wk2, wv0, wv1, wv2, cos_ref, sin_ref,
                   n_ref, q_ref, k_ref, v_ref):
    @pl.when(pl.program_id(0) == 0)
    def _():
        x = x_ref[...].astype(F32)
        scale = lax.rsqrt(jnp.mean(x * x, -1, keepdims=True) + EPSILON)
        n_ref[...] = (x * scale * gain_ref[...]).astype(BF16)

    cosine, sine = cos_ref[...], sin_ref[...]
    q = rotated(project_rows(n_ref, where_ref, (wq0, wq1, wq2)), cosine, sine, 1.0)
    q_ref[...] = q.astype(BF16) * jnp.asarray(1.0 / math.sqrt(HEAD), BF16)
    k = rotated(project_rows(n_ref, where_ref, (wk0, wk1, wk2)), cosine, sine, 1.0)
    k_ref[...] = k.astype(BF16)
    v_ref[...] = project_rows(n_ref, where_ref, (wv0, wv1, wv2)).astype(BF16)


def project_earlier_kernel(where_ref, x_ref, gain_ref, wk0, wk1, wk2, wv0, wv1, wv2, cos_ref, sin_ref,
                           k_ref, v_ref, n_ref):
    @pl.when(where_ref[0] != 0)
    def _():
        @pl.when(pl.program_id(0) == 0)
        def _():
            x = x_ref[...].astype(F32)
            scale = lax.rsqrt(jnp.mean(x * x, -1, keepdims=True) + EPSILON)
            n_ref[...] = (x * scale * gain_ref[...]).astype(BF16)

        k = rotated(project_rows(n_ref, where_ref, (wk0, wk1, wk2)), cos_ref[...], sin_ref[...], 1.0)
        k_ref[...] = k.astype(BF16)
        v_ref[...] = project_rows(n_ref, where_ref, (wv0, wv1, wv2)).astype(BF16)

    @pl.when(where_ref[0] == 0)
    def _():
        k_ref[...] = jnp.zeros_like(k_ref)
        v_ref[...] = jnp.zeros_like(v_ref)


def weight_specs(rows, n, first):
    packed = pl.BlockSpec((rows // 2, n), lambda i: (0, first // n + i))
    return [pl.BlockSpec((rows, n), lambda i: (0, i)), packed, packed]


def project(where, x, gain, wq, wk, wv, pack, cosine, sine):
    tokens, width = x.shape
    steps = 4
    half = width // 2
    nq, nk = wq.shape[1], wk.shape[1]
    qb, kb = nq // steps, nk // steps
    o_spec = lambda n: pl.BlockSpec((tokens, n), lambda i: (0, i))
    shape = jax.ShapeDtypeStruct
    return pallas(
        project_kernel,
        grid=(steps,),
        in_specs=[SCALAR, whole((tokens, width)), whole((1, width)),
                  *weight_specs(half, qb, 0), *weight_specs(half, kb, nq), *weight_specs(half, kb, nq + nk),
                  whole((tokens, LANES)), whole((tokens, LANES))],
        out_specs=[pl.BlockSpec((tokens, width), lambda i: (0, 0)), o_spec(qb), o_spec(kb), o_spec(kb)],
        out_shape=[shape((tokens, width), BF16), shape((tokens, nq), BF16), shape((tokens, nk), BF16),
                   shape((tokens, nk), BF16)],
        compiler_params=params(),
        cost_estimate=cost(0.1),
        name="project",
    )(where, x, gain, wq, *pack, wk, *pack, wv, *pack, cosine, sine)


def project_earlier(where, x, gain, wk, wv, pack, cosine, sine):
    tokens, width = x.shape
    steps = 2
    half = width // 2
    nk = wk.shape[1]
    kb = nk // steps
    o_spec = pl.BlockSpec((tokens, kb), lambda i: (0, i))
    shape = jax.ShapeDtypeStruct
    return pallas(
        project_earlier_kernel,
        grid=(steps,),
        in_specs=[SCALAR, whole((tokens, width)), whole((1, width)),
                  *weight_specs(half, kb, 2 * nk), *weight_specs(half, kb, 3 * nk),
                  whole((tokens, LANES)), whole((tokens, LANES))],
        out_specs=[o_spec, o_spec],
        out_shape=[shape((tokens, nk), BF16), shape((tokens, nk), BF16)],
        scratch_shapes=[pltpu.VMEM((tokens, width), BF16)],
        compiler_params=params(),
        cost_estimate=cost(0.1),
        name="project_earlier",
    )(where, x, gain, wk, *pack, wv, *pack, cosine, sine)


def lane_half(shape, which):
    lane = lax.broadcasted_iota(jnp.int32, shape, 1)
    return ((lane // HEAD) % 2 == which).astype(F32)


def doubled(tile, which):
    kept = tile.astype(F32) * lane_half(tile.shape, which)
    return kept + pltpu.roll(kept, HEAD, 1)


def fill_bias(bias, prefix_ref, g):
    shape = bias.shape
    key = lax.broadcasted_iota(jnp.int32, shape, 0)
    query = lax.broadcasted_iota(jnp.int32, shape, 1)
    seen = (key <= query) | (key + g * shape[0] < prefix_ref[0])
    bias[...] = jnp.where(seen, 0.0, MASKED)


def attend_kernel(g_ref, prefix_ref, q_ref, k0_ref, v0_ref, k1_ref, v1_ref, o_ref, lse_ref, bias):
    g = g_ref[0]
    which = pl.program_id(0) % 2

    @pl.when(pl.program_id(0) == 0)
    def _():
        fill_bias(bias, prefix_ref, g)

    def run(blocks):
        q = q_ref[...].astype(F32)
        keys = [doubled(k[...], which).astype(BF16) for k, _ in blocks]
        values = [doubled(v[...], which).T[:HEAD].astype(BF16) for _, v in blocks]
        outs = []
        for a in range(2):
            qa = (q * lane_half(q.shape, a)).astype(BF16)
            scores = [nt(k, qa) for k in keys]
            scores[0] = scores[0] + bias[...]
            peak = functools.reduce(jnp.maximum, [jnp.max(s, 0, keepdims=True) for s in scores])
            weights = [jnp.exp(s - peak) for s in scores]
            total = sum(jnp.sum(w, 0, keepdims=True) for w in weights)
            out = sum(nn(v, w.astype(BF16)) for v, w in zip(values, weights))
            outs.append(out * (1.0 / total))
            lse_ref[0, a : a + 1, :] = peak + jnp.log(total)
        o_ref[...] = jnp.concatenate(outs, 0).T.astype(BF16)

    @pl.when(g == 0)
    def _():
        run([(k0_ref, v0_ref)])

    @pl.when(g != 0)
    def _():
        run([(k0_ref, v0_ref), (k1_ref, v1_ref)])


def attend(g, prefix, q, k0, v0, k1, v1):
    tokens = q.shape[0]
    kv = pl.BlockSpec((tokens, 128), lambda i: (0, i // 2))
    qs = pl.BlockSpec((tokens, 128), lambda i: (0, i))
    return pallas(
        attend_kernel,
        grid=(KV_HEADS,),
        in_specs=[SCALAR, SCALAR, qs, kv, kv, kv, kv],
        out_specs=[qs, pl.BlockSpec((1, 8, tokens), lambda i: (i, 0, 0))],
        out_shape=[jax.ShapeDtypeStruct(q.shape, BF16), jax.ShapeDtypeStruct((KV_HEADS, 8, tokens), F32)],
        scratch_shapes=[pltpu.VMEM((tokens, tokens), F32)],
        compiler_params=params(),
        cost_estimate=cost(0.1),
        name="attend",
    )(g, prefix, q, k0, v0, k1, v1)


def attend_back_kernel(g_ref, prefix_ref, q_ref, k0_ref, v0_ref, k1_ref, v1_ref, do_ref, lse_ref,
                       cos_ref, sin_ref, dq_ref, own_ref, early_ref, bias):
    g = g_ref[0]
    which = pl.program_id(0) % 2

    @pl.when(pl.program_id(0) == 0)
    def _():
        fill_bias(bias, prefix_ref, g)

    def run(blocks):
        q = q_ref[...].astype(F32)
        do = do_ref[...].astype(F32)
        keys = [doubled(b[0][...], which) for b in blocks]
        keys_t = [k.T[:HEAD].astype(BF16) for k in keys]
        keys = [k.astype(BF16) for k in keys]
        values = [doubled(b[1][...], which).astype(BF16) for b in blocks]
        dks = [0.0 for _ in blocks]
        dvs = [0.0 for _ in blocks]
        dqs = []
        for a in range(2):
            half = lane_half(q.shape, a)
            qa = (q * half).astype(BF16)
            doa = (do * half).astype(BF16)
            lse = lse_ref[0, a : a + 1, :]
            scores = [nt(k, qa) for k in keys]
            scores[0] = scores[0] + bias[...]
            probs = [jnp.exp(s - lse) for s in scores]
            dps = [nt(v, doa) for v in values]
            delta = sum(jnp.sum(p * dp, 0, keepdims=True) for p, dp in zip(probs, dps))
            dq = 0.0
            for n in range(len(blocks)):
                ds = (probs[n] * (dps[n] - delta)).astype(BF16)
                dvs[n] = dvs[n] + nn(probs[n].astype(BF16), doa)
                dks[n] = dks[n] + nn(ds, qa)
                dq = dq + nn(keys_t[n], ds)
            dqs.append(dq)
        dq = jnp.concatenate(dqs, 0).T * (1.0 / math.sqrt(HEAD))
        dq_ref[...] = rotated(dq, cos_ref[...], sin_ref[...], -1.0).astype(BF16)
        for n, (_, _, outs) in enumerate(blocks):
            for ref, grad in zip(outs, (dks[n], dvs[n])):
                both = grad + pltpu.roll(grad, HEAD, 1)
                part = both * lane_half(both.shape, which)

                @pl.when(which == 0)
                def _():
                    ref[...] = part.astype(ref.dtype)

                @pl.when(which != 0)
                def _():
                    ref[...] = (ref[...].astype(F32) + part).astype(ref.dtype)

    own = (k0_ref, v0_ref, (own_ref.at[0], own_ref.at[1]))
    earlier = (k1_ref, v1_ref, (early_ref.at[0], early_ref.at[1]))

    @pl.when(g == 0)
    def _():
        run([own])
        early_ref[...] = jnp.zeros_like(early_ref)

    @pl.when(g != 0)
    def _():
        run([own, earlier])


def attend_back(g, prefix, q, k0, v0, k1, v1, do, lse, cosine, sine, first, count):
    tokens = q.shape[0]
    kv = pl.BlockSpec((tokens, LANES), lambda i: (0, first // 2 + i // 2))
    qs = pl.BlockSpec((tokens, LANES), lambda i: (0, first + i))
    both = pl.BlockSpec((2, tokens, LANES), lambda i: (0, 0, i // 2))
    shape = jax.ShapeDtypeStruct
    kv_shape = (2, tokens, count * HEAD)
    return pallas(
        attend_back_kernel,
        grid=(count,),
        in_specs=[SCALAR, SCALAR, qs, kv, kv, kv, kv, qs,
                  pl.BlockSpec((1, 8, tokens), lambda i: (first + i, 0, 0)),
                  whole((tokens, LANES)), whole((tokens, LANES))],
        out_specs=[pl.BlockSpec((tokens, LANES), lambda i: (0, i)), both, both],
        out_shape=[shape((tokens, count * LANES), BF16), shape(kv_shape, F32), shape(kv_shape, BF16)],
        scratch_shapes=[pltpu.VMEM((tokens, tokens), F32)],
        compiler_params=params(),
        cost_estimate=cost(0.1),
        name="attend_back",
    )(g, prefix, q, k0, v0, k1, v1, do, lse, cosine, sine)


def output_kernel(where_ref, a_ref, wo0, wo1, wo2, x_ref, gain_ref, res_ref, n_ref):
    res = x_ref[...].astype(F32) + project_rows(a_ref, where_ref, (wo0, wo1, wo2))
    res_ref[...] = res
    scale = lax.rsqrt(jnp.mean(res * res, -1, keepdims=True) + EPSILON)
    n_ref[...] = (res * scale * gain_ref[...]).astype(BF16)


def output(where, attended, wo, x, gain):
    tokens, width = x.shape
    rows = 256
    row = pl.BlockSpec((rows, width), lambda i: (i, 0))
    return pallas(
        output_kernel,
        grid=(tokens // rows,),
        in_specs=[SCALAR, row, *(whole(w.shape) for w in wo), row, whole((1, width))],
        out_specs=[row, row],
        out_shape=[jax.ShapeDtypeStruct((tokens, width), F32), jax.ShapeDtypeStruct((tokens, width), BF16)],
        compiler_params=params(),
        cost_estimate=cost(0.1),
        name="output",
    )(where, attended, *wo, x, gain)


def gates_of(rows, router_t, member):
    logits = jnp.where(member > 0.0, nt(rows, router_t), MASKED)
    peak = jnp.max(logits, -1, keepdims=True)
    weights = jnp.where(member > 0.0, jnp.exp(logits - peak), 0.0)
    return weights / jnp.sum(weights, -1, keepdims=True)


def experts_kernel(*refs, first, start, adding, carrying, final):
    refs = list(refs)
    take = lambda n: [refs.pop(0) for _ in range(n)]
    g_ref, x, c = take(3)
    if first:
        member, router, order = take(3)
    else:
        gates, xt, ct = take(3)
    win, wout = take(2)
    keep_in, send_in = take(2) if adding else (None, None)
    grad_in, sum_in, gg_in = take(3) if carrying else (None, None, None)
    keep, send, grad, total = take(4)
    gg_out = None if final else take(1)[0]
    if first:
        gates, xt, ct = take(3)
    hid_scr, dgu_scr, grad_scr, sum_scr, gg_scr = take(5)
    step = pl.program_id(0)
    width = x.shape[1]
    column = g_ref[0] * (EXPERTS // 2) + start + step

    @pl.when(step == 0)
    def _():
        if first:
            gates[...] = gates_of(x[...], router[...], member[...])
            xt[...] = nt(order[...], x[...]).astype(BF16)
            ct[...] = nt(order[...], c[...]).astype(BF16)
        gg_scr[...] = gg_in[...] if carrying else jnp.zeros_like(gg_scr)

    probs = gates[...]
    mine = lax.broadcasted_iota(jnp.int32, probs.shape, 1) == column
    p = jnp.sum(jnp.where(mine, probs, 0.0), 1, keepdims=True)
    gate_up = nn(x[...], win[0])
    back = nn(c[...], wout[0])
    gate, up = gate_up[:, :FF], gate_up[:, FF:]
    sig = 1.0 / (1.0 + jnp.exp(-gate))
    act = gate * sig
    hid = act * up
    gg_scr[...] = jnp.where(mine, jnp.sum(hid * back, 1, keepdims=True), gg_scr[...])
    back = back * p
    dgate = back * up * (sig * (1.0 + gate * (1.0 - sig)))
    hid_scr[...] = (hid * p).astype(BF16)
    dgu_scr[:, :FF] = dgate.astype(BF16)
    dgu_scr[:, FF:] = (back * act).astype(BF16)
    for scr, old, value in ((sum_scr, sum_in, nt(hid_scr[...], wout[0])), (grad_scr, grad_in, nt(dgu_scr[...], win[0]))):

        @pl.when(step == 0)
        def _():
            scr[...] = value + old[...] if carrying else value

        @pl.when(step != 0)
        def _():
            scr[...] += value

    for out, old, base in ((keep, keep_in, 0), (send, send_in, width // 2)):
        rows = pl.ds(base, width // 2)
        for cols, left, right in ((slice(0, 2 * FF), xt, dgu_scr), (slice(2 * FF, 3 * FF), ct, hid_scr)):
            value = nn(left[rows], right[...])
            if adding:
                value = value + old[0, :, cols].astype(F32)
            out[0, :, cols] = value.astype(BF16)

    @pl.when(step == pl.num_programs(0) - 1)
    def _():
        total[...] = sum_scr[...].astype(total.dtype)
        if final:
            grad[:, :width] = grad_scr[...].astype(BF16)
            grad[:, width:] = gg_scr[...].astype(BF16)
        else:
            grad[...] = grad_scr[...]
            gg_out[...] = gg_scr[...]


def experts(g, x, c, win, wout, start, count, fresh=None, known=None, adding=None, carrying=None, final=False):
    tokens, width = x.shape
    cols = 3 * FF
    shape = jax.ShapeDtypeStruct
    half = pl.BlockSpec((1, width // 2, cols), lambda i: (i, 0, 0))
    wide, narrow = (tokens, width), (tokens, LANES)
    args = [g, x, c]
    specs = [SCALAR, whole(wide), whole(wide)]
    for a in fresh or known:
        args.append(a)
        specs.append(whole(a.shape))
    args += [win, wout]
    specs += [pl.BlockSpec((1, width, 2 * FF), lambda i: (start + i, 0, 0)),
              pl.BlockSpec((1, width, FF), lambda i: (start + i, 0, 0))]
    if adding:
        args += adding
        specs += [half, half]
    if carrying:
        args += carrying
        specs += [whole(wide), whole(wide), whole(narrow)]
    outs = [half, half]
    shapes = [shape((count, width // 2, cols), BF16), shape((count, width // 2, cols), BF16)]
    ends = [((tokens, width + LANES), BF16), (wide, BF16)] if final else [(wide, F32), (wide, F32), (narrow, F32)]
    if fresh:
        ends += [(narrow, F32), ((width, tokens), BF16), ((width, tokens), BF16)]
    outs += [whole(size) for size, _ in ends]
    shapes += [shape(size, kind) for size, kind in ends]
    return pallas(
        functools.partial(experts_kernel, first=fresh is not None, start=start, adding=adding is not None,
                          carrying=carrying is not None, final=final),
        grid=(count,),
        in_specs=specs,
        out_specs=outs,
        out_shape=shapes,
        scratch_shapes=[pltpu.VMEM((tokens, FF), BF16), pltpu.VMEM((tokens, 2 * FF), BF16),
                        pltpu.VMEM(wide, F32), pltpu.VMEM(wide, F32), pltpu.VMEM(narrow, F32)],
        compiler_params=params(60),
        cost_estimate=cost(8 * count),
        name="experts",
    )(*args)


def middle_kernel(where_ref, c_ref, grad_ref, back_ref, gg_ref, p_ref, router_ref, res_ref, gain_ref,
                  wo0, wo1, wo2, dres_ref, low_ref, da_ref, dl_ref, dgain_ref):
    width = c_ref.shape[1]
    p = p_ref[...]
    gg = gg_ref[...] + back_ref[:, width:].astype(F32)
    dlogits = p * (gg - jnp.sum(p * gg, 1, keepdims=True))
    dl_ref[...] = dlogits.astype(BF16)
    high = dlogits.astype(BF16)
    rest = (dlogits - high.astype(F32)).astype(BF16)
    router = router_ref[...]
    grad = grad_ref[...] + back_ref[:, :width].astype(F32) + (nn(high, router) + nn(rest, router))
    res = res_ref[...]
    scale = lax.rsqrt(jnp.mean(res * res, -1, keepdims=True) + EPSILON)
    part = jnp.broadcast_to(jnp.sum(grad * (res * scale), 0, keepdims=True), dgain_ref.shape)

    @pl.when(pl.program_id(0) == 0)
    def _():
        dgain_ref[...] = part

    @pl.when(pl.program_id(0) != 0)
    def _():
        dgain_ref[...] += part

    w = grad * gain_ref[...]
    dres = c_ref[...].astype(F32) + (scale * w - res * (scale * scale * scale)
                                     * jnp.mean(w * res, -1, keepdims=True))
    dres_ref[...] = dres
    low = dres.astype(BF16)
    low_ref[...] = low
    for at, wo in zip(pieces(where_ref, width), (wo0, wo1, wo2)):
        da_ref[:, at] = nt(low, wo[...]).astype(BF16)


def middle(where, c, grad, back, gg, p, router_t, res, gain, wo):
    tokens, width = c.shape
    rows = 256
    row = lambda n: pl.BlockSpec((rows, n), lambda i: (i, 0))
    shape = jax.ShapeDtypeStruct
    return pallas(
        middle_kernel,
        grid=(tokens // rows,),
        in_specs=[SCALAR, row(width), row(width), row(width + LANES), row(LANES), row(LANES),
                  whole((LANES, width)), row(width), whole((1, width)), *(whole(w.shape) for w in wo)],
        out_specs=[row(width), row(width), row(width), row(LANES), pl.BlockSpec((8, width), lambda i: (0, 0))],
        out_shape=[shape((tokens, width), F32), shape((tokens, width), BF16), shape((tokens, width), BF16),
                   shape((tokens, LANES), BF16), shape((8, width), F32)],
        compiler_params=params(),
        cost_estimate=cost(100),
        name="middle",
    )(where, c, grad, back, gg, p, router_t, res, gain, *wo)


def weight_kernel(*refs, joined, pieces_sent):
    refs = list(refs)
    take = lambda n: [refs.pop(0) for _ in range(n)]
    xt, dq, own, early, cos, sin = take(6)
    order, low, att, xt_ffn, dlogits, dgain = take(6) if joined else [None] * 6
    keep, dkv = take(2)
    sends = take(pieces_sent)
    half = keep.shape[0]
    dk = rotated(own[0] + early[0].astype(F32), cos[...], sin[...], -1.0).astype(BF16)
    dv = (own[1] + early[1].astype(F32)).astype(BF16)
    nq, nk = dq.shape[1], dk.shape[1]
    dkv[:, :nk] = dk
    dkv[:, nk:] = dv
    if joined:
        low_t, gain_rows = take(2)
        low_t[...] = nt(order[...], low[...]).astype(BF16)
        row = lax.broadcasted_iota(jnp.int32, gain_rows.shape, 0)
        gain_rows[...] = jnp.where(row == EXPERTS, dgain[0:1, :], 0.0).astype(BF16)
    def put(cols, rows, value):
        value = value.astype(BF16)
        if rows.start == 0:
            keep[:, cols] = value
        else:
            size = half // pieces_sent
            for n, send in enumerate(sends):
                send[:, cols] = value[n * size : (n + 1) * size]

    for base in (0, half):
        rows = pl.ds(base, half)
        put(slice(0, nq), rows, nn(xt[rows], dq[...]))
        first = nq + 2 * nk
        put(slice(nq, first), rows, nn(xt[rows], dkv[...]))
        if joined:
            wide = att.shape[1]
            put(slice(first, first + wide), rows, nn(low_t[rows], att[...]))
            put(slice(first + wide, first + wide + LANES), rows,
                nn(xt_ffn[rows], dlogits[...]) + nt(order[rows], gain_rows[...]))


def weight_grads(xt, dq, own, early, cosine, sine, pieces_sent, joined=None):
    width, tokens = xt.shape
    nq, nk = dq.shape[1], own.shape[2]
    shape = jax.ShapeDtypeStruct
    cols = nq + 2 * nk + (joined[2].shape[1] + LANES if joined else 0)
    out = shape((width // 2, cols), BF16)
    vmem = pl.BlockSpec(memory_space=pltpu.VMEM)
    args = (xt, dq, own, early, cosine, sine, *(joined or ()))
    sent = shape((width // 2 // pieces_sent, cols), BF16)
    return pallas(
        functools.partial(weight_kernel, joined=bool(joined), pieces_sent=pieces_sent),
        in_specs=[vmem] * len(args),
        out_specs=[vmem] * (2 + pieces_sent),
        out_shape=[out, shape((tokens, 2 * nk), BF16)] + [sent] * pieces_sent,
        scratch_shapes=[pltpu.VMEM((width, tokens), BF16), pltpu.VMEM((LANES, width), BF16)] if joined else [],
        compiler_params=params(),
        cost_estimate=cost(0.1),
        name="weight_grads",
    )(*args)


def input_kernel(where_ref, *refs, parts):
    refs = list(refs)
    take = lambda n: [refs.pop(0) for _ in range(n)]
    dqs, dkvs, wq, wk, wv = take(parts), take(parts), take(1), take(1), take(1)
    packs = take(2)
    x_ref, gain_ref, dres_ref, out_ref, grad = refs
    nq, nk = wq[0].shape[1], wk[0].shape[1]
    columns = []
    for n in range(parts):
        q0, k0 = n * nq // parts, n * nk // parts
        q1, k1 = q0 + nq // parts, k0 + nk // parts
        dkv = dkvs[n][...]
        half = dkv.shape[1] // 2
        for left, own, first, (lo, hi) in (
                (dqs[n][...], wq[0], 0, (q0, q1)),
                (dkv[:, :half], wk[0], nq, (k0, k1)),
                (dkv[:, half:], wv[0], nq + nk, (k0, k1))):
            columns.append((left, own, slice(lo, hi), slice(first + lo, first + hi)))
    at = pieces(where_ref, x_ref.shape[1])
    grad[:, at[0]] = sum(nt(left, own[:, mine]) for left, own, mine, _ in columns)
    for place, pack in zip(at[1:], packs):
        grad[:, place] = sum(nt(left, pack[:, packed]) for left, _, _, packed in columns)
    x = x_ref[...].astype(F32)
    scale = lax.rsqrt(jnp.mean(x * x, -1, keepdims=True) + EPSILON)
    w = grad[...] * gain_ref[...]
    out_ref[...] = dres_ref[...] + (scale * w - x * (scale * scale * scale) * jnp.mean(w * x, -1, keepdims=True))


def input_grads(where, dqs, dkvs, wq, wk, wv, pack, x, gain, dres):
    tokens, width = x.shape
    rows = 256
    row = lambda a: pl.BlockSpec((rows, a.shape[1]), lambda i: (i, 0))
    weights = (wq, wk, wv, *pack)
    return pallas(
        functools.partial(input_kernel, parts=len(dqs)),
        grid=(tokens // rows,),
        in_specs=[SCALAR, *map(row, dqs), *map(row, dkvs), *(whole(w.shape) for w in weights), row(x),
                  whole((1, width)), row(dres)],
        out_specs=row(dres),
        out_shape=jax.ShapeDtypeStruct((tokens, width), F32),
        scratch_shapes=[pltpu.VMEM((rows, width), F32)],
        compiler_params=params(),
        cost_estimate=cost(0.1),
        name="input_grads",
    )(where, *dqs, *dkvs, *weights, x, gain, dres)


def exchange(value, *bits):
    count = lax.axis_size("replica")
    flip = sum(count if b == "group" else 1 << b for b in bits)
    return lax.ppermute(value, ("group", "replica"), [(i, i ^ flip) for i in range(2 * count)])


def after(value, *others):
    out = lax.optimization_barrier((value, *others))
    return out[0], list(out[1:])


def deal(out, to, entries, rows):
    at = 0
    finest = min(p.shape[1] for part, _ in entries for p in part)
    for start, total in rows:
        for first in range(start, start + total, min(finest, total)):
            size = min(finest - first % finest, start + total - first)
            value = 0.0
            for part, e in entries:
                height = part[0].shape[1]
                inner = first % height
                value = value + part[first // height][e, inner : inner + size, :].astype(F32)
            out[to, at : at + size, :] = value.astype(BF16)
            at += size


def split_kernel(*refs, groups, ranges):
    refs = list(refs)
    parts = [[[refs.pop(0) for _ in range(n)] for n in counts] for counts, _, _ in groups]
    to = 0
    for group, (_, first, count) in zip(parts, groups):
        for n in range(count):
            entries = [(p, n + (first if p[0].shape[0] > count else 0)) for p in group]
            for out, rows in zip(refs, ranges):
                deal(out, to, entries, rows)
            to += 1


def stream_kernel(*refs, count, pieces):
    parts, outs = [[r] for r in refs[:count]], list(refs[count:])
    for first, size, ranges in pieces:
        mine = [outs.pop(0) for _ in ranges]

        @pl.when((pl.program_id(0) >= first) & (pl.program_id(0) < first + size))
        def _():
            for out, rows in zip(mine, ranges):
                deal(out, 0, [(p, 0) for p in parts], rows)


def ranges_of(axes, chunk, bits):
    spots = np.stack(np.unravel_index(np.arange(2 ** len(axes)), (2,) * len(axes)), 1)
    at = [axes.index(b) for b in bits]
    ranges = []
    for combo in np.ndindex(*(2,) * len(bits)):
        rows = []
        for n in np.nonzero((spots[:, at] == combo).all(1))[0]:
            if rows and rows[-1][0] + rows[-1][1] == n * chunk:
                rows[-1] = (rows[-1][0], rows[-1][1] + chunk)
            else:
                rows.append((int(n) * chunk, chunk))
        ranges.append(tuple(rows))
    return tuple(ranges)


def flips_of(bits):
    return [[b for b, on in zip(bits, combo) if on] for combo in list(np.ndindex(*(2,) * len(bits)))[1:]]


class Run:
    def __init__(self, parts, axes, chunk, first=0, count=1):
        self.parts, self.axes, self.chunk, self.first, self.count = list(parts), list(axes), chunk, first, count


def split(runs, *bits):
    axes, chunk = runs[0].axes, runs[0].chunk
    ranges = ranges_of(axes, chunk, bits)
    cols = runs[0].parts[0].shape[2]
    total = sum(r.count for r in runs)
    flat = lambda part: list(part) if isinstance(part, (list, tuple)) else [part]
    args = [a for r in runs for p in r.parts for a in flat(p)]
    vmem = pl.BlockSpec(memory_space=pltpu.VMEM)
    kept, *sends = pallas(
        functools.partial(
            split_kernel, ranges=ranges,
            groups=tuple((tuple(len(flat(p)) for p in r.parts), r.first, r.count) for r in runs)),
        in_specs=[vmem] * len(args),
        out_specs=[vmem] * len(ranges),
        out_shape=[jax.ShapeDtypeStruct((total, sum(n for _, n in rows), cols), BF16) for rows in ranges],
        compiler_params=params(),
        cost_estimate=cost(0.1),
        name="split",
    )(*args)
    return Run([kept, *(exchange(s, *flip) for s, flip in zip(sends, flips_of(bits)))],
               [b for b in axes if b not in bits], chunk, 0, total)


def split_apart(run, *pieces):
    rows, cols = run.parts[0].shape[1:]
    shapes, specs, plan, first = [], [], [], 0
    for bits, count in pieces:
        ranges = ranges_of(run.axes, run.chunk, bits)
        plan.append((first, count, ranges))
        for chosen in ranges:
            size = sum(n for _, n in chosen)
            shapes.append(jax.ShapeDtypeStruct((count, size, cols), BF16))
            specs.append(pl.BlockSpec(
                (1, size, cols), lambda i, first=first, count=count: (jnp.clip(i - first, 0, count - 1), 0, 0)))
        first += count
    outs = list(pallas(
        functools.partial(stream_kernel, count=len(run.parts), pieces=tuple(plan)),
        grid=(first,),
        in_specs=[pl.BlockSpec((1, rows, cols), lambda i: (i, 0, 0))] * len(run.parts),
        out_specs=specs,
        out_shape=shapes,
        compiler_params=params(),
        cost_estimate=cost(0.1),
        name="split_apart",
    )(*run.parts))
    runs = []
    for bits, count in pieces:
        kept = outs.pop(0)
        received = [exchange(outs.pop(0), *flip) for flip in flips_of(bits)]
        runs.append(Run([kept, *received], [b for b in run.axes if b not in bits], run.chunk, 0, count))
    return runs


def finish_attention_kernel(*refs, counts):
    refs = list(refs)
    take = lambda n: [refs.pop(0) for _ in range(n)]
    joined, alone = take(counts[0]), take(counts[1])
    wq, wk, wv, gain = take(4)
    dq, dk, dv, do, drouter, dgain_attn, dgain_ffn = refs
    a = sum(p[0].astype(F32) for p in joined)
    b = sum(p[0].astype(F32) for p in alone)
    nq, nk = wq.shape[1] // 2, wk.shape[1] // 2
    dgain = 0.0
    for n, part in enumerate((a, b)):
        for ref, w, size, first in ((dq, wq, nq, 0), (dk, wk, nk, nq), (dv, wv, nk, nq + nk)):
            grad = part[:, first : first + size]
            ref[:, n * size : (n + 1) * size] = grad
            dgain = dgain + jnp.sum(grad * w[:, n * size : (n + 1) * size].astype(F32), 1, keepdims=True)
    dgain_attn[...] = dgain / gain[...]
    first = nq + 2 * nk
    width = do.shape[0]
    do[...] = a[:, first : first + width].T
    last = a[:, first + width :]
    drouter[...] = last[:, :EXPERTS]
    lane = lax.broadcasted_iota(jnp.int32, last.shape, 1)
    dgain_ffn[...] = jnp.sum(jnp.where(lane == EXPERTS, last, 0.0), 1, keepdims=True)


def finish_attention(joined, alone, wq, wk, wv, gain, width):
    chunk = wq.shape[0]
    shape = lambda *s: jax.ShapeDtypeStruct(s, F32)
    args = (*joined, *alone, wq, wk, wv, gain)
    vmem = pl.BlockSpec(memory_space=pltpu.VMEM)
    return pallas(
        functools.partial(finish_attention_kernel, counts=(len(joined), len(alone))),
        in_specs=[vmem] * len(args),
        out_specs=[vmem] * 7,
        out_shape=[shape(chunk, wq.shape[1]), shape(chunk, wk.shape[1]), shape(chunk, wv.shape[1]),
                   shape(width, chunk), shape(chunk, EXPERTS), shape(chunk, 1), shape(chunk, 1)],
        compiler_params=params(),
        cost_estimate=cost(0.1),
        name="finish_attention",
    )(*args)


def finish_experts_kernel(g_ref, *refs):
    own, other, (win, wout) = refs[: len(refs) // 2 - 1], refs[len(refs) // 2 - 1 : -2], refs[-2:]
    count = win.shape[0] // 2
    g = g_ref[0]
    for parts, side in ((own, g), (other, 1 - g)):
        e = 0
        for p in parts:
            for n in range(p.shape[0]):
                win[side * count + e] = p[n, :, : 2 * FF].astype(F32)
                wout[side * count + e] = p[n, :, 2 * FF :].astype(F32)
                e += 1


def finish_experts(g, own, other):
    chunk = own[0].shape[1]
    shape = lambda *s: jax.ShapeDtypeStruct(s, F32)
    vmem = pl.BlockSpec(memory_space=pltpu.VMEM)
    return pallas(
        finish_experts_kernel,
        in_specs=[SCALAR] + [vmem] * (2 * len(own)),
        out_specs=[vmem] * 2,
        out_shape=[shape(EXPERTS, chunk, 2 * FF), shape(EXPERTS, chunk, FF)],
        compiler_params=params(),
        cost_estimate=cost(0.1),
        name="finish_experts",
    )(g, *own, *other)


def on_device(
    block_in, attn_gain, query_weight, key_weight, value_weight, out_weight, ffn_gain, router_weight,
    expert_in, expert_out, routes, prefix, cotangent,
):
    FOLLOWED.clear()
    replicas = lax.axis_size("replica")
    bits = replicas.bit_length() - 1
    tokens, width = block_in.shape[1:]
    half = width // 2
    chunk = half // replicas
    group, replica = lax.axis_index("group"), lax.axis_index("replica")
    core = replica % 2
    g = group.astype(jnp.int32).reshape(1)
    where = jnp.stack([group, core]).astype(jnp.int32)
    x, cot = block_in[0], cotangent[0]
    swap = lambda v: exchange(v, "group")

    def ordered(own, other, axis):
        return jnp.where(group == 0, jnp.concatenate([own, other], axis), jnp.concatenate([other, own], axis))

    quarter = lambda w: lax.dynamic_slice_in_dim(w, core * (w.shape[0] // 2), w.shape[0] // 2, 0)
    pack_send = jnp.concatenate([quarter(query_weight), quarter(key_weight), quarter(value_weight)], 1)
    pack = swap(pack_send)
    small = jnp.concatenate([attn_gain[None], ffn_gain[None], router_weight.T], 0)
    vectors = ordered(small, swap(small), 1)
    gain_attn, gain_ffn = vectors[0:1].astype(F32), vectors[1:2].astype(F32)
    router_t = jnp.concatenate([vectors[2:], jnp.zeros((LANES - EXPERTS, width), BF16)], 0)
    lanes = jnp.arange(LANES, dtype=jnp.int32)
    member = (routes[0][:, :, None] == lanes[None, None, :]).any(1).astype(F32)

    frequency = THETA_BASE ** (-jnp.arange(HEAD // 2, dtype=F32) * 2.0 / HEAD)

    def tables(first):
        angles = (first + jnp.arange(tokens, dtype=jnp.int32)).astype(F32)[:, None] * frequency[None, :]
        cosine, sine = jnp.cos(angles), jnp.sin(angles)
        return jnp.tile(cosine, (1, 4)), jnp.concatenate([-sine, sine, -sine, sine], 1)

    cosine, sine = tables(group * tokens)
    early_tables = tables(0)
    place = np.arange(width)
    blocks, inner = place // chunk, place % chunk
    reverse = np.zeros_like(blocks)
    for b in range(bits):
        reverse |= ((blocks >> 1 >> (bits - 1 - b)) & 1) << b
    feature = ((jnp.asarray(blocks & 1, jnp.int32) ^ group) * half
               + (jnp.asarray(reverse, jnp.int32) ^ replica) * chunk + jnp.asarray(inner, jnp.int32))
    order = (feature[:, None] == jnp.arange(width, dtype=jnp.int32)[None, :]).astype(BF16)

    mine = lambda a: lax.dynamic_slice_in_dim(a, replica * chunk, chunk, 0)
    rows = (mine(query_weight), mine(key_weight), mine(value_weight), mine(attn_gain).astype(F32)[:, None])
    pack, (cosine, sine, member, order, x_send, gain_attn, wo_send, cot_send, *more) = after(
        pack, cosine, sine, member, order, x, gain_attn, quarter(out_weight), cot, *early_tables, *rows)
    early_tables, rows = more[:2], more[2:]
    x_early = lax.ppermute(x_send, "group", [(0, 1)])
    pack = (pack, exchange(pack, 0))

    normed_attn, q, k, v = project(where, x, gain_attn, query_weight, key_weight, value_weight, pack, cosine, sine)
    normed_t = nt(order, normed_attn).astype(BF16)
    x_early, (q, normed_t) = after(x_early, q, normed_t)
    wo = swap(wo_send)
    cot_other = swap(cot_send)
    k1, v1 = project_earlier(where, x_early, gain_attn, key_weight, value_weight, pack, *early_tables)
    attended, lse = attend(g, prefix, q, k, v, k1, v1)
    wo, (attended,) = after(wo, attended)
    wo = (out_weight, wo, exchange(wo, 0))
    residual, normed = output(where, attended, wo, x, gain_ffn)
    member_other = swap(member.astype(BF16)).astype(F32)
    normed, (cot_other, member_other) = after(normed, cot_other, member_other)
    normed_other = swap(normed)
    count = expert_in.shape[0] // 2
    near = lambda *a, **k: experts(g, normed, cot, expert_in, expert_out, *a, **k)
    far = lambda *a, **k: experts(g, *a[0], expert_in, expert_out, *a[1:], **k)
    keep, send, grad_own, sum_own, gg_own, *known = near(0, count, fresh=(member, router_t, order))
    gates, xt_own, _ = known
    normed_other, (keep,) = after(normed_other, keep)
    keep_a, send_a, *sums, gates_o, xt_o, ct_o = far(
        (normed_other, cot_other), 0, count, fresh=(member_other, router_t, order), adding=(keep, send))
    received_a = exchange(send_a, 0)
    keep, send, back, sum_other = far(
        (normed_other, cot_other), count, count, known=(gates_o, xt_o, ct_o), carrying=sums, final=True)
    back = swap(back)
    dims = [*range(1, bits), "group"]
    two = count // 2
    first, second, *rest = [*range(1, bits)]
    run_a = Run((keep_a, received_a), dims, chunk, 0, count)
    run0, run1 = split_apart(run_a, ((first,), two), ((second,), two))
    keep_b, send_b, grad_own, sum_own, gg_own = near(
        count, count, known=known, adding=(keep, send), carrying=(grad_own, sum_own, gg_own))
    back, (keep_b, sum_send) = after(back, keep_b, sum_other)
    run_b = Run((keep_b, exchange(send_b, 0)), dims, chunk, 0, count)
    sum_other = swap(sum_send)
    run0, run1 = split([run0], second), split([run1], first)

    grad_res, grad_low, grad_att, grad_logits, grad_gain = middle(
        where, cot, grad_own, back, gg_own, gates, router_t, residual, gain_ffn, wo)
    run2, run3 = split_apart(run_b, ((first,), two), ((second,), two))
    heads = KV_HEADS // 2
    attn = lambda first: attend_back(g, prefix, q, k, v, k1, v1, grad_att, lse, cosine, sine, first, heads)
    to_earlier = lambda a: lax.ppermute(a, "group", [(1, 0)])
    dq0, own0, early0 = attn(0)
    early0 = to_earlier(early0)
    FOLLOWED.append(sum_other)
    for bit in rest:
        run0, run1 = split([run0], bit), split([run1], bit)
    dq1, own1, early1 = attn(heads)
    early1 = to_earlier(early1)
    run2, run3 = split([run2], second), split([run3], first)
    one = lambda keep, sends: Run((keep[None], [exchange(s, 0)[None] for s in sends]), dims, chunk)
    keep0, dkv0, *sends = weight_grads(
        normed_t, dq0, own0, early0, cosine, sine, 1,
        joined=(order, grad_low, attended, xt_own, grad_logits, grad_gain))
    attn0 = one(keep0, sends)
    pairs = lambda *bits: [bits[i : i + 2] for i in range(0, len(bits), 2)]
    pairs0, pairs1 = pairs(second, first, "group", *rest), pairs("group", second, first, *rest)
    attn0 = split([attn0], *pairs0[0])
    keep1, dkv1, *sends = weight_grads(normed_t, dq1, own1, early1, cosine, sine, 1)
    attn1 = one(keep1, sends)
    swap_a = split([run0, run1], "group")
    input_grad = input_grads(where, (dq0, dq1), (dkv0, dkv1), query_weight, key_weight, value_weight, pack,
                             x, gain_attn, grad_res)
    attn1 = split([attn1], *pairs1[0])
    for bit in rest:
        run2, run3 = split([run2], bit), split([run3], bit)
    for pair0, pair1 in zip(pairs0[1:], pairs1[1:]):
        attn0 = split([attn0], *pair0)
        attn1 = split([attn1], *pair1)
    swap_b = split([run2, run3], "group")
    block_out = (residual + sum_own + sum_other.astype(F32)).astype(BF16)

    query_grad, key_grad, value_grad, out_grad, router_grad, attn_gain_grad, ffn_gain_grad = finish_attention(
        attn0.parts, attn1.parts, *rows, width)
    expert_in_grad, expert_out_grad = finish_experts(
        g, (swap_a.parts[0], swap_b.parts[0]), (swap_a.parts[1], swap_b.parts[1]))
    return (
        block_out[None], input_grad[None], attn_gain_grad[:, 0], query_grad, key_grad, value_grad, out_grad,
        ffn_gain_grad[:, 0], router_grad, expert_in_grad, expert_out_grad,
    )


def solution(mesh):
    placed = (
        P("replica", "group", None),
        P("group"),
        P("group", None),
        P("group", None),
        P("group", None),
        P("group", None),
        P("group"),
        P("group", None),
        P("group", None, None),
        P("group", None, None),
        P("replica", "group", None),
        P("replica"),
        P("replica", "group", None),
    )
    both = ("group", "replica")
    return jax.shard_map(
        on_device,
        mesh=mesh,
        in_specs=placed,
        out_specs=(
            P("replica", "group", None),
            P("replica", "group", None),
            P(both),
            P(both, None),
            P(both, None),
            P(both, None),
            P(None, both),
            P(both),
            P(both, None),
            P(None, both, None),
            P(None, both, None),
        ),
        check_vma=False,
    )
```

```python
import functools
import math

import jax
import jax.numpy as jnp
import numpy as np
from jax import lax
from jax.experimental import pallas as pl
from jax.experimental.pallas import tpu as pltpu
from jax.sharding import PartitionSpec as P

HEADS = 16
KV_HEADS = 8
HEAD = 64
FF = 512
TOP = 8
EXPERTS = 16

EPSILON = 1e-06
THETA_BASE = 10000.0
MASKED = -1e30
HIGHEST = lax.Precision.HIGHEST
F32 = jnp.float32
BF16 = jnp.bfloat16
MIB = 1 << 20


def nn(left, right):
    return lax.dot_general(left, right, (((1,), (0,)), ((), ())), preferred_element_type=F32)


def nt(left, right):
    return lax.dot_general(left, right, (((1,), (1,)), ((), ())), preferred_element_type=F32)


def params(limit=24):
    return pltpu.CompilerParams(vmem_limit_bytes=limit * MIB)


def cost(microseconds):
    return pl.CostEstimate(flops=int(microseconds * 0.9e9), bytes_accessed=int(microseconds * 1e5), transcendentals=0)


def whole(shape):
    return pl.BlockSpec(shape, lambda *_: (0,) * len(shape), pipeline_mode=pl.Buffered(1))


SCALAR = pl.BlockSpec(memory_space=pltpu.SMEM)

FOLLOWED = []


def pallas(kernel, *, in_specs, out_shape, **more):
    def call(*args):
        tokens, count = list(FOLLOWED), len(in_specs)

        def body(*refs):
            kernel(*refs[:count], *refs[count + len(tokens) :])

        out = pl.pallas_call(
            body,
            in_specs=[*in_specs, *[pl.BlockSpec(memory_space=pl.ANY)] * len(tokens)],
            out_shape=out_shape,
            **more,
        )(*args, *tokens)
        FOLLOWED[:] = [min(jax.tree.leaves(out), key=lambda a: a.size)]
        return out

    return call
LANES = 128


def pieces(where_ref, width):
    g, core = where_ref[0], where_ref[1]
    half, quarter = width // 2, width // 4
    other = (1 - g) * half
    at = lambda start, size: pl.ds(pl.multiple_of(start, size), size)
    return (at(g * half, half), at(other + core * quarter, quarter), at(other + (1 - core) * quarter, quarter))


def project_rows(ref, where_ref, weights):
    cols = pieces(where_ref, ref.shape[1])
    return sum(nn(ref[:, c], w[...]) for c, w in zip(cols, weights))


def swap_halves(tile):
    lane = lax.broadcasted_iota(jnp.int32, tile.shape, 1) % HEAD
    return jnp.where(
        lane < HEAD // 2, pltpu.roll(tile, 128 - HEAD // 2, 1), pltpu.roll(tile, HEAD // 2, 1)
    )


def rotated(values, cosine, sine, sign):
    tiles = []
    for start in range(0, values.shape[1], 128):
        tile = values[:, start : start + 128]
        tiles.append(tile * cosine + swap_halves(tile) * (sine * sign))
    return tiles[0] if len(tiles) == 1 else jnp.concatenate(tiles, 1)


def tables_kernel(g_ref, rate_ref, cos_ref, sin_ref, early_cos_ref, early_sin_ref):
    shape = cos_ref.shape
    lane = lax.broadcasted_iota(jnp.int32, shape, 1)
    row = lax.broadcasted_iota(jnp.int32, shape, 0)
    sign = jnp.where(lane % HEAD < HEAD // 2, -1.0, 1.0)
    for first, cos, sin in ((g_ref[0] * shape[0], cos_ref, sin_ref), (0, early_cos_ref, early_sin_ref)):
        angle = (row + first).astype(F32) * rate_ref[...]
        cos[...] = jnp.cos(angle)
        sin[...] = jnp.sin(angle) * sign


def tables(g, tokens):
    rate = THETA_BASE ** (-jnp.arange(HEAD // 2, dtype=F32) * 2.0 / HEAD)
    shape = jax.ShapeDtypeStruct((tokens, LANES), F32)
    vmem = pl.BlockSpec(memory_space=pltpu.VMEM)
    return pallas(
        tables_kernel,
        in_specs=[SCALAR, vmem],
        out_specs=[vmem] * 4,
        out_shape=[shape] * 4,
        compiler_params=params(),
        cost_estimate=cost(0.1),
        name="tables",
    )(g, jnp.tile(rate, LANES * 2 // HEAD)[None])


def project_kernel(where_ref, x_ref, gain_ref, wq0, wq1, wq2, wk0, wk1, wk2, wv0, wv1, wv2, cos_ref, sin_ref,
                   order_ref, n_ref, q_ref, k_ref, v_ref, nt_ref):
    @pl.when(pl.program_id(0) == 0)
    def _():
        x = x_ref[...].astype(F32)
        scale = lax.rsqrt(jnp.mean(x * x, -1, keepdims=True) + EPSILON)
        n_ref[...] = (x * scale * gain_ref[...]).astype(BF16)

    cosine, sine = cos_ref[...], sin_ref[...]
    q = rotated(project_rows(n_ref, where_ref, (wq0, wq1, wq2)), cosine, sine, 1.0)
    q_ref[...] = q.astype(BF16) * jnp.asarray(1.0 / math.sqrt(HEAD), BF16)
    k = rotated(project_rows(n_ref, where_ref, (wk0, wk1, wk2)), cosine, sine, 1.0)
    k_ref[...] = k.astype(BF16)
    v_ref[...] = project_rows(n_ref, where_ref, (wv0, wv1, wv2)).astype(BF16)
    nt_ref[...] = nt(order_ref[...], n_ref[...]).astype(BF16)


def project_earlier_kernel(where_ref, x_ref, gain_ref, wk0, wk1, wk2, wv0, wv1, wv2, cos_ref, sin_ref,
                           k_ref, v_ref, n_ref):
    @pl.when(where_ref[0] != 0)
    def _():
        @pl.when(pl.program_id(0) == 0)
        def _():
            x = x_ref[...].astype(F32)
            scale = lax.rsqrt(jnp.mean(x * x, -1, keepdims=True) + EPSILON)
            n_ref[...] = (x * scale * gain_ref[...]).astype(BF16)

        k = rotated(project_rows(n_ref, where_ref, (wk0, wk1, wk2)), cos_ref[...], sin_ref[...], 1.0)
        k_ref[...] = k.astype(BF16)
        v_ref[...] = project_rows(n_ref, where_ref, (wv0, wv1, wv2)).astype(BF16)

    @pl.when(where_ref[0] == 0)
    def _():
        k_ref[...] = jnp.zeros_like(k_ref)
        v_ref[...] = jnp.zeros_like(v_ref)


def weight_specs(rows, n, first):
    packed = pl.BlockSpec((rows // 2, n), lambda i: (0, first // n + i))
    return [pl.BlockSpec((rows, n), lambda i: (0, i)), packed, packed]


def project(where, x, gain, wq, wk, wv, pack, cosine, sine, order):
    tokens, width = x.shape
    steps = 4
    half = width // 2
    nq, nk = wq.shape[1], wk.shape[1]
    qb, kb = nq // steps, nk // steps
    o_spec = lambda n: pl.BlockSpec((tokens, n), lambda i: (0, i))
    shape = jax.ShapeDtypeStruct
    return pallas(
        project_kernel,
        grid=(steps,),
        in_specs=[SCALAR, whole((tokens, width)), whole((1, width)),
                  *weight_specs(half, qb, 0), *weight_specs(half, kb, 0), *weight_specs(half, kb, nk),
                  whole((tokens, LANES)), whole((tokens, LANES)),
                  pl.BlockSpec((width // steps, width), lambda i: (i, 0))],
        out_specs=[pl.BlockSpec((tokens, width), lambda i: (0, 0)), o_spec(qb), o_spec(kb), o_spec(kb),
                   pl.BlockSpec((width // steps, tokens), lambda i: (i, 0))],
        out_shape=[shape((tokens, width), BF16), shape((tokens, nq), BF16), shape((tokens, nk), BF16),
                   shape((tokens, nk), BF16), shape((width, tokens), BF16)],
        compiler_params=params(62),
        cost_estimate=cost(3),
        name="project",
    )(where, x, gain, wq, *pack[0], wk, *pack[1], wv, *pack[1], cosine, sine, order)


def project_earlier(where, x, gain, wk, wv, pack, cosine, sine):
    tokens, width = x.shape
    steps = 2
    half = width // 2
    nk = wk.shape[1]
    kb = nk // steps
    o_spec = pl.BlockSpec((tokens, kb), lambda i: (0, i))
    shape = jax.ShapeDtypeStruct
    return pallas(
        project_earlier_kernel,
        grid=(steps,),
        in_specs=[SCALAR, whole((tokens, width)), whole((1, width)),
                  *weight_specs(half, kb, 0), *weight_specs(half, kb, nk),
                  whole((tokens, LANES)), whole((tokens, LANES))],
        out_specs=[o_spec, o_spec],
        out_shape=[shape((tokens, nk), BF16), shape((tokens, nk), BF16)],
        scratch_shapes=[pltpu.VMEM((tokens, width), BF16)],
        compiler_params=params(62),
        cost_estimate=cost(0.1),
        name="project_earlier",
    )(where, x, gain, wk, *pack[1], wv, *pack[1], cosine, sine)


def lane_half(shape, which):
    lane = lax.broadcasted_iota(jnp.int32, shape, 1)
    return ((lane // HEAD) % 2 == which).astype(F32)


def doubled(tile, which):
    kept = tile.astype(F32) * lane_half(tile.shape, which)
    return kept + pltpu.roll(kept, HEAD, 1)


def fill_bias(bias, prefix_ref, g):
    shape = bias.shape
    key = lax.broadcasted_iota(jnp.int32, shape, 0)
    query = lax.broadcasted_iota(jnp.int32, shape, 1)
    seen = (key <= query) | (key + g * shape[0] < prefix_ref[0])
    bias[...] = jnp.where(seen, 0.0, MASKED)


def attend_kernel(g_ref, prefix_ref, q_ref, k0_ref, v0_ref, k1_ref, v1_ref, o_ref, lse_ref, bias):
    g = g_ref[0]
    which = pl.program_id(0) % 2

    @pl.when(pl.program_id(0) == 0)
    def _():
        fill_bias(bias, prefix_ref, g)

    def run(blocks):
        q = q_ref[...].astype(F32)
        keys = [doubled(k[...], which).astype(BF16) for k, _ in blocks]
        values = [doubled(v[...], which).T[:HEAD].astype(BF16) for _, v in blocks]
        outs = []
        for a in range(2):
            qa = (q * lane_half(q.shape, a)).astype(BF16)
            scores = [nt(k, qa) for k in keys]
            scores[0] = scores[0] + bias[...]
            peak = functools.reduce(jnp.maximum, [jnp.max(s, 0, keepdims=True) for s in scores])
            weights = [jnp.exp(s - peak) for s in scores]
            total = sum(jnp.sum(w, 0, keepdims=True) for w in weights)
            out = sum(nn(v, w.astype(BF16)) for v, w in zip(values, weights))
            outs.append(out * (1.0 / total))
            lse_ref[0, a : a + 1, :] = peak + jnp.log(total)
        o_ref[...] = jnp.concatenate(outs, 0).T.astype(BF16)

    @pl.when(g == 0)
    def _():
        run([(k0_ref, v0_ref)])

    @pl.when(g != 0)
    def _():
        run([(k0_ref, v0_ref), (k1_ref, v1_ref)])


def attend(g, prefix, q, k0, v0, k1, v1):
    tokens = q.shape[0]
    kv = pl.BlockSpec((tokens, 128), lambda i: (0, i // 2))
    qs = pl.BlockSpec((tokens, 128), lambda i: (0, i))
    return pallas(
        attend_kernel,
        grid=(KV_HEADS,),
        in_specs=[SCALAR, SCALAR, qs, kv, kv, kv, kv],
        out_specs=[qs, pl.BlockSpec((1, 8, tokens), lambda i: (i, 0, 0))],
        out_shape=[jax.ShapeDtypeStruct(q.shape, BF16), jax.ShapeDtypeStruct((KV_HEADS, 8, tokens), F32)],
        scratch_shapes=[pltpu.VMEM((tokens, tokens), F32)],
        compiler_params=params(),
        cost_estimate=cost(0.1),
        name="attend",
    )(g, prefix, q, k0, v0, k1, v1)


def attend_back_kernel(g_ref, prefix_ref, q_ref, k0_ref, v0_ref, k1_ref, v1_ref, do_ref, lse_ref,
                       cos_ref, sin_ref, dq_ref, own_ref, early_ref, bias):
    g = g_ref[0]
    which = pl.program_id(0) % 2

    @pl.when(pl.program_id(0) == 0)
    def _():
        fill_bias(bias, prefix_ref, g)

    def run(blocks):
        q = q_ref[...].astype(F32)
        do = do_ref[...].astype(F32)
        keys = [doubled(b[0][...], which) for b in blocks]
        keys_t = [k.T[:HEAD].astype(BF16) for k in keys]
        keys = [k.astype(BF16) for k in keys]
        values = [doubled(b[1][...], which).astype(BF16) for b in blocks]
        dks = [0.0 for _ in blocks]
        dvs = [0.0 for _ in blocks]
        dqs = []
        for a in range(2):
            half = lane_half(q.shape, a)
            qa = (q * half).astype(BF16)
            doa = (do * half).astype(BF16)
            lse = lse_ref[0, a : a + 1, :]
            scores = [nt(k, qa) for k in keys]
            scores[0] = scores[0] + bias[...]
            probs = [jnp.exp(s - lse) for s in scores]
            dps = [nt(v, doa) for v in values]
            delta = sum(jnp.sum(p * dp, 0, keepdims=True) for p, dp in zip(probs, dps))
            dq = 0.0
            for n in range(len(blocks)):
                ds = (probs[n] * (dps[n] - delta)).astype(BF16)
                dvs[n] = dvs[n] + nn(probs[n].astype(BF16), doa)
                dks[n] = dks[n] + nn(ds, qa)
                dq = dq + nn(keys_t[n], ds)
            dqs.append(dq)
        dq = jnp.concatenate(dqs, 0).T * (1.0 / math.sqrt(HEAD))
        dq_ref[...] = rotated(dq, cos_ref[...], sin_ref[...], -1.0).astype(BF16)
        for n, (_, _, outs) in enumerate(blocks):
            for ref, grad in zip(outs, (dks[n], dvs[n])):
                both = grad + pltpu.roll(grad, HEAD, 1)
                part = both * lane_half(both.shape, which)

                @pl.when(which == 0)
                def _():
                    ref[...] = part.astype(ref.dtype)

                @pl.when(which != 0)
                def _():
                    ref[...] = (ref[...].astype(F32) + part).astype(ref.dtype)

    own = (k0_ref, v0_ref, (own_ref.at[0], own_ref.at[1]))
    earlier = (k1_ref, v1_ref, (early_ref.at[0], early_ref.at[1]))

    @pl.when(g == 0)
    def _():
        run([own])
        early_ref[...] = jnp.zeros_like(early_ref)

    @pl.when(g != 0)
    def _():
        run([own, earlier])


def attend_back(g, prefix, q, k0, v0, k1, v1, do, lse, cosine, sine, first, count):
    tokens = q.shape[0]
    kv = pl.BlockSpec((tokens, LANES), lambda i: (0, first // 2 + i // 2))
    qs = pl.BlockSpec((tokens, LANES), lambda i: (0, first + i))
    both = pl.BlockSpec((2, tokens, LANES), lambda i: (0, 0, i // 2))
    shape = jax.ShapeDtypeStruct
    kv_shape = (2, tokens, count * HEAD)
    return pallas(
        attend_back_kernel,
        grid=(count,),
        in_specs=[SCALAR, SCALAR, qs, kv, kv, kv, kv, qs,
                  pl.BlockSpec((1, 8, tokens), lambda i: (first + i, 0, 0)),
                  whole((tokens, LANES)), whole((tokens, LANES))],
        out_specs=[pl.BlockSpec((tokens, LANES), lambda i: (0, i)), both, both],
        out_shape=[shape((tokens, count * LANES), BF16), shape(kv_shape, F32), shape(kv_shape, BF16)],
        scratch_shapes=[pltpu.VMEM((tokens, tokens), F32)],
        compiler_params=params(),
        cost_estimate=cost(12),
        name="attend_back",
    )(g, prefix, q, k0, v0, k1, v1, do, lse, cosine, sine)


def output_kernel(where_ref, a_ref, wo0, wo1, wo2, x_ref, gain_ref, res_ref, n_ref):
    res = x_ref[...].astype(F32) + project_rows(a_ref, where_ref, (wo0, wo1, wo2))
    res_ref[...] = res
    scale = lax.rsqrt(jnp.mean(res * res, -1, keepdims=True) + EPSILON)
    n_ref[...] = (res * scale * gain_ref[...]).astype(BF16)


def halves_spec(w):
    shape = (w.shape[0] // 2, w.shape[1])
    return [pl.BlockSpec(shape, lambda *_, n=n: (n, 0), pipeline_mode=pl.Buffered(1)) for n in range(2)]


def output(where, attended, wo, x, gain):
    tokens, width = x.shape
    rows = 256
    row = pl.BlockSpec((rows, width), lambda i: (i, 0))
    return pallas(
        output_kernel,
        grid=(tokens // rows,),
        in_specs=[SCALAR, row, whole(wo[0].shape), *halves_spec(wo[1]), row, whole((1, width))],
        out_specs=[row, row],
        out_shape=[jax.ShapeDtypeStruct((tokens, width), F32), jax.ShapeDtypeStruct((tokens, width), BF16)],
        compiler_params=params(),
        cost_estimate=cost(0.1),
        name="output",
    )(where, attended, *wo, wo[1], x, gain)


def gates_of(rows, router_t, member):
    logits = jnp.where(member > 0.0, nt(rows, router_t), MASKED)
    peak = jnp.max(logits, -1, keepdims=True)
    weights = jnp.where(member > 0.0, jnp.exp(logits - peak), 0.0)
    return weights / jnp.sum(weights, -1, keepdims=True)


def experts_kernel(*refs, first, start, adding, carrying, final):
    refs = list(refs)
    take = lambda n: [refs.pop(0) for _ in range(n)]
    g_ref, x, c = take(3)
    if first:
        member, router, order_in = take(3)
    else:
        gates, xt_in, ct_in = take(3)
    win, wout = take(2)
    olds_in = [take(2) for _ in adding]
    grad_in, sum_in, gg_in = take(3) if carrying else (None, None, None)
    keep, send, grad, total = take(4)
    gg_out = None if final else take(1)[0]
    if first:
        gates, xt_out, ct_out = take(3)
    hid_scr, dgu_scr, grad_scr, sum_scr, gg_scr, xt, ct, sems = take(8)
    order = take(1)[0] if first else None
    keep_old, send_old = take(2) if adding else (None, None)
    grad_low, sum_low = take(2) if final else (grad_scr, sum_scr)
    step = pl.program_id(0)
    at_start, at_end = step == 0, step == pl.num_programs(0) - 1
    width = x.shape[1]
    column = g_ref[0] * (EXPERTS // 2) + start + step
    copy = lambda n, source, target: pltpu.make_async_copy(source, target, sems.at[n])
    loads = [copy(0, order_in, order)] if first else [copy(0, xt_in, xt), copy(1, ct_in, ct)]
    sums_in = [copy(2, grad_in, grad_scr), copy(3, sum_in, sum_scr)] if carrying else []
    olds, before = [], 0
    for (keep_in, send_in), (skip, number) in zip(olds_in, adding):
        at = step - before + skip
        olds.append((before, number, [copy(4, keep_in.at[at], keep_old), copy(5, send_in.at[at], send_old)]))
        before += number

    def for_olds(act):
        for before, number, copies in olds:

            @pl.when((step >= before) & (step < before + number))
            def _():
                for old in copies:
                    act(old)

    sums_out = [copy(6, grad_low, grad), copy(7, sum_low, total)]
    turned_out = [copy(8, xt, xt_out), copy(9, ct, ct_out)] if first else []

    @pl.when(at_start)
    def _():
        for load in loads + sums_in:
            load.start()
        if first:
            gates[...] = gates_of(x[...], router[...], member[...])
        gg_scr[...] = gg_in[...] if carrying else jnp.zeros_like(gg_scr)

    for_olds(lambda old: old.start())
    probs = gates[...]
    mine = lax.broadcasted_iota(jnp.int32, probs.shape, 1) == column
    p = jnp.sum(jnp.where(mine, probs, 0.0), 1, keepdims=True)
    gate_up = nn(x[...], win[0])
    back = nn(c[...], wout[0])
    gate, up = gate_up[:, :FF], gate_up[:, FF:]
    sig = 1.0 / (1.0 + jnp.exp(-gate))
    act = gate * sig
    hid = act * up
    gg_scr[...] = jnp.where(mine, jnp.sum(hid * back, 1, keepdims=True), gg_scr[...])
    back = back * p
    dgate = back * up * (sig * (1.0 + gate * (1.0 - sig)))
    hid_scr[...] = (hid * p).astype(BF16)
    dgu_scr[:, :FF] = dgate.astype(BF16)
    dgu_scr[:, FF:] = (back * act).astype(BF16)

    if carrying:

        @pl.when(at_start)
        def _():
            for load in sums_in:
                load.wait()

    for scr, value in ((sum_scr, nt(hid_scr[...], wout[0])), (grad_scr, nt(dgu_scr[...], win[0]))):
        if carrying:
            scr[...] += value
        else:

            @pl.when(at_start)
            def _():
                scr[...] = value

            @pl.when(jnp.logical_not(at_start))
            def _():
                scr[...] += value

    @pl.when(at_end)
    def _():
        if final:
            sum_low[...] = sum_scr[...].astype(BF16)
            grad_low[:, :width] = grad_scr[...].astype(BF16)
            grad_low[:, width:] = gg_scr[...].astype(BF16)
        else:
            gg_out[...] = gg_scr[...]
        for store in sums_out:
            store.start()

    @pl.when(at_start)
    def _():
        for load in loads:
            load.wait()
        if first:
            xt[...] = nt(order[...], x[...]).astype(BF16)
            ct[...] = nt(order[...], c[...]).astype(BF16)
            for store in turned_out:
                store.start()

    for_olds(lambda old: old.wait())
    for out, old, base in ((keep, keep_old, 0), (send, send_old, width // 2)):
        rows = pl.ds(base, width // 2)
        for cols, left, right in ((slice(0, 2 * FF), xt, dgu_scr), (slice(2 * FF, 3 * FF), ct, hid_scr)):
            value = nn(left[rows], right[...])
            if adding:
                value = value + old[:, cols].astype(F32)
            out[0, :, cols] = value.astype(BF16)

    @pl.when(at_end)
    def _():
        for store in sums_out + turned_out:
            store.wait()


def experts(g, x, c, win, wout, start, count, fresh=None, known=None, adding=(), carrying=None, final=False):
    tokens, width = x.shape
    cols = 3 * FF
    shape = jax.ShapeDtypeStruct
    half = pl.BlockSpec((1, width // 2, cols), lambda i: (i, 0, 0))
    anywhere = pl.BlockSpec(memory_space=pl.ANY)
    wide, narrow, turned = (tokens, width), (tokens, LANES), (width, tokens)
    back = (tokens, width + LANES)
    args = [g, x, c, *(fresh or known), win, wout]
    specs = [SCALAR, whole(wide), whole(wide)]
    specs += [whole(narrow), whole(fresh[1].shape), anywhere] if fresh else [whole(narrow), anywhere, anywhere]
    specs += [pl.BlockSpec((1, width, 2 * FF), lambda i: (start + i, 0, 0)),
              pl.BlockSpec((1, width, FF), lambda i: (start + i, 0, 0))]
    for keep, send, _, _ in adding:
        args += [keep, send]
        specs += [anywhere, anywhere]
    if carrying:
        args += carrying
        specs += [anywhere, anywhere, whole(narrow)]
    outs = [half, half, anywhere, anywhere]
    shapes = [shape((count, width // 2, cols), BF16), shape((count, width // 2, cols), BF16)]
    if final:
        shapes += [shape(back, BF16), shape(wide, BF16)]
    else:
        outs += [whole(narrow)]
        shapes += [shape(wide, F32), shape(wide, F32), shape(narrow, F32)]
    if fresh:
        outs += [whole(narrow), anywhere, anywhere]
        shapes += [shape(narrow, F32), shape(turned, BF16), shape(turned, BF16)]
    scratch = [pltpu.VMEM((tokens, FF), BF16), pltpu.VMEM((tokens, 2 * FF), BF16),
               pltpu.VMEM(wide, F32), pltpu.VMEM(wide, F32), pltpu.VMEM(narrow, F32),
               pltpu.VMEM(turned, BF16), pltpu.VMEM(turned, BF16), pltpu.SemaphoreType.DMA((10,))]
    if fresh:
        scratch += [pltpu.VMEM((width, width), BF16)]
    if adding:
        scratch += [pltpu.VMEM((width // 2, cols), BF16)] * 2
    if final:
        scratch += [pltpu.VMEM(back, BF16), pltpu.VMEM(wide, BF16)]
    return pallas(
        functools.partial(experts_kernel, first=fresh is not None, start=start,
                          adding=tuple(entries for _, _, *entries in adding),
                          carrying=carrying is not None, final=final),
        grid=(count,),
        in_specs=specs,
        out_specs=outs,
        out_shape=shapes,
        scratch_shapes=scratch,
        compiler_params=params(62),
        cost_estimate=cost((3 if adding and carrying else 8) * count),
        name="experts",
    )(*args)


def middle_kernel(where_ref, c_ref, grad_ref, back_ref, gg_ref, p_ref, router_ref, res_ref, gain_ref,
                  wo0, wo1, wo2, dres_ref, low_ref, da_ref, dl_ref, dgain_ref):
    width = c_ref.shape[1]
    p = p_ref[...]
    gg = gg_ref[...] + back_ref[:, width:].astype(F32)
    dlogits = p * (gg - jnp.sum(p * gg, 1, keepdims=True))
    dl_ref[...] = dlogits.astype(BF16)
    high = dlogits.astype(BF16)
    rest = (dlogits - high.astype(F32)).astype(BF16)
    router = router_ref[...]
    grad = grad_ref[...] + back_ref[:, :width].astype(F32) + (nn(high, router) + nn(rest, router))
    res = res_ref[...]
    scale = lax.rsqrt(jnp.mean(res * res, -1, keepdims=True) + EPSILON)
    part = jnp.broadcast_to(jnp.sum(grad * (res * scale), 0, keepdims=True), dgain_ref.shape)

    @pl.when(pl.program_id(0) == 0)
    def _():
        dgain_ref[...] = part

    @pl.when(pl.program_id(0) != 0)
    def _():
        dgain_ref[...] += part

    w = grad * gain_ref[...]
    dres = c_ref[...].astype(F32) + (scale * w - res * (scale * scale * scale)
                                     * jnp.mean(w * res, -1, keepdims=True))
    dres_ref[...] = dres
    low = dres.astype(BF16)
    low_ref[...] = low
    for at, wo in zip(pieces(where_ref, width), (wo0, wo1, wo2)):
        da_ref[:, at] = nt(low, wo[...]).astype(BF16)


def middle(where, c, grad, back, gg, p, router_t, res, gain, wo):
    tokens, width = c.shape
    rows = 256
    row = lambda n: pl.BlockSpec((rows, n), lambda i: (i, 0))
    shape = jax.ShapeDtypeStruct
    return pallas(
        middle_kernel,
        grid=(tokens // rows,),
        in_specs=[SCALAR, row(width), row(width), row(width + LANES), row(LANES), row(LANES),
                  whole((LANES, width)), row(width), whole((1, width)), whole(wo[0].shape), *halves_spec(wo[1])],
        out_specs=[row(width), row(width), row(width), row(LANES), pl.BlockSpec((8, width), lambda i: (0, 0))],
        out_shape=[shape((tokens, width), F32), shape((tokens, width), BF16), shape((tokens, width), BF16),
                   shape((tokens, LANES), BF16), shape((8, width), F32)],
        compiler_params=params(),
        cost_estimate=cost(100),
        name="middle",
    )(where, c, grad, back, gg, p, router_t, res, gain, *wo, wo[1])


def weight_kernel(*refs, joined, pieces_sent):
    refs = list(refs)
    take = lambda n: [refs.pop(0) for _ in range(n)]
    xt, dq, own, early, cos, sin = take(6)
    order, low, att, xt_ffn, dlogits, dgain = take(6) if joined else [None] * 6
    keep, dkv = take(2)
    sends = take(pieces_sent)
    half = keep.shape[0]
    dk = rotated(own[0] + early[0].astype(F32), cos[...], sin[...], -1.0).astype(BF16)
    dv = (own[1] + early[1].astype(F32)).astype(BF16)
    nq, nk = dq.shape[1], dk.shape[1]
    dkv[:, :nk] = dk
    dkv[:, nk:] = dv
    if joined:
        low_t, gain_rows = take(2)
        low_t[...] = nt(order[...], low[...]).astype(BF16)
        row = lax.broadcasted_iota(jnp.int32, gain_rows.shape, 0)
        gain_rows[...] = jnp.where(row == EXPERTS, dgain[0:1, :], 0.0).astype(BF16)
    def put(cols, rows, value):
        value = value.astype(BF16)
        if rows.start == 0:
            keep[:, cols] = value
        else:
            size = half // pieces_sent
            for n, send in enumerate(sends):
                send[:, cols] = value[n * size : (n + 1) * size]

    for base in (0, half):
        rows = pl.ds(base, half)
        put(slice(0, nq), rows, nn(xt[rows], dq[...]))
        first = nq + 2 * nk
        put(slice(nq, first), rows, nn(xt[rows], dkv[...]))
        if joined:
            wide = att.shape[1]
            put(slice(first, first + wide), rows, nn(low_t[rows], att[...]))
            put(slice(first + wide, first + wide + LANES), rows,
                nn(xt_ffn[rows], dlogits[...]) + nt(order[rows], gain_rows[...]))


def weight_grads(xt, dq, own, early, cosine, sine, pieces_sent, joined=None):
    width, tokens = xt.shape
    nq, nk = dq.shape[1], own.shape[2]
    shape = jax.ShapeDtypeStruct
    cols = nq + 2 * nk + (joined[2].shape[1] + LANES if joined else 0)
    out = shape((width // 2, cols), BF16)
    vmem = pl.BlockSpec(memory_space=pltpu.VMEM)
    args = (xt, dq, own, early, cosine, sine, *(joined or ()))
    sent = shape((width // 2 // pieces_sent, cols), BF16)
    return pallas(
        functools.partial(weight_kernel, joined=bool(joined), pieces_sent=pieces_sent),
        in_specs=[vmem] * len(args),
        out_specs=[vmem] * (2 + pieces_sent),
        out_shape=[out, shape((tokens, 2 * nk), BF16)] + [sent] * pieces_sent,
        scratch_shapes=[pltpu.VMEM((width, tokens), BF16), pltpu.VMEM((LANES, width), BF16)] if joined else [],
        compiler_params=params(),
        cost_estimate=cost(0.1 if joined else 60),
        name="weight_grads",
    )(*args)


def input_kernel(where_ref, *refs, parts):
    refs = list(refs)
    take = lambda n: [refs.pop(0) for _ in range(n)]
    dqs, dkvs, wq, wk, wv = take(parts), take(parts), take(1), take(1), take(1)
    packs = take(4)
    x_ref, gain_ref, dres_ref, out_ref, grad = refs
    nq, nk = wq[0].shape[1], wk[0].shape[1]
    columns = []
    for n in range(parts):
        q0, k0 = n * nq // parts, n * nk // parts
        q1, k1 = q0 + nq // parts, k0 + nk // parts
        dkv = dkvs[n][...]
        half = dkv.shape[1] // 2
        for left, own, first, (lo, hi) in (
                (dqs[n][...], wq[0], None, (q0, q1)),
                (dkv[:, :half], wk[0], 0, (k0, k1)),
                (dkv[:, half:], wv[0], nk, (k0, k1))):
            packed = slice(lo, hi) if first is None else slice(first + lo, first + hi)
            columns.append((left, own, slice(lo, hi), (first is not None, packed)))
    at = pieces(where_ref, x_ref.shape[1])
    grad[:, at[0]] = sum(nt(left, own[:, mine]) for left, own, mine, _ in columns)
    for place, pack in zip(at[1:], (packs[0::2], packs[1::2])):
        grad[:, place] = sum(nt(left, pack[which][:, packed]) for left, _, _, (which, packed) in columns)
    x = x_ref[...].astype(F32)
    scale = lax.rsqrt(jnp.mean(x * x, -1, keepdims=True) + EPSILON)
    w = grad[...] * gain_ref[...]
    out_ref[...] = dres_ref[...] + (scale * w - x * (scale * scale * scale) * jnp.mean(w * x, -1, keepdims=True))


def input_grads(where, dqs, dkvs, wq, wk, wv, pack, x, gain, dres):
    tokens, width = x.shape
    rows = 256
    row = lambda a: pl.BlockSpec((rows, a.shape[1]), lambda i: (i, 0))
    weights = (wq, wk, wv, *pack[0], *pack[1])
    return pallas(
        functools.partial(input_kernel, parts=len(dqs)),
        grid=(tokens // rows,),
        in_specs=[SCALAR, *map(row, dqs), *map(row, dkvs), *(whole(w.shape) for w in weights), row(x),
                  whole((1, width)), row(dres)],
        out_specs=row(dres),
        out_shape=jax.ShapeDtypeStruct((tokens, width), F32),
        scratch_shapes=[pltpu.VMEM((rows, width), F32)],
        compiler_params=params(),
        cost_estimate=cost(5),
        name="input_grads",
    )(where, *dqs, *dkvs, *weights, x, gain, dres)


def exchange(value, *bits):
    count = lax.axis_size("replica")
    flip = sum(count if b == "group" else 1 << b for b in bits)
    return lax.ppermute(value, ("group", "replica"), [(i, i ^ flip) for i in range(2 * count)])


def after(value, *others):
    out = lax.optimization_barrier((value, *others))
    return out[0], list(out[1:])


def deal(out, to, entries, rows):
    at = 0
    finest = min(p.shape[1] for part, _ in entries for p in part)
    for start, total in rows:
        for first in range(start, start + total, min(finest, total)):
            size = min(finest - first % finest, start + total - first)
            value = 0.0
            for part, e in entries:
                height = part[0].shape[1]
                inner = first % height
                value = value + part[first // height][e, inner : inner + size, :].astype(F32)
            out[to, at : at + size, :] = value.astype(BF16)
            at += size


def split_kernel(*refs, groups, ranges):
    refs = list(refs)
    parts = [[[refs.pop(0) for _ in range(n)] for n in counts] for counts, _, _ in groups]
    to = 0
    for group, (_, first, count) in zip(parts, groups):
        for n in range(count):
            entries = [(p, n + (first if p[0].shape[0] > count else 0)) for p in group]
            for out, rows in zip(refs, ranges):
                deal(out, to, entries, rows)
            to += 1


def stream_kernel(*refs, count, pieces):
    parts, outs = [[r] for r in refs[:count]], list(refs[count:])
    for first, size, ranges in pieces:
        mine = [outs.pop(0) for _ in ranges]

        @pl.when((pl.program_id(0) >= first) & (pl.program_id(0) < first + size))
        def _():
            for out, rows in zip(mine, ranges):
                deal(out, 0, [(p, 0) for p in parts], rows)


def ranges_of(axes, chunk, bits):
    spots = np.stack(np.unravel_index(np.arange(2 ** len(axes)), (2,) * len(axes)), 1)
    at = [axes.index(b) for b in bits]
    ranges = []
    for combo in np.ndindex(*(2,) * len(bits)):
        rows = []
        for n in np.nonzero((spots[:, at] == combo).all(1))[0]:
            if rows and rows[-1][0] + rows[-1][1] == n * chunk:
                rows[-1] = (rows[-1][0], rows[-1][1] + chunk)
            else:
                rows.append((int(n) * chunk, chunk))
        ranges.append(tuple(rows))
    return tuple(ranges)


def flips_of(bits):
    return [[b for b, on in zip(bits, combo) if on] for combo in list(np.ndindex(*(2,) * len(bits)))[1:]]


class Run:
    def __init__(self, parts, axes, chunk, first=0, count=1):
        self.parts, self.axes, self.chunk, self.first, self.count = list(parts), list(axes), chunk, first, count


def split(runs, *bits):
    axes, chunk = runs[0].axes, runs[0].chunk
    ranges = ranges_of(axes, chunk, bits)
    cols = runs[0].parts[0].shape[2]
    total = sum(r.count for r in runs)
    flat = lambda part: list(part) if isinstance(part, (list, tuple)) else [part]
    args = [a for r in runs for p in r.parts for a in flat(p)]
    vmem = pl.BlockSpec(memory_space=pltpu.VMEM)
    kept, *sends = pallas(
        functools.partial(
            split_kernel, ranges=ranges,
            groups=tuple((tuple(len(flat(p)) for p in r.parts), r.first, r.count) for r in runs)),
        in_specs=[vmem] * len(args),
        out_specs=[vmem] * len(ranges),
        out_shape=[jax.ShapeDtypeStruct((total, sum(n for _, n in rows), cols), BF16) for rows in ranges],
        compiler_params=params(),
        cost_estimate=cost(0.1),
        name="split",
    )(*args)
    return Run([kept, *(exchange(s, *flip) for s, flip in zip(sends, flips_of(bits)))],
               [b for b in axes if b not in bits], chunk, 0, total)


def split_each_kernel(*refs, counts, firsts, sizes, ranges):
    refs = list(refs)
    parts = [[[refs.pop(0)] for _ in range(n)] for n in counts]
    for part, first, size, chosen in zip(parts, firsts, sizes, ranges):
        outs = [refs.pop(0) for _ in chosen]
        for n in range(size):
            entries = [(p, n + (first if p[0].shape[0] > size else 0)) for p in part]
            for out, rows in zip(outs, chosen):
                deal(out, n, entries, rows)


def split_each(*pieces):
    ranges = tuple(ranges_of(run.axes, run.chunk, (bit,)) for run, bit in pieces)
    args = [p for run, _ in pieces for p in run.parts]
    shapes = [
        jax.ShapeDtypeStruct((run.count, sum(n for _, n in rows), run.parts[0].shape[2]), BF16)
        for (run, _), chosen in zip(pieces, ranges) for rows in chosen]
    vmem = pl.BlockSpec(memory_space=pltpu.VMEM)
    outs = list(pallas(
        functools.partial(
            split_each_kernel, ranges=ranges, counts=tuple(len(run.parts) for run, _ in pieces),
            firsts=tuple(run.first for run, _ in pieces), sizes=tuple(run.count for run, _ in pieces)),
        in_specs=[vmem] * len(args),
        out_specs=[vmem] * len(shapes),
        out_shape=shapes,
        compiler_params=params(),
        cost_estimate=cost(0.1),
        name="split_each",
    )(*args))
    made = []
    for run, bit in pieces:
        kept, send = outs.pop(0), outs.pop(0)
        made.append(Run([kept, exchange(send, bit)], [b for b in run.axes if b != bit], run.chunk, 0, run.count))
    return made


def split_apart(run, *pieces):
    rows, cols = run.parts[0].shape[1:]
    shapes, specs, plan, first = [], [], [], 0
    for bits, count in pieces:
        ranges = ranges_of(run.axes, run.chunk, bits)
        plan.append((first, count, ranges))
        for chosen in ranges:
            size = sum(n for _, n in chosen)
            shapes.append(jax.ShapeDtypeStruct((count, size, cols), BF16))
            specs.append(pl.BlockSpec(
                (1, size, cols), lambda i, first=first, count=count: (jnp.clip(i - first, 0, count - 1), 0, 0)))
        first += count
    outs = list(pallas(
        functools.partial(stream_kernel, count=len(run.parts), pieces=tuple(plan)),
        grid=(first,),
        in_specs=[pl.BlockSpec((1, rows, cols), lambda i: (i, 0, 0))] * len(run.parts),
        out_specs=specs,
        out_shape=shapes,
        compiler_params=params(),
        cost_estimate=cost(0.1),
        name="split_apart",
    )(*run.parts))
    runs = []
    for bits, count in pieces:
        kept = outs.pop(0)
        received = [exchange(outs.pop(0), *flip) for flip in flips_of(bits)]
        runs.append(Run([kept, *received], [b for b in run.axes if b not in bits], run.chunk, 0, count))
    return runs


def block_sum(residual, own, other):
    def kernel(a, b, c, out):
        out[...] = (a[...] + b[...] + c[...].astype(F32)).astype(BF16)

    tokens, width = residual.shape
    row = pl.BlockSpec((tokens // 4, width), lambda i: (i, 0))
    return pallas(
        kernel,
        grid=(4,),
        in_specs=[row] * 3,
        out_specs=row,
        out_shape=jax.ShapeDtypeStruct(residual.shape, BF16),
        compiler_params=params(),
        cost_estimate=cost(0.1),
        name="block_sum",
    )(residual, own, other)


def finish_attention_kernel(*refs, counts):
    refs = list(refs)
    take = lambda n: [refs.pop(0) for _ in range(n)]
    joined, alone = take(counts[0]), take(counts[1])
    wq, wk, wv, gain = take(4)
    dq, dk, dv, do, drouter, dgain_attn, dgain_ffn = refs
    a = sum(p[0].astype(F32) for p in joined)
    b = sum(p[0].astype(F32) for p in alone)
    nq, nk = wq.shape[1] // 2, wk.shape[1] // 2
    dgain = 0.0
    for n, part in enumerate((a, b)):
        for ref, w, size, first in ((dq, wq, nq, 0), (dk, wk, nk, nq), (dv, wv, nk, nq + nk)):
            grad = part[:, first : first + size]
            ref[:, n * size : (n + 1) * size] = grad
            dgain = dgain + jnp.sum(grad * w[:, n * size : (n + 1) * size].astype(F32), 1, keepdims=True)
    dgain_attn[...] = dgain / gain[...]
    first = nq + 2 * nk
    width = do.shape[0]
    do[...] = a[:, first : first + width].T
    last = a[:, first + width :]
    drouter[...] = last[:, :EXPERTS]
    lane = lax.broadcasted_iota(jnp.int32, last.shape, 1)
    dgain_ffn[...] = jnp.sum(jnp.where(lane == EXPERTS, last, 0.0), 1, keepdims=True)


def finish_attention(joined, alone, wq, wk, wv, gain, width):
    chunk = wq.shape[0]
    shape = lambda *s: jax.ShapeDtypeStruct(s, F32)
    args = (*joined, *alone, wq, wk, wv, gain)
    vmem = pl.BlockSpec(memory_space=pltpu.VMEM)
    return pallas(
        functools.partial(finish_attention_kernel, counts=(len(joined), len(alone))),
        in_specs=[vmem] * len(args),
        out_specs=[vmem] * 7,
        out_shape=[shape(chunk, wq.shape[1]), shape(chunk, wk.shape[1]), shape(chunk, wv.shape[1]),
                   shape(width, chunk), shape(chunk, EXPERTS), shape(chunk, 1), shape(chunk, 1)],
        compiler_params=params(),
        cost_estimate=cost(0.1),
        name="finish_attention",
    )(*args)


def finish_experts_kernel(g_ref, *refs):
    own, other, (win, wout) = refs[: len(refs) // 2 - 1], refs[len(refs) // 2 - 1 : -2], refs[-2:]
    count = win.shape[0] // 2
    g = g_ref[0]
    for parts, side in ((own, g), (other, 1 - g)):
        e = 0
        for p in parts:
            for n in range(p.shape[0]):
                win[side * count + e] = p[n, :, : 2 * FF].astype(F32)
                wout[side * count + e] = p[n, :, 2 * FF :].astype(F32)
                e += 1


def finish_experts(g, own, other):
    chunk = own[0].shape[1]
    shape = lambda *s: jax.ShapeDtypeStruct(s, F32)
    vmem = pl.BlockSpec(memory_space=pltpu.VMEM)
    return pallas(
        finish_experts_kernel,
        in_specs=[SCALAR] + [vmem] * (2 * len(own)),
        out_specs=[vmem] * 2,
        out_shape=[shape(EXPERTS, chunk, 2 * FF), shape(EXPERTS, chunk, FF)],
        compiler_params=params(),
        cost_estimate=cost(0.1),
        name="finish_experts",
    )(g, *own, *other)


def on_device(
    block_in, attn_gain, query_weight, key_weight, value_weight, out_weight, ffn_gain, router_weight,
    expert_in, expert_out, routes, prefix, cotangent,
):
    FOLLOWED.clear()
    replicas = lax.axis_size("replica")
    bits = replicas.bit_length() - 1
    tokens, width = block_in.shape[1:]
    half = width // 2
    chunk = half // replicas
    group, replica = lax.axis_index("group"), lax.axis_index("replica")
    core = replica % 2
    g = group.astype(jnp.int32).reshape(1)
    where = jnp.stack([group, core]).astype(jnp.int32)
    x, cot = block_in[0], cotangent[0]
    swap = lambda v: exchange(v, "group")

    def ordered(own, other, axis):
        return jnp.where(group == 0, jnp.concatenate([own, other], axis), jnp.concatenate([other, own], axis))

    quarter = lambda w: lax.dynamic_slice_in_dim(w, core * (w.shape[0] // 2), w.shape[0] // 2, 0)
    pack_q, pack_kv = quarter(query_weight), jnp.concatenate([quarter(key_weight), quarter(value_weight)], 1)
    pack_q, (pack_kv, x_send, wo_send, cot_send) = after(pack_q, pack_kv, x, out_weight, cot)
    pack_q, pack_kv = swap(pack_q), swap(pack_kv)
    x_early = lax.ppermute(x_send, "group", [(0, 1)])
    wo = (out_weight, swap(wo_send))
    cot_other = swap(cot_send)
    lanes = jnp.arange(LANES, dtype=jnp.int32)
    member = (routes[0][:, :, None] == lanes[None, None, :]).any(1).astype(F32)
    member_t = (routes[0].T[:, None, :] == lanes[None, :EXPERTS, None]).any(0).astype(BF16)
    small = jnp.concatenate([attn_gain[None], ffn_gain[None], router_weight.T, member_t], 0)
    small_other = swap(small)
    vectors = ordered(small[: 2 + EXPERTS], small_other[: 2 + EXPERTS], 1)
    member_other = jnp.pad(small_other[2 + EXPERTS :].T.astype(F32), ((0, 0), (0, LANES - EXPERTS)))
    gain_attn, gain_ffn = vectors[0:1].astype(F32), vectors[1:2].astype(F32)
    router_t = jnp.concatenate([vectors[2:], jnp.zeros((LANES - EXPERTS, width), BF16)], 0)

    cosine, sine, *early_tables = tables(g, tokens)
    place = np.arange(width)
    blocks, inner = place // chunk, place % chunk
    reverse = np.zeros_like(blocks)
    for b in range(bits):
        reverse |= ((blocks >> 1 >> (bits - 1 - b)) & 1) << b
    feature = ((jnp.asarray(blocks & 1, jnp.int32) ^ group) * half
               + (jnp.asarray(reverse, jnp.int32) ^ replica) * chunk + jnp.asarray(inner, jnp.int32))
    order = (feature[:, None] == jnp.arange(width, dtype=jnp.int32)[None, :]).astype(BF16)

    mine = lambda a: lax.dynamic_slice_in_dim(a, replica * chunk, chunk, 0)
    rows = (mine(query_weight), mine(key_weight), mine(value_weight), mine(attn_gain).astype(F32)[:, None])
    pack_q, (pack_kv, cosine, sine, member, order, gain_attn, member_other, *more) = after(
        pack_q, pack_kv, cosine, sine, member, order, gain_attn, member_other, *early_tables, *rows)
    early_tables, rows = more[:2], more[2:]
    pack = (pack_q, exchange(pack_q, 0)), (pack_kv, exchange(pack_kv, 0))

    _, q, k, v, normed_t = project(
        where, x, gain_attn, query_weight, key_weight, value_weight, pack, cosine, sine, order)
    k1, v1 = project_earlier(where, x_early, gain_attn, key_weight, value_weight, pack, *early_tables)
    attended, lse = attend(g, prefix, q, k, v, k1, v1)
    whole_where = jnp.stack([group, 0 * core]).astype(jnp.int32)
    residual, normed = output(whole_where, attended, wo, x, gain_ffn)
    normed_other = swap(normed)
    count = expert_in.shape[0] // 2
    near = lambda *a, **k: experts(g, normed, cot, expert_in, expert_out, *a, **k)
    far = lambda *a, **k: experts(g, *a[0], expert_in, expert_out, *a[1:], **k)
    keep, send, grad_own, sum_own, gg_own, *known = near(0, count, fresh=(member, router_t, order))
    gates, xt_own, _ = known
    normed_other, (cot_other, keep) = after(normed_other, cot_other, keep)
    keep_a, send_a, *sums, gates_o, xt_o, ct_o = far(
        (normed_other, cot_other), 0, count, fresh=(member_other, router_t, order), adding=[(keep, send, 0, count)])
    received_a = exchange(send_a, 0)
    keep, send, back, sum_other = far(
        (normed_other, cot_other), count, count, known=(gates_o, xt_o, ct_o), carrying=sums, final=True)
    back = swap(back)
    two = count // 2
    dims = [*range(1, bits), "group"]
    first, second, *rest = [*range(1, bits)]
    run_a = Run((keep_a, received_a), dims, chunk, 0, count)
    run0, run1 = split_apart(run_a, ((first,), two), ((second,), two))
    sums, run_b = (grad_own, sum_own, gg_own), []
    for part in (0, two):
        keep_b, send_b, *sums = near(
            count + part, two, known=known, adding=[(keep, send, part, two)], carrying=sums)
        run_b.append(Run((keep_b, exchange(send_b, 0)), dims, chunk, 0, two))
    grad_own, sum_own, gg_own = sums
    back, (keep_b,) = after(back, keep_b)
    run0, run1 = split_each((run0, second), (run1, first))

    grad_res, grad_low, grad_att, grad_logits, grad_gain = middle(
        whole_where, cot, grad_own, back, gg_own, gates, router_t, residual, gain_ffn, wo)
    grad_low, (sum_send,) = after(grad_low, sum_other)
    sum_other = swap(sum_send)
    (run2,), (run3,) = (split_apart(run, ((first,), two)) for run in run_b)
    heads = KV_HEADS // 2
    attn = lambda first: attend_back(g, prefix, q, k, v, k1, v1, grad_att, lse, cosine, sine, first, heads)
    to_earlier = lambda a: lax.ppermute(a, "group", [(1, 0)])
    dq0, own0, early0 = attn(0)
    early0 = to_earlier(early0)
    run_a = run0, run1
    for bit in rest:
        run_a = [split(run_a, bit)]
    dq1, own1, early1 = attn(heads)
    early1 = to_earlier(early1)
    one = lambda keep, sends: Run((keep[None], [exchange(s, 0)[None] for s in sends]), dims, chunk)
    keep0, dkv0, *sends = weight_grads(
        normed_t, dq0, own0, early0, cosine, sine, 1,
        joined=(order, grad_low, attended, xt_own, grad_logits, grad_gain))
    attn0 = one(keep0, sends)
    run2 = split([run2], second)
    block_out = block_sum(residual, sum_own, sum_other)
    swap_a = split(run_a, "group")
    keep1, dkv1, *sends = weight_grads(normed_t, dq1, own1, early1, cosine, sine, 1)
    attn1 = one(keep1, sends)
    order0, order1 = ["group", first, second, *rest], [first, "group", second, *rest]
    attn0 = split([attn0], order0.pop(0))
    input_grad = input_grads(where, (dq0, dq1), (dkv0, dkv1), query_weight, key_weight, value_weight, pack,
                             x, gain_attn, grad_res)
    attn1 = split([attn1], order1.pop(0))
    run3 = split([run3], second)
    for bit in rest:
        run2 = split([run2], bit)
    for _ in range(2):
        attn0 = split([attn0], order0.pop(0))
        attn1 = split([attn1], order1.pop(0))
    for bit in rest:
        run3 = split([run3], bit)
    while order0:
        attn0 = split([attn0], order0.pop(0))
        attn1 = split([attn1], order1.pop(0))
    swap_b = split([run2, run3], "group")

    query_grad, key_grad, value_grad, out_grad, router_grad, attn_gain_grad, ffn_gain_grad = finish_attention(
        attn0.parts, attn1.parts, *rows, width)
    expert_in_grad, expert_out_grad = finish_experts(
        g, (swap_a.parts[0], swap_b.parts[0]), (swap_a.parts[1], swap_b.parts[1]))
    return (
        block_out[None], input_grad[None], attn_gain_grad[:, 0], query_grad, key_grad, value_grad, out_grad,
        ffn_gain_grad[:, 0], router_grad, expert_in_grad, expert_out_grad,
    )


def solution(mesh):
    placed = (
        P("replica", "group", None),
        P("group"),
        P("group", None),
        P("group", None),
        P("group", None),
        P("group", None),
        P("group"),
        P("group", None),
        P("group", None, None),
        P("group", None, None),
        P("replica", "group", None),
        P("replica"),
        P("replica", "group", None),
    )
    both = ("group", "replica")
    return jax.shard_map(
        on_device,
        mesh=mesh,
        in_specs=placed,
        out_specs=(
            P("replica", "group", None),
            P("replica", "group", None),
            P(both),
            P(both, None),
            P(both, None),
            P(both, None),
            P(None, both),
            P(both),
            P(both, None),
            P(None, both, None),
            P(None, both, None),
        ),
        check_vma=False,
    )
```

```python
import functools
import math

import jax
import jax.numpy as jnp
import numpy as np
from jax import lax
from jax.experimental import pallas as pl
from jax.experimental.pallas import tpu as pltpu
from jax.sharding import PartitionSpec as P

HEADS = 16
KV_HEADS = 8
HEAD = 64
FF = 512
TOP = 8
EXPERTS = 16

EPSILON = 1e-06
THETA_BASE = 10000.0
MASKED = -1e30
HIGHEST = lax.Precision.HIGHEST
F32 = jnp.float32
BF16 = jnp.bfloat16
MIB = 1 << 20


def nn(left, right):
    return lax.dot_general(left, right, (((1,), (0,)), ((), ())), preferred_element_type=F32)


def nt(left, right):
    return lax.dot_general(left, right, (((1,), (1,)), ((), ())), preferred_element_type=F32)


def params(limit=24):
    return pltpu.CompilerParams(vmem_limit_bytes=limit * MIB)


def cost(microseconds):
    return pl.CostEstimate(flops=int(microseconds * 0.9e9), bytes_accessed=int(microseconds * 1e5), transcendentals=0)


def whole(shape):
    return pl.BlockSpec(shape, lambda *_: (0,) * len(shape), pipeline_mode=pl.Buffered(1))


SCALAR = pl.BlockSpec(memory_space=pltpu.SMEM)

FOLLOWED = []


def pallas(kernel, *, in_specs, out_shape, **more):
    def call(*args):
        tokens, count = list(FOLLOWED), len(in_specs)

        def body(*refs):
            kernel(*refs[:count], *refs[count + len(tokens) :])

        out = pl.pallas_call(
            body,
            in_specs=[*in_specs, *[pl.BlockSpec(memory_space=pl.ANY)] * len(tokens)],
            out_shape=out_shape,
            **more,
        )(*args, *tokens)
        FOLLOWED[:] = [min(jax.tree.leaves(out), key=lambda a: a.size)]
        return out

    return call
LANES = 128


def pieces(where_ref, width):
    g, core = where_ref[0], where_ref[1]
    half, quarter = width // 2, width // 4
    other = (1 - g) * half
    at = lambda start, size: pl.ds(pl.multiple_of(start, size), size)
    return (at(g * half, half), at(other + core * quarter, quarter), at(other + (1 - core) * quarter, quarter))


def project_rows(ref, where_ref, weights):
    cols = pieces(where_ref, ref.shape[1])
    return sum(nn(ref[:, c], w[...]) for c, w in zip(cols, weights))


def swap_halves(tile):
    lane = lax.broadcasted_iota(jnp.int32, tile.shape, 1) % HEAD
    return jnp.where(
        lane < HEAD // 2, pltpu.roll(tile, 128 - HEAD // 2, 1), pltpu.roll(tile, HEAD // 2, 1)
    )


def rotated(values, cosine, sine, sign):
    tiles = []
    for start in range(0, values.shape[1], 128):
        tile = values[:, start : start + 128]
        tiles.append(tile * cosine + swap_halves(tile) * (sine * sign))
    return tiles[0] if len(tiles) == 1 else jnp.concatenate(tiles, 1)


def tables_kernel(g_ref, rate_ref, cos_ref, sin_ref, early_cos_ref, early_sin_ref):
    shape = cos_ref.shape
    lane = lax.broadcasted_iota(jnp.int32, shape, 1)
    row = lax.broadcasted_iota(jnp.int32, shape, 0)
    sign = jnp.where(lane % HEAD < HEAD // 2, -1.0, 1.0)
    for first, cos, sin in ((g_ref[0] * shape[0], cos_ref, sin_ref), (0, early_cos_ref, early_sin_ref)):
        angle = (row + first).astype(F32) * rate_ref[...]
        cos[...] = jnp.cos(angle)
        sin[...] = jnp.sin(angle) * sign


def tables(g, tokens):
    rate = THETA_BASE ** (-jnp.arange(HEAD // 2, dtype=F32) * 2.0 / HEAD)
    shape = jax.ShapeDtypeStruct((tokens, LANES), F32)
    vmem = pl.BlockSpec(memory_space=pltpu.VMEM)
    return pallas(
        tables_kernel,
        in_specs=[SCALAR, vmem],
        out_specs=[vmem] * 4,
        out_shape=[shape] * 4,
        compiler_params=params(),
        cost_estimate=cost(0.1),
        name="tables",
    )(g, jnp.tile(rate, LANES * 2 // HEAD)[None])


def project_kernel(where_ref, x_ref, gain_ref, wq0, wq1, wq2, wk0, wk1, wk2, wv0, wv1, wv2, cos_ref, sin_ref,
                   order_ref, n_ref, q_ref, k_ref, v_ref, nt_ref):
    @pl.when(pl.program_id(0) == 0)
    def _():
        x = x_ref[...].astype(F32)
        scale = lax.rsqrt(jnp.mean(x * x, -1, keepdims=True) + EPSILON)
        n_ref[...] = (x * scale * gain_ref[...]).astype(BF16)

    cosine, sine = cos_ref[...], sin_ref[...]
    q = rotated(project_rows(n_ref, where_ref, (wq0, wq1, wq2)), cosine, sine, 1.0)
    q_ref[...] = q.astype(BF16) * jnp.asarray(1.0 / math.sqrt(HEAD), BF16)
    k = rotated(project_rows(n_ref, where_ref, (wk0, wk1, wk2)), cosine, sine, 1.0)
    k_ref[...] = k.astype(BF16)
    v_ref[...] = project_rows(n_ref, where_ref, (wv0, wv1, wv2)).astype(BF16)
    nt_ref[...] = nt(order_ref[...], n_ref[...]).astype(BF16)


def project_earlier_kernel(where_ref, x_ref, gain_ref, wk0, wk1, wk2, wv0, wv1, wv2, cos_ref, sin_ref,
                           k_ref, v_ref, n_ref):
    @pl.when(where_ref[0] != 0)
    def _():
        @pl.when(pl.program_id(0) == 0)
        def _():
            x = x_ref[...].astype(F32)
            scale = lax.rsqrt(jnp.mean(x * x, -1, keepdims=True) + EPSILON)
            n_ref[...] = (x * scale * gain_ref[...]).astype(BF16)

        k = rotated(project_rows(n_ref, where_ref, (wk0, wk1, wk2)), cos_ref[...], sin_ref[...], 1.0)
        k_ref[...] = k.astype(BF16)
        v_ref[...] = project_rows(n_ref, where_ref, (wv0, wv1, wv2)).astype(BF16)

    @pl.when(where_ref[0] == 0)
    def _():
        k_ref[...] = jnp.zeros_like(k_ref)
        v_ref[...] = jnp.zeros_like(v_ref)


def weight_specs(rows, n, first):
    packed = pl.BlockSpec((rows // 2, n), lambda i: (0, first // n + i))
    return [pl.BlockSpec((rows, n), lambda i: (0, i)), packed, packed]


def project(where, x, gain, wq, wk, wv, pack, cosine, sine, order):
    tokens, width = x.shape
    steps = 4
    half = width // 2
    nq, nk = wq.shape[1], wk.shape[1]
    qb, kb = nq // steps, nk // steps
    o_spec = lambda n: pl.BlockSpec((tokens, n), lambda i: (0, i))
    shape = jax.ShapeDtypeStruct
    return pallas(
        project_kernel,
        grid=(steps,),
        in_specs=[SCALAR, whole((tokens, width)), whole((1, width)),
                  *weight_specs(half, qb, 0), *weight_specs(half, kb, 0), *weight_specs(half, kb, nk),
                  whole((tokens, LANES)), whole((tokens, LANES)),
                  pl.BlockSpec((width // steps, width), lambda i: (i, 0))],
        out_specs=[pl.BlockSpec((tokens, width), lambda i: (0, 0)), o_spec(qb), o_spec(kb), o_spec(kb),
                   pl.BlockSpec((width // steps, tokens), lambda i: (i, 0))],
        out_shape=[shape((tokens, width), BF16), shape((tokens, nq), BF16), shape((tokens, nk), BF16),
                   shape((tokens, nk), BF16), shape((width, tokens), BF16)],
        compiler_params=params(62),
        cost_estimate=cost(3),
        name="project",
    )(where, x, gain, wq, *pack[0], wk, *pack[1], wv, *pack[1], cosine, sine, order)


def project_earlier(where, x, gain, wk, wv, pack, cosine, sine):
    tokens, width = x.shape
    steps = 2
    half = width // 2
    nk = wk.shape[1]
    kb = nk // steps
    o_spec = pl.BlockSpec((tokens, kb), lambda i: (0, i))
    shape = jax.ShapeDtypeStruct
    return pallas(
        project_earlier_kernel,
        grid=(steps,),
        in_specs=[SCALAR, whole((tokens, width)), whole((1, width)),
                  *weight_specs(half, kb, 0), *weight_specs(half, kb, nk),
                  whole((tokens, LANES)), whole((tokens, LANES))],
        out_specs=[o_spec, o_spec],
        out_shape=[shape((tokens, nk), BF16), shape((tokens, nk), BF16)],
        scratch_shapes=[pltpu.VMEM((tokens, width), BF16)],
        compiler_params=params(62),
        cost_estimate=cost(0.1),
        name="project_earlier",
    )(where, x, gain, wk, *pack[1], wv, *pack[1], cosine, sine)


def lane_half(shape, which):
    lane = lax.broadcasted_iota(jnp.int32, shape, 1)
    return ((lane // HEAD) % 2 == which).astype(F32)


def doubled(tile, which):
    kept = tile.astype(F32) * lane_half(tile.shape, which)
    return kept + pltpu.roll(kept, HEAD, 1)


def fill_bias(bias, prefix_ref, g):
    shape = bias.shape
    key = lax.broadcasted_iota(jnp.int32, shape, 0)
    query = lax.broadcasted_iota(jnp.int32, shape, 1) % shape[0]
    seen = (key <= query) | (key + g * shape[0] < prefix_ref[0])
    bias[...] = jnp.where(seen, 0.0, MASKED)


def stacked_heads(tile):
    tile = tile.astype(F32)
    return jnp.concatenate([(tile * lane_half(tile.shape, a)).astype(BF16) for a in range(2)], 0)


def attend_kernel(g_ref, prefix_ref, q_ref, k0_ref, v0_ref, k1_ref, v1_ref, o_ref, lse_ref, bias):
    g = g_ref[0]
    which = pl.program_id(0) % 2

    @pl.when(pl.program_id(0) == 0)
    def _():
        fill_bias(bias, prefix_ref, g)

    away = jnp.where(g == 0, -MASKED, 0.0)
    tokens = q_ref.shape[0]
    q = stacked_heads(q_ref[...])
    keys = jnp.concatenate([doubled(k[...], which).astype(BF16) for k in (k0_ref, k1_ref)], 0)
    values = jnp.concatenate([doubled(v[...], which).T[:HEAD].astype(BF16) for v in (v0_ref, v1_ref)], 1)
    scores = nt(keys, q)
    own, early = scores[:tokens] + bias[...], scores[tokens:]
    peak = jnp.maximum(jnp.max(own, 0, keepdims=True), jnp.max(early, 0, keepdims=True) - away)
    own, early = jnp.exp(own - peak), jnp.exp(early - (peak + away))
    total = jnp.sum(own, 0, keepdims=True) + jnp.sum(early, 0, keepdims=True)
    out = nn(values, jnp.concatenate([own.astype(BF16), early.astype(BF16)], 0)) * (1.0 / total)
    lse = peak + jnp.log(total)
    lse_ref[0, 0:1, :] = lse[:, :tokens]
    lse_ref[0, 1:2, :] = lse[:, tokens:]
    o_ref[...] = jnp.concatenate([out[:, :tokens], out[:, tokens:]], 0).T.astype(BF16)


def attend(g, prefix, q, k0, v0, k1, v1):
    tokens = q.shape[0]
    kv = pl.BlockSpec((tokens, 128), lambda i: (0, i // 2))
    qs = pl.BlockSpec((tokens, 128), lambda i: (0, i))
    return pallas(
        attend_kernel,
        grid=(KV_HEADS,),
        in_specs=[SCALAR, SCALAR, qs, kv, kv, kv, kv],
        out_specs=[qs, pl.BlockSpec((1, 8, tokens), lambda i: (i, 0, 0))],
        out_shape=[jax.ShapeDtypeStruct(q.shape, BF16), jax.ShapeDtypeStruct((KV_HEADS, 8, tokens), F32)],
        scratch_shapes=[pltpu.VMEM((tokens, 2 * tokens), F32)],
        compiler_params=params(62),
        cost_estimate=cost(0.1),
        name="attend",
    )(g, prefix, q, k0, v0, k1, v1)


def attend_back_kernel(g_ref, prefix_ref, q_ref, k0_ref, v0_ref, k1_ref, v1_ref, do_ref, lse_ref,
                       cos_ref, sin_ref, dq_ref, own_ref, early_ref, bias):
    g = g_ref[0]
    which = pl.program_id(0) % 2

    @pl.when(pl.program_id(0) == 0)
    def _():
        fill_bias(bias, prefix_ref, g)

    away = jnp.where(g == 0, -MASKED, 0.0)
    tokens = q_ref.shape[0]
    q, do = stacked_heads(q_ref[...]), stacked_heads(do_ref[...])
    keys = [doubled(k[...], which) for k in (k0_ref, k1_ref)]
    keys_t = jnp.concatenate([k.T[:HEAD].astype(BF16) for k in keys], 1)
    keys = jnp.concatenate([k.astype(BF16) for k in keys], 0)
    values = jnp.concatenate([doubled(v[...], which).astype(BF16) for v in (v0_ref, v1_ref)], 0)
    lse = jnp.concatenate([lse_ref[0, 0:1, :], lse_ref[0, 1:2, :]], 1)
    scores = nt(keys, q)
    probs = jnp.concatenate(
        [jnp.exp(scores[:tokens] + bias[...] - lse), jnp.exp(scores[tokens:] - (lse + away))], 0)
    dprobs = nt(values, do)
    delta = jnp.sum(probs * dprobs, 0, keepdims=True)
    dscores = (probs * (dprobs - delta)).astype(BF16)
    dv = nn(probs.astype(BF16), do)
    dk = nn(dscores, q)
    dq = nn(keys_t, dscores)
    dq = jnp.concatenate([dq[:, :tokens], dq[:, tokens:]], 0).T * (1.0 / math.sqrt(HEAD))
    dq_ref[...] = rotated(dq, cos_ref[...], sin_ref[...], -1.0).astype(BF16)
    for row, grad in enumerate((dk, dv)):
        both = grad + pltpu.roll(grad, HEAD, 1)
        part = both * lane_half(both.shape, which)
        for ref, rows in ((own_ref, slice(0, tokens)), (early_ref, slice(tokens, 2 * tokens))):

            @pl.when(which == 0)
            def _():
                ref[row] = part[rows].astype(ref.dtype)

            @pl.when(which != 0)
            def _():
                ref[row] = (ref[row].astype(F32) + part[rows]).astype(ref.dtype)


def attend_back(g, prefix, q, k0, v0, k1, v1, do, lse, cosine, sine, first, count):
    tokens = q.shape[0]
    kv = pl.BlockSpec((tokens, LANES), lambda i: (0, first // 2 + i // 2))
    qs = pl.BlockSpec((tokens, LANES), lambda i: (0, first + i))
    both = pl.BlockSpec((2, tokens, LANES), lambda i: (0, 0, i // 2))
    shape = jax.ShapeDtypeStruct
    kv_shape = (2, tokens, count * HEAD)
    return pallas(
        attend_back_kernel,
        grid=(count,),
        in_specs=[SCALAR, SCALAR, qs, kv, kv, kv, kv, qs,
                  pl.BlockSpec((1, 8, tokens), lambda i: (first + i, 0, 0)),
                  whole((tokens, LANES)), whole((tokens, LANES))],
        out_specs=[pl.BlockSpec((tokens, LANES), lambda i: (0, i)), both, both],
        out_shape=[shape((tokens, count * LANES), BF16), shape(kv_shape, F32), shape(kv_shape, BF16)],
        scratch_shapes=[pltpu.VMEM((tokens, 2 * tokens), F32)],
        compiler_params=params(28),
        cost_estimate=cost(12),
        name="attend_back",
    )(g, prefix, q, k0, v0, k1, v1, do, lse, cosine, sine)


def output_kernel(where_ref, a_ref, wo0, wo1, wo2, x_ref, gain_ref, res_ref, n_ref):
    res = x_ref[...].astype(F32) + project_rows(a_ref, where_ref, (wo0, wo1, wo2))
    res_ref[...] = res
    scale = lax.rsqrt(jnp.mean(res * res, -1, keepdims=True) + EPSILON)
    n_ref[...] = (res * scale * gain_ref[...]).astype(BF16)


def halves_spec(w):
    shape = (w.shape[0] // 2, w.shape[1])
    return [pl.BlockSpec(shape, lambda *_, n=n: (n, 0), pipeline_mode=pl.Buffered(1)) for n in range(2)]


def output(where, attended, wo, x, gain):
    tokens, width = x.shape
    rows = 256
    row = pl.BlockSpec((rows, width), lambda i: (i, 0))
    return pallas(
        output_kernel,
        grid=(tokens // rows,),
        in_specs=[SCALAR, row, whole(wo[0].shape), *halves_spec(wo[1]), row, whole((1, width))],
        out_specs=[row, row],
        out_shape=[jax.ShapeDtypeStruct((tokens, width), F32), jax.ShapeDtypeStruct((tokens, width), BF16)],
        compiler_params=params(),
        cost_estimate=cost(0.1),
        name="output",
    )(where, attended, *wo, wo[1], x, gain)


def gates_of(rows, router_t, member):
    logits = jnp.where(member > 0.0, nt(rows, router_t), MASKED)
    peak = jnp.max(logits, -1, keepdims=True)
    weights = jnp.where(member > 0.0, jnp.exp(logits - peak), 0.0)
    return weights / jnp.sum(weights, -1, keepdims=True)


def experts_kernel(*refs, first, start, adding, carrying, final):
    refs = list(refs)
    take = lambda n: [refs.pop(0) for _ in range(n)]
    g_ref, x, c = take(3)
    if first:
        member, router, order_in = take(3)
    else:
        gates, xt_in, ct_in = take(3)
    win, wout = take(2)
    olds_in = [take(2) for _ in adding]
    grad_in, sum_in, gg_in = take(3) if carrying else (None, None, None)
    keep, send, grad, total = take(4)
    gg_out = None if final else take(1)[0]
    if first:
        gates, xt_out, ct_out = take(3)
    hid_scr, dgu_scr, grad_scr, sum_scr, gg_scr, xt, ct, sems = take(8)
    order = take(1)[0] if first else None
    keep_old, send_old = take(2) if adding else (None, None)
    grad_low, sum_low = take(2) if final else (grad_scr, sum_scr)
    step = pl.program_id(0)
    at_start, at_end = step == 0, step == pl.num_programs(0) - 1
    width = x.shape[1]
    column = g_ref[0] * (EXPERTS // 2) + start + step
    copy = lambda n, source, target: pltpu.make_async_copy(source, target, sems.at[n])
    loads = [copy(0, order_in, order)] if first else [copy(0, xt_in, xt), copy(1, ct_in, ct)]
    sums_in = [copy(2, grad_in, grad_scr), copy(3, sum_in, sum_scr)] if carrying else []
    olds = []
    for (keep_in, send_in), (skip, _) in zip(olds_in, adding):
        olds += [copy(4, keep_in.at[step + skip], keep_old), copy(5, send_in.at[step + skip], send_old)]
    sums_out = [copy(6, grad_low, grad), copy(7, sum_low, total)]
    turned_out = [copy(8, xt, xt_out), copy(9, ct, ct_out)] if first else []

    @pl.when(at_start)
    def _():
        for load in loads + sums_in:
            load.start()
        if first:
            gates[...] = gates_of(x[...], router[...], member[...])
        gg_scr[...] = gg_in[...] if carrying else jnp.zeros_like(gg_scr)

    for old in olds:
        old.start()
    probs = gates[...]
    mine = lax.broadcasted_iota(jnp.int32, probs.shape, 1) == column
    p = jnp.sum(jnp.where(mine, probs, 0.0), 1, keepdims=True)
    gate_up = nn(x[...], win[0])
    back = nn(c[...], wout[0])
    gate, up = gate_up[:, :FF], gate_up[:, FF:]
    sig = 1.0 / (1.0 + jnp.exp(-gate))
    act = gate * sig
    hid = act * up
    gg_scr[...] = jnp.where(mine, jnp.sum(hid * back, 1, keepdims=True), gg_scr[...])
    back = back * p
    dgate = back * up * (sig * (1.0 + gate * (1.0 - sig)))
    hid_scr[...] = (hid * p).astype(BF16)
    dgu_scr[:, :FF] = dgate.astype(BF16)
    dgu_scr[:, FF:] = (back * act).astype(BF16)

    if carrying:

        @pl.when(at_start)
        def _():
            for load in sums_in:
                load.wait()

    for scr, value in ((sum_scr, nt(hid_scr[...], wout[0])), (grad_scr, nt(dgu_scr[...], win[0]))):
        if carrying:
            scr[...] += value
        else:

            @pl.when(at_start)
            def _():
                scr[...] = value

            @pl.when(jnp.logical_not(at_start))
            def _():
                scr[...] += value

    @pl.when(at_end)
    def _():
        if final:
            sum_low[...] = sum_scr[...].astype(BF16)
            grad_low[:, :width] = grad_scr[...].astype(BF16)
            grad_low[:, width:] = gg_scr[...].astype(BF16)
        else:
            gg_out[...] = gg_scr[...]
        for store in sums_out:
            store.start()

    @pl.when(at_start)
    def _():
        for load in loads:
            load.wait()
        if first:
            xt[...] = nt(order[...], x[...]).astype(BF16)
            ct[...] = nt(order[...], c[...]).astype(BF16)
            for store in turned_out:
                store.start()

    for old in olds:
        old.wait()
    for out, old, base in ((keep, keep_old, 0), (send, send_old, width // 2)):
        rows = pl.ds(base, width // 2)
        for cols, left, right in ((slice(0, 2 * FF), xt, dgu_scr), (slice(2 * FF, 3 * FF), ct, hid_scr)):
            value = nn(left[rows], right[...])
            if adding:
                value = value + old[:, cols].astype(F32)
            out[0, :, cols] = value.astype(BF16)

    @pl.when(at_end)
    def _():
        for store in sums_out + turned_out:
            store.wait()


def experts(g, x, c, win, wout, start, count, fresh=None, known=None, adding=(), carrying=None, final=False):
    tokens, width = x.shape
    cols = 3 * FF
    shape = jax.ShapeDtypeStruct
    half = pl.BlockSpec((1, width // 2, cols), lambda i: (i, 0, 0))
    anywhere = pl.BlockSpec(memory_space=pl.ANY)
    wide, narrow, turned = (tokens, width), (tokens, LANES), (width, tokens)
    back = (tokens, width + LANES)
    args = [g, x, c, *(fresh or known), win, wout]
    specs = [SCALAR, whole(wide), whole(wide)]
    specs += [whole(narrow), whole(fresh[1].shape), anywhere] if fresh else [whole(narrow), anywhere, anywhere]
    specs += [pl.BlockSpec((1, width, 2 * FF), lambda i: (start + i, 0, 0)),
              pl.BlockSpec((1, width, FF), lambda i: (start + i, 0, 0))]
    for keep, send, _, _ in adding:
        args += [keep, send]
        specs += [anywhere, anywhere]
    if carrying:
        args += carrying
        specs += [anywhere, anywhere, whole(narrow)]
    outs = [half, half, anywhere, anywhere]
    shapes = [shape((count, width // 2, cols), BF16), shape((count, width // 2, cols), BF16)]
    if final:
        shapes += [shape(back, BF16), shape(wide, BF16)]
    else:
        outs += [whole(narrow)]
        shapes += [shape(wide, F32), shape(wide, F32), shape(narrow, F32)]
    if fresh:
        outs += [whole(narrow), anywhere, anywhere]
        shapes += [shape(narrow, F32), shape(turned, BF16), shape(turned, BF16)]
    scratch = [pltpu.VMEM((tokens, FF), BF16), pltpu.VMEM((tokens, 2 * FF), BF16),
               pltpu.VMEM(wide, F32), pltpu.VMEM(wide, F32), pltpu.VMEM(narrow, F32),
               pltpu.VMEM(turned, BF16), pltpu.VMEM(turned, BF16), pltpu.SemaphoreType.DMA((10,))]
    if fresh:
        scratch += [pltpu.VMEM((width, width), BF16)]
    if adding:
        scratch += [pltpu.VMEM((width // 2, cols), BF16)] * 2
    if final:
        scratch += [pltpu.VMEM(back, BF16), pltpu.VMEM(wide, BF16)]
    return pallas(
        functools.partial(experts_kernel, first=fresh is not None, start=start,
                          adding=tuple(entries for _, _, *entries in adding),
                          carrying=carrying is not None, final=final),
        grid=(count,),
        in_specs=specs,
        out_specs=outs,
        out_shape=shapes,
        scratch_shapes=scratch,
        compiler_params=params(62),
        cost_estimate=cost((3 if adding and carrying else 8) * count),
        name="experts",
    )(*args)


def middle_kernel(where_ref, c_ref, grad_ref, back_ref, gg_ref, p_ref, router_ref, res_ref, gain_ref,
                  wo0, wo1, wo2, dres_ref, low_ref, da_ref, dl_ref, dgain_ref):
    width = c_ref.shape[1]
    p = p_ref[...]
    gg = gg_ref[...] + back_ref[:, width:].astype(F32)
    dlogits = p * (gg - jnp.sum(p * gg, 1, keepdims=True))
    dl_ref[...] = dlogits.astype(BF16)
    high = dlogits.astype(BF16)
    rest = (dlogits - high.astype(F32)).astype(BF16)
    router = router_ref[...]
    grad = grad_ref[...] + back_ref[:, :width].astype(F32) + (nn(high, router) + nn(rest, router))
    res = res_ref[...]
    scale = lax.rsqrt(jnp.mean(res * res, -1, keepdims=True) + EPSILON)
    part = jnp.broadcast_to(jnp.sum(grad * (res * scale), 0, keepdims=True), dgain_ref.shape)

    @pl.when(pl.program_id(0) == 0)
    def _():
        dgain_ref[...] = part

    @pl.when(pl.program_id(0) != 0)
    def _():
        dgain_ref[...] += part

    w = grad * gain_ref[...]
    dres = c_ref[...].astype(F32) + (scale * w - res * (scale * scale * scale)
                                     * jnp.mean(w * res, -1, keepdims=True))
    dres_ref[...] = dres
    low = dres.astype(BF16)
    low_ref[...] = low
    for at, wo in zip(pieces(where_ref, width), (wo0, wo1, wo2)):
        da_ref[:, at] = nt(low, wo[...]).astype(BF16)


def middle(where, c, grad, back, gg, p, router_t, res, gain, wo):
    tokens, width = c.shape
    rows = 256
    row = lambda n: pl.BlockSpec((rows, n), lambda i: (i, 0))
    shape = jax.ShapeDtypeStruct
    return pallas(
        middle_kernel,
        grid=(tokens // rows,),
        in_specs=[SCALAR, row(width), row(width), row(width + LANES), row(LANES), row(LANES),
                  whole((LANES, width)), row(width), whole((1, width)), whole(wo[0].shape), *halves_spec(wo[1])],
        out_specs=[row(width), row(width), row(width), row(LANES), pl.BlockSpec((8, width), lambda i: (0, 0))],
        out_shape=[shape((tokens, width), F32), shape((tokens, width), BF16), shape((tokens, width), BF16),
                   shape((tokens, LANES), BF16), shape((8, width), F32)],
        compiler_params=params(),
        cost_estimate=cost(100),
        name="middle",
    )(where, c, grad, back, gg, p, router_t, res, gain, *wo, wo[1])


def weight_kernel(*refs, joined):
    refs = list(refs)
    take = lambda n: [refs.pop(0) for _ in range(n)]
    xt, dq, own, early, cos, sin = take(6)
    order, low, att, xt_ffn, dlogits, dgain = take(6) if joined else [None] * 6
    keep, dkv, send = take(3)
    half = keep.shape[0]
    dk = rotated(own[0] + early[0].astype(F32), cos[...], sin[...], -1.0).astype(BF16)
    dv = (own[1] + early[1].astype(F32)).astype(BF16)
    nq, nk = dq.shape[1], dk.shape[1]
    dkv[:, :nk] = dk
    dkv[:, nk:] = dv
    if joined:
        low_t, gain_rows = take(2)
        low_t[...] = nt(order[...], low[...]).astype(BF16)
        row = lax.broadcasted_iota(jnp.int32, gain_rows.shape, 0)
        gain_rows[...] = jnp.where(row == EXPERTS, dgain[0:1, :], 0.0).astype(BF16)
    def put(cols, rows, value):
        (keep if rows.start == 0 else send)[:, cols] = value.astype(BF16)

    for base in (0, half):
        rows = pl.ds(base, half)
        put(slice(0, nq), rows, nn(xt[rows], dq[...]))
        first = nq + 2 * nk
        put(slice(nq, first), rows, nn(xt[rows], dkv[...]))
        if joined:
            wide = att.shape[1]
            put(slice(first, first + wide), rows, nn(low_t[rows], att[...]))
            put(slice(first + wide, first + wide + LANES), rows,
                nn(xt_ffn[rows], dlogits[...]) + nt(order[rows], gain_rows[...]))


def weight_grads(xt, dq, own, early, cosine, sine, joined=None):
    width, tokens = xt.shape
    nq, nk = dq.shape[1], own.shape[2]
    shape = jax.ShapeDtypeStruct
    cols = nq + 2 * nk + (joined[2].shape[1] + LANES if joined else 0)
    out = shape((width // 2, cols), BF16)
    vmem = pl.BlockSpec(memory_space=pltpu.VMEM)
    args = (xt, dq, own, early, cosine, sine, *(joined or ()))
    return pallas(
        functools.partial(weight_kernel, joined=bool(joined)),
        in_specs=[vmem] * len(args),
        out_specs=[vmem] * 3,
        out_shape=[out, shape((tokens, 2 * nk), BF16), out],
        scratch_shapes=[pltpu.VMEM((width, tokens), BF16), pltpu.VMEM((LANES, width), BF16)] if joined else [],
        compiler_params=params(),
        cost_estimate=cost(0.1 if joined else 60),
        name="weight_grads",
    )(*args)


def input_kernel(where_ref, *refs, parts):
    refs = list(refs)
    take = lambda n: [refs.pop(0) for _ in range(n)]
    dqs, dkvs, wq, wk, wv = take(parts), take(parts), take(1), take(1), take(1)
    packs = take(4)
    x_ref, gain_ref, dres_ref, out_ref, grad = refs
    nq, nk = wq[0].shape[1], wk[0].shape[1]
    columns = []
    for n in range(parts):
        q0, k0 = n * nq // parts, n * nk // parts
        q1, k1 = q0 + nq // parts, k0 + nk // parts
        dkv = dkvs[n][...]
        half = dkv.shape[1] // 2
        for left, own, first, (lo, hi) in (
                (dqs[n][...], wq[0], None, (q0, q1)),
                (dkv[:, :half], wk[0], 0, (k0, k1)),
                (dkv[:, half:], wv[0], nk, (k0, k1))):
            packed = slice(lo, hi) if first is None else slice(first + lo, first + hi)
            columns.append((left, own, slice(lo, hi), (first is not None, packed)))
    at = pieces(where_ref, x_ref.shape[1])
    grad[:, at[0]] = sum(nt(left, own[:, mine]) for left, own, mine, _ in columns)
    for place, pack in zip(at[1:], (packs[0::2], packs[1::2])):
        grad[:, place] = sum(nt(left, pack[which][:, packed]) for left, _, _, (which, packed) in columns)
    x = x_ref[...].astype(F32)
    scale = lax.rsqrt(jnp.mean(x * x, -1, keepdims=True) + EPSILON)
    w = grad[...] * gain_ref[...]
    out_ref[...] = dres_ref[...] + (scale * w - x * (scale * scale * scale) * jnp.mean(w * x, -1, keepdims=True))


def input_grads(where, dqs, dkvs, wq, wk, wv, pack, x, gain, dres):
    tokens, width = x.shape
    rows = 256
    row = lambda a: pl.BlockSpec((rows, a.shape[1]), lambda i: (i, 0))
    weights = (wq, wk, wv, *pack[0], *pack[1])
    return pallas(
        functools.partial(input_kernel, parts=len(dqs)),
        grid=(tokens // rows,),
        in_specs=[SCALAR, *map(row, dqs), *map(row, dkvs), *(whole(w.shape) for w in weights), row(x),
                  whole((1, width)), row(dres)],
        out_specs=row(dres),
        out_shape=jax.ShapeDtypeStruct((tokens, width), F32),
        scratch_shapes=[pltpu.VMEM((rows, width), F32)],
        compiler_params=params(),
        cost_estimate=cost(5),
        name="input_grads",
    )(where, *dqs, *dkvs, *weights, x, gain, dres)


def exchange(value, *bits):
    count = lax.axis_size("replica")
    flip = sum(count if b == "group" else 1 << b for b in bits)
    return lax.ppermute(value, ("group", "replica"), [(i, i ^ flip) for i in range(2 * count)])


def after(value, *others):
    out = lax.optimization_barrier((value, *others))
    return out[0], list(out[1:])


def deal(out, to, entries, rows):
    def some(source, target, size):
        value = sum(p[e, pl.ds(source, size), :].astype(F32) for p, e in entries)
        out[to, pl.ds(target, size), :] = value.astype(BF16)

    at = 0
    for start, total in rows:
        step = 32
        if total % step == 0 and total > step and start % step == 0 and at % step == 0:

            @pl.loop(0, total // step)
            def _(i, start=start, at=at):
                some(pl.multiple_of(start + i * step, step), pl.multiple_of(at + i * step, step), step)

        else:
            some(start, at, total)
        at += total


def deal_entries(out, to, parts, firsts, count, rows):
    @pl.loop(0, count)
    def _(n):
        deal(out, to + n, [(p, first + n) for p, first in zip(parts, firsts)], rows)


def split_kernel(*refs, groups):
    refs = list(refs)
    parts = [[refs.pop(0) for _ in firsts] for firsts, _, _, _, _ in groups]
    for part, (firsts, count, outs, to, ranges) in zip(parts, groups):
        for out, rows in zip(outs, ranges):
            deal_entries(refs[out], to, part, firsts, count, rows)


def stream_kernel(*refs, count, pieces):
    parts, outs = refs[:count], list(refs[count:])
    for first, size, ranges in pieces:
        mine = [outs.pop(0) for _ in ranges]

        @pl.when((pl.program_id(0) >= first) & (pl.program_id(0) < first + size))
        def _():
            for out, rows in zip(mine, ranges):
                deal(out, 0, [(p, 0) for p in parts], rows)


def ranges_of(axes, chunk, bits):
    spots = np.stack(np.unravel_index(np.arange(2 ** len(axes)), (2,) * len(axes)), 1)
    at = [axes.index(b) for b in bits]
    ranges = []
    for combo in np.ndindex(*(2,) * len(bits)):
        rows = []
        for n in np.nonzero((spots[:, at] == combo).all(1))[0]:
            if rows and rows[-1][0] + rows[-1][1] == n * chunk:
                rows[-1] = (rows[-1][0], rows[-1][1] + chunk)
            else:
                rows.append((int(n) * chunk, chunk))
        ranges.append(tuple(rows))
    return tuple(ranges)


def flips_of(bits):
    return [[b for b, on in zip(bits, combo) if on] for combo in list(np.ndindex(*(2,) * len(bits)))[1:]]


class Run:
    def __init__(self, parts, axes, chunk, first=0, count=1):
        self.parts, self.axes, self.chunk, self.first, self.count = list(parts), list(axes), chunk, first, count


def firsts_of(run):
    return tuple(run.first if p.shape[0] > run.count else 0 for p in run.parts)


def split_call(groups, args, shapes):
    vmem = pl.BlockSpec(memory_space=pltpu.VMEM)
    return pallas(
        functools.partial(split_kernel, groups=tuple(groups)),
        in_specs=[vmem] * len(args),
        out_specs=[vmem] * len(shapes),
        out_shape=[jax.ShapeDtypeStruct(shape, BF16) for shape in shapes],
        compiler_params=params(),
        cost_estimate=cost(0.1),
        name="split",
    )(*args)


def split(runs, bit):
    axes, chunk = runs[0].axes, runs[0].chunk
    ranges = ranges_of(axes, chunk, (bit,))
    total, groups = 0, []
    for run in runs:
        groups.append((firsts_of(run), run.count, (0, 1), total, ranges))
        total += run.count
    shapes = [(total, sum(n for _, n in rows), runs[0].parts[0].shape[2]) for rows in ranges]
    kept, send = split_call(groups, [p for run in runs for p in run.parts], shapes)
    return Run([kept, exchange(send, bit)], [b for b in axes if b != bit], chunk, 0, total)


def split_each(*pieces):
    groups, shapes = [], []
    for run, bit in pieces:
        ranges = ranges_of(run.axes, run.chunk, (bit,))
        groups.append((firsts_of(run), run.count, (len(shapes), len(shapes) + 1), 0, ranges))
        shapes += [(run.count, sum(n for _, n in rows), run.parts[0].shape[2]) for rows in ranges]
    outs = list(split_call(groups, [p for run, _ in pieces for p in run.parts], shapes))
    made = []
    for run, bit in pieces:
        kept, send = outs.pop(0), outs.pop(0)
        made.append(Run([kept, exchange(send, bit)], [b for b in run.axes if b != bit], run.chunk, 0, run.count))
    return made


def split_apart(run, *pieces):
    rows, cols = run.parts[0].shape[1:]
    shapes, specs, plan, first = [], [], [], 0
    for bits, count in pieces:
        ranges = ranges_of(run.axes, run.chunk, bits)
        plan.append((first, count, ranges))
        for chosen in ranges:
            size = sum(n for _, n in chosen)
            shapes.append(jax.ShapeDtypeStruct((count, size, cols), BF16))
            specs.append(pl.BlockSpec(
                (1, size, cols), lambda i, first=first, count=count: (jnp.clip(i - first, 0, count - 1), 0, 0)))
        first += count
    outs = list(pallas(
        functools.partial(stream_kernel, count=len(run.parts), pieces=tuple(plan)),
        grid=(first,),
        in_specs=[pl.BlockSpec((1, rows, cols), lambda i: (i, 0, 0))] * len(run.parts),
        out_specs=specs,
        out_shape=shapes,
        compiler_params=params(62 if first > 2 else 24),
        cost_estimate=cost(0.1),
        name="split_apart",
    )(*run.parts))
    runs = []
    for bits, count in pieces:
        kept = outs.pop(0)
        received = [exchange(outs.pop(0), *flip) for flip in flips_of(bits)]
        runs.append(Run([kept, *received], [b for b in run.axes if b not in bits], run.chunk, 0, count))
    return runs


def block_sum(residual, own, other):
    def kernel(a, b, c, out):
        out[...] = (a[...] + b[...] + c[...].astype(F32)).astype(BF16)

    tokens, width = residual.shape
    row = pl.BlockSpec((tokens // 4, width), lambda i: (i, 0))
    return pallas(
        kernel,
        grid=(4,),
        in_specs=[row] * 3,
        out_specs=row,
        out_shape=jax.ShapeDtypeStruct(residual.shape, BF16),
        compiler_params=params(),
        cost_estimate=cost(0.1),
        name="block_sum",
    )(residual, own, other)


def finish_attention_kernel(*refs, counts):
    refs = list(refs)
    take = lambda n: [refs.pop(0) for _ in range(n)]
    joined, alone = take(counts[0]), take(counts[1])
    wq, wk, wv, gain = take(4)
    dq, dk, dv, do, drouter, dgain_attn, dgain_ffn = refs
    a = sum(p[0].astype(F32) for p in joined)
    b = sum(p[0].astype(F32) for p in alone)
    nq, nk = wq.shape[1] // 2, wk.shape[1] // 2
    dgain = 0.0
    for n, part in enumerate((a, b)):
        for ref, w, size, first in ((dq, wq, nq, 0), (dk, wk, nk, nq), (dv, wv, nk, nq + nk)):
            grad = part[:, first : first + size]
            ref[:, n * size : (n + 1) * size] = grad
            dgain = dgain + jnp.sum(grad * w[:, n * size : (n + 1) * size].astype(F32), 1, keepdims=True)
    dgain_attn[...] = dgain / gain[...]
    first = nq + 2 * nk
    width = do.shape[0]
    do[...] = a[:, first : first + width].T
    last = a[:, first + width :]
    drouter[...] = last[:, :EXPERTS]
    lane = lax.broadcasted_iota(jnp.int32, last.shape, 1)
    dgain_ffn[...] = jnp.sum(jnp.where(lane == EXPERTS, last, 0.0), 1, keepdims=True)


def finish_attention(joined, alone, wq, wk, wv, gain, width):
    chunk = wq.shape[0]
    shape = lambda *s: jax.ShapeDtypeStruct(s, F32)
    args = (*joined, *alone, wq, wk, wv, gain)
    vmem = pl.BlockSpec(memory_space=pltpu.VMEM)
    return pallas(
        functools.partial(finish_attention_kernel, counts=(len(joined), len(alone))),
        in_specs=[vmem] * len(args),
        out_specs=[vmem] * 7,
        out_shape=[shape(chunk, wq.shape[1]), shape(chunk, wk.shape[1]), shape(chunk, wv.shape[1]),
                   shape(width, chunk), shape(chunk, EXPERTS), shape(chunk, 1), shape(chunk, 1)],
        compiler_params=params(),
        cost_estimate=cost(0.1),
        name="finish_attention",
    )(*args)


def finish_experts_kernel(g_ref, *refs):
    own, other, (win, wout) = refs[: len(refs) // 2 - 1], refs[len(refs) // 2 - 1 : -2], refs[-2:]
    count = win.shape[0] // 2
    g = g_ref[0]
    for parts, side in ((own, g), (other, 1 - g)):
        e = 0
        for p in parts:
            for n in range(p.shape[0]):
                win[side * count + e] = p[n, :, : 2 * FF].astype(F32)
                wout[side * count + e] = p[n, :, 2 * FF :].astype(F32)
                e += 1


def finish_experts(g, own, other):
    chunk = own[0].shape[1]
    shape = lambda *s: jax.ShapeDtypeStruct(s, F32)
    vmem = pl.BlockSpec(memory_space=pltpu.VMEM)
    return pallas(
        finish_experts_kernel,
        in_specs=[SCALAR] + [vmem] * (2 * len(own)),
        out_specs=[vmem] * 2,
        out_shape=[shape(EXPERTS, chunk, 2 * FF), shape(EXPERTS, chunk, FF)],
        compiler_params=params(),
        cost_estimate=cost(0.1),
        name="finish_experts",
    )(g, *own, *other)


def on_device(
    block_in, attn_gain, query_weight, key_weight, value_weight, out_weight, ffn_gain, router_weight,
    expert_in, expert_out, routes, prefix, cotangent,
):
    FOLLOWED.clear()
    replicas = lax.axis_size("replica")
    bits = replicas.bit_length() - 1
    tokens, width = block_in.shape[1:]
    half = width // 2
    chunk = half // replicas
    group, replica = lax.axis_index("group"), lax.axis_index("replica")
    core = replica % 2
    g = group.astype(jnp.int32).reshape(1)
    where = jnp.stack([group, core]).astype(jnp.int32)
    x, cot = block_in[0], cotangent[0]
    swap = lambda v: exchange(v, "group")

    def ordered(own, other, axis):
        return jnp.where(group == 0, jnp.concatenate([own, other], axis), jnp.concatenate([other, own], axis))

    quarter = lambda w: lax.dynamic_slice_in_dim(w, core * (w.shape[0] // 2), w.shape[0] // 2, 0)
    pack_q, pack_kv = quarter(query_weight), jnp.concatenate([quarter(key_weight), quarter(value_weight)], 1)
    pack_q, (pack_kv, x_send, wo_send, cot_send) = after(pack_q, pack_kv, x, out_weight, cot)
    pack_q, pack_kv = swap(pack_q), swap(pack_kv)
    x_early = lax.ppermute(x_send, "group", [(0, 1)])
    wo = (out_weight, swap(wo_send))
    cot_other = swap(cot_send)
    lanes = jnp.arange(LANES, dtype=jnp.int32)
    member = (routes[0][:, :, None] == lanes[None, None, :]).any(1).astype(F32)
    member_t = (routes[0].T[:, None, :] == lanes[None, :EXPERTS, None]).any(0).astype(BF16)
    small = jnp.concatenate([attn_gain[None], ffn_gain[None], router_weight.T, member_t], 0)
    small_other = swap(small)
    vectors = ordered(small[: 2 + EXPERTS], small_other[: 2 + EXPERTS], 1)
    member_other = jnp.pad(small_other[2 + EXPERTS :].T.astype(F32), ((0, 0), (0, LANES - EXPERTS)))
    gain_attn, gain_ffn = vectors[0:1].astype(F32), vectors[1:2].astype(F32)
    router_t = jnp.concatenate([vectors[2:], jnp.zeros((LANES - EXPERTS, width), BF16)], 0)

    cosine, sine, *early_tables = tables(g, tokens)
    place = np.arange(width)
    blocks, inner = place // chunk, place % chunk
    reverse = np.zeros_like(blocks)
    for b in range(bits):
        reverse |= ((blocks >> 1 >> (bits - 1 - b)) & 1) << b
    feature = ((jnp.asarray(blocks & 1, jnp.int32) ^ group) * half
               + (jnp.asarray(reverse, jnp.int32) ^ replica) * chunk + jnp.asarray(inner, jnp.int32))
    order = (feature[:, None] == jnp.arange(width, dtype=jnp.int32)[None, :]).astype(BF16)

    mine = lambda a: lax.dynamic_slice_in_dim(a, replica * chunk, chunk, 0)
    rows = (mine(query_weight), mine(key_weight), mine(value_weight), mine(attn_gain).astype(F32)[:, None])
    pack_q, (pack_kv, cosine, sine, member, order, gain_attn, member_other, *more) = after(
        pack_q, pack_kv, cosine, sine, member, order, gain_attn, member_other, *early_tables, *rows)
    early_tables, rows = more[:2], more[2:]
    pack = (pack_q, exchange(pack_q, 0)), (pack_kv, exchange(pack_kv, 0))

    _, q, k, v, normed_t = project(
        where, x, gain_attn, query_weight, key_weight, value_weight, pack, cosine, sine, order)
    k1, v1 = project_earlier(where, x_early, gain_attn, key_weight, value_weight, pack, *early_tables)
    attended, lse = attend(g, prefix, q, k, v, k1, v1)
    whole_where = jnp.stack([group, 0 * core]).astype(jnp.int32)
    residual, normed = output(whole_where, attended, wo, x, gain_ffn)
    normed_other = swap(normed)
    count = expert_in.shape[0] // 2
    near = lambda *a, **k: experts(g, normed, cot, expert_in, expert_out, *a, **k)
    far = lambda *a, **k: experts(g, *a[0], expert_in, expert_out, *a[1:], **k)
    keep, send, grad_own, sum_own, gg_own, *known = near(0, count, fresh=(member, router_t, order))
    gates, xt_own, _ = known
    normed_other, (cot_other, keep) = after(normed_other, cot_other, keep)
    keep_a, send_a, *sums, gates_o, xt_o, ct_o = far(
        (normed_other, cot_other), 0, count, fresh=(member_other, router_t, order), adding=[(keep, send, 0, count)])
    received_a = exchange(send_a, 0)
    keep, send, back, sum_other = far(
        (normed_other, cot_other), count, count, known=(gates_o, xt_o, ct_o), carrying=sums, final=True)
    back = swap(back)
    two = count // 2
    dims = [*range(1, bits), "group"]
    first, second, *rest = [*range(1, bits)]
    run_a = Run((keep_a, received_a), dims, chunk, 0, count)
    run0, run1 = split_apart(run_a, ((first,), two), ((second,), two))
    sums, run_b = (grad_own, sum_own, gg_own), []
    for part in (0, two):
        keep_b, send_b, *sums = near(
            count + part, two, known=known, adding=[(keep, send, part, two)], carrying=sums)
        run_b.append(Run((keep_b, exchange(send_b, 0)), dims, chunk, 0, two))
    grad_own, sum_own, gg_own = sums
    back, (keep_b,) = after(back, keep_b)
    run0, run1 = split_each((run0, second), (run1, first))

    grad_res, grad_low, grad_att, grad_logits, grad_gain = middle(
        whole_where, cot, grad_own, back, gg_own, gates, router_t, residual, gain_ffn, wo)
    grad_low, (sum_send,) = after(grad_low, sum_other)
    sum_other = swap(sum_send)
    (run2,), (run3,) = (split_apart(run, ((first,), two)) for run in run_b)
    heads = KV_HEADS // 2
    attn = lambda first: attend_back(g, prefix, q, k, v, k1, v1, grad_att, lse, cosine, sine, first, heads)
    to_earlier = lambda a: lax.ppermute(a, "group", [(1, 0)])
    dq0, own0, early0 = attn(0)
    early0 = to_earlier(early0)
    run_a = run0, run1
    for bit in rest:
        run_a = [split(run_a, bit)]
    dq1, own1, early1 = attn(heads)
    early1 = to_earlier(early1)
    one = lambda keep, send: Run((keep[None], exchange(send, 0)[None]), dims, chunk)
    keep0, dkv0, send0 = weight_grads(
        normed_t, dq0, own0, early0, cosine, sine,
        joined=(order, grad_low, attended, xt_own, grad_logits, grad_gain))
    attn0 = one(keep0, send0)
    run2 = split([run2], second)
    block_out = block_sum(residual, sum_own, sum_other)
    swap_a = split(run_a, "group")
    keep1, dkv1, send1 = weight_grads(normed_t, dq1, own1, early1, cosine, sine)
    attn1 = one(keep1, send1)
    order0, order1 = ["group", first, second, *rest], [first, "group", second, *rest]
    attn0 = split([attn0], order0.pop(0))
    input_grad = input_grads(where, (dq0, dq1), (dkv0, dkv1), query_weight, key_weight, value_weight, pack,
                             x, gain_attn, grad_res)
    attn1 = split([attn1], order1.pop(0))
    run3 = split([run3], second)
    for bit in rest:
        run2 = split([run2], bit)
    for _ in range(2):
        attn0 = split([attn0], order0.pop(0))
        attn1 = split([attn1], order1.pop(0))
    for bit in rest:
        run3 = split([run3], bit)
    while order0:
        attn0 = split([attn0], order0.pop(0))
        attn1 = split([attn1], order1.pop(0))
    swap_b = split([run2, run3], "group")

    query_grad, key_grad, value_grad, out_grad, router_grad, attn_gain_grad, ffn_gain_grad = finish_attention(
        attn0.parts, attn1.parts, *rows, width)
    expert_in_grad, expert_out_grad = finish_experts(
        g, (swap_a.parts[0], swap_b.parts[0]), (swap_a.parts[1], swap_b.parts[1]))
    return (
        block_out[None], input_grad[None], attn_gain_grad[:, 0], query_grad, key_grad, value_grad, out_grad,
        ffn_gain_grad[:, 0], router_grad, expert_in_grad, expert_out_grad,
    )


def solution(mesh):
    placed = (
        P("replica", "group", None),
        P("group"),
        P("group", None),
        P("group", None),
        P("group", None),
        P("group", None),
        P("group"),
        P("group", None),
        P("group", None, None),
        P("group", None, None),
        P("replica", "group", None),
        P("replica"),
        P("replica", "group", None),
    )
    both = ("group", "replica")
    return jax.shard_map(
        on_device,
        mesh=mesh,
        in_specs=placed,
        out_specs=(
            P("replica", "group", None),
            P("replica", "group", None),
            P(both),
            P(both, None),
            P(both, None),
            P(both, None),
            P(None, both),
            P(both),
            P(both, None),
            P(None, both, None),
            P(None, both, None),
        ),
        check_vma=False,
    )
```

```python
import functools
import math

import jax
import jax.numpy as jnp
import numpy as np
from jax import lax
from jax.experimental import pallas as pl
from jax.experimental.pallas import tpu as pltpu
from jax.sharding import PartitionSpec as P

HEADS = 16
KV_HEADS = 8
HEAD = 64
FF = 512
TOP = 8
EXPERTS = 16

EPSILON = 1e-06
THETA_BASE = 10000.0
MASKED = -1e30
HIGHEST = lax.Precision.HIGHEST
F32 = jnp.float32
BF16 = jnp.bfloat16
MIB = 1 << 20


def nn(left, right):
    return lax.dot_general(left, right, (((1,), (0,)), ((), ())), preferred_element_type=F32)


def nt(left, right):
    return lax.dot_general(left, right, (((1,), (1,)), ((), ())), preferred_element_type=F32)


def params(limit=24):
    return pltpu.CompilerParams(vmem_limit_bytes=limit * MIB)


def cost(microseconds):
    return pl.CostEstimate(flops=int(microseconds * 0.9e9), bytes_accessed=int(microseconds * 1e5), transcendentals=0)


def whole(shape):
    return pl.BlockSpec(shape, lambda *_: (0,) * len(shape), pipeline_mode=pl.Buffered(1))


SCALAR = pl.BlockSpec(memory_space=pltpu.SMEM)

FOLLOWED = []


def pallas(kernel, *, in_specs, out_shape, **more):
    def call(*args):
        tokens, count = list(FOLLOWED), len(in_specs)

        def body(*refs):
            kernel(*refs[:count], *refs[count + len(tokens) :])

        out = pl.pallas_call(
            body,
            in_specs=[*in_specs, *[pl.BlockSpec(memory_space=pl.ANY)] * len(tokens)],
            out_shape=out_shape,
            **more,
        )(*args, *tokens)
        FOLLOWED[:] = [min(jax.tree.leaves(out), key=lambda a: a.size)]
        return out

    return call
LANES = 128


def pieces(where_ref, width):
    g, core = where_ref[0], where_ref[1]
    half, quarter = width // 2, width // 4
    other = (1 - g) * half
    at = lambda start, size: pl.ds(pl.multiple_of(start, size), size)
    return (at(g * half, half), at(other + core * quarter, quarter), at(other + (1 - core) * quarter, quarter))


def project_rows(ref, where_ref, weights):
    cols = pieces(where_ref, ref.shape[1])
    return sum(nn(ref[:, c], w[...]) for c, w in zip(cols, weights))


def swap_halves(tile):
    lane = lax.broadcasted_iota(jnp.int32, tile.shape, 1) % HEAD
    return jnp.where(
        lane < HEAD // 2, pltpu.roll(tile, 128 - HEAD // 2, 1), pltpu.roll(tile, HEAD // 2, 1)
    )


def rotated(values, cosine, sine, sign):
    tiles = []
    for start in range(0, values.shape[1], 128):
        tile = values[:, start : start + 128]
        tiles.append(tile * cosine + swap_halves(tile) * (sine * sign))
    return tiles[0] if len(tiles) == 1 else jnp.concatenate(tiles, 1)


def tables_kernel(g_ref, rate_ref, cos_ref, sin_ref, early_cos_ref, early_sin_ref):
    shape = cos_ref.shape
    lane = lax.broadcasted_iota(jnp.int32, shape, 1)
    row = lax.broadcasted_iota(jnp.int32, shape, 0)
    sign = jnp.where(lane % HEAD < HEAD // 2, -1.0, 1.0)
    for first, cos, sin in ((g_ref[0] * shape[0], cos_ref, sin_ref), (0, early_cos_ref, early_sin_ref)):
        angle = (row + first).astype(F32) * rate_ref[...]
        cos[...] = jnp.cos(angle)
        sin[...] = jnp.sin(angle) * sign


def tables(g, tokens):
    rate = THETA_BASE ** (-jnp.arange(HEAD // 2, dtype=F32) * 2.0 / HEAD)
    shape = jax.ShapeDtypeStruct((tokens, LANES), F32)
    vmem = pl.BlockSpec(memory_space=pltpu.VMEM)
    return pallas(
        tables_kernel,
        in_specs=[SCALAR, vmem],
        out_specs=[vmem] * 4,
        out_shape=[shape] * 4,
        compiler_params=params(),
        cost_estimate=cost(0.1),
        name="tables",
    )(g, jnp.tile(rate, LANES * 2 // HEAD)[None])


def project_kernel(where_ref, x_ref, gain_ref, wq0, wq1, wq2, wk0, wk1, wk2, wv0, wv1, wv2, cos_ref, sin_ref,
                   order_ref, n_ref, q_ref, k_ref, v_ref, nt_ref):
    @pl.when(pl.program_id(0) == 0)
    def _():
        x = x_ref[...].astype(F32)
        scale = lax.rsqrt(jnp.mean(x * x, -1, keepdims=True) + EPSILON)
        n_ref[...] = (x * scale * gain_ref[...]).astype(BF16)

    cosine, sine = cos_ref[...], sin_ref[...]
    q = rotated(project_rows(n_ref, where_ref, (wq0, wq1, wq2)), cosine, sine, 1.0)
    q_ref[...] = q.astype(BF16) * jnp.asarray(1.0 / math.sqrt(HEAD), BF16)
    k = rotated(project_rows(n_ref, where_ref, (wk0, wk1, wk2)), cosine, sine, 1.0)
    k_ref[...] = k.astype(BF16)
    v_ref[...] = project_rows(n_ref, where_ref, (wv0, wv1, wv2)).astype(BF16)
    nt_ref[...] = nt(order_ref[...], n_ref[...]).astype(BF16)


def project_earlier_kernel(where_ref, x_ref, gain_ref, wk0, wk1, wk2, wv0, wv1, wv2, cos_ref, sin_ref,
                           k_ref, v_ref, n_ref):
    @pl.when(where_ref[0] != 0)
    def _():
        @pl.when(pl.program_id(0) == 0)
        def _():
            x = x_ref[...].astype(F32)
            scale = lax.rsqrt(jnp.mean(x * x, -1, keepdims=True) + EPSILON)
            n_ref[...] = (x * scale * gain_ref[...]).astype(BF16)

        k = rotated(project_rows(n_ref, where_ref, (wk0, wk1, wk2)), cos_ref[...], sin_ref[...], 1.0)
        k_ref[...] = k.astype(BF16)
        v_ref[...] = project_rows(n_ref, where_ref, (wv0, wv1, wv2)).astype(BF16)

    @pl.when(where_ref[0] == 0)
    def _():
        k_ref[...] = jnp.zeros_like(k_ref)
        v_ref[...] = jnp.zeros_like(v_ref)


def weight_specs(rows, n, first):
    packed = pl.BlockSpec((rows // 2, n), lambda i: (0, first // n + i))
    return [pl.BlockSpec((rows, n), lambda i: (0, i)), packed, packed]


def project(where, x, gain, wq, wk, wv, pack, cosine, sine, order):
    tokens, width = x.shape
    steps = 4
    half = width // 2
    nq, nk = wq.shape[1], wk.shape[1]
    qb, kb = nq // steps, nk // steps
    o_spec = lambda n: pl.BlockSpec((tokens, n), lambda i: (0, i))
    shape = jax.ShapeDtypeStruct
    return pallas(
        project_kernel,
        grid=(steps,),
        in_specs=[SCALAR, whole((tokens, width)), whole((1, width)),
                  *weight_specs(half, qb, 0), *weight_specs(half, kb, 0), *weight_specs(half, kb, nk),
                  whole((tokens, LANES)), whole((tokens, LANES)),
                  pl.BlockSpec((width // steps, width), lambda i: (i, 0))],
        out_specs=[pl.BlockSpec((tokens, width), lambda i: (0, 0)), o_spec(qb), o_spec(kb), o_spec(kb),
                   pl.BlockSpec((width // steps, tokens), lambda i: (i, 0))],
        out_shape=[shape((tokens, width), BF16), shape((tokens, nq), BF16), shape((tokens, nk), BF16),
                   shape((tokens, nk), BF16), shape((width, tokens), BF16)],
        compiler_params=params(62),
        cost_estimate=cost(3),
        name="project",
    )(where, x, gain, wq, *pack[0], wk, *pack[1], wv, *pack[1], cosine, sine, order)


def project_earlier(where, x, gain, wk, wv, pack, cosine, sine):
    tokens, width = x.shape
    steps = 2
    half = width // 2
    nk = wk.shape[1]
    kb = nk // steps
    o_spec = pl.BlockSpec((tokens, kb), lambda i: (0, i))
    shape = jax.ShapeDtypeStruct
    return pallas(
        project_earlier_kernel,
        grid=(steps,),
        in_specs=[SCALAR, whole((tokens, width)), whole((1, width)),
                  *weight_specs(half, kb, 0), *weight_specs(half, kb, nk),
                  whole((tokens, LANES)), whole((tokens, LANES))],
        out_specs=[o_spec, o_spec],
        out_shape=[shape((tokens, nk), BF16), shape((tokens, nk), BF16)],
        scratch_shapes=[pltpu.VMEM((tokens, width), BF16)],
        compiler_params=params(62),
        cost_estimate=cost(0.1),
        name="project_earlier",
    )(where, x, gain, wk, *pack[1], wv, *pack[1], cosine, sine)


def lane_half(shape, which):
    lane = lax.broadcasted_iota(jnp.int32, shape, 1)
    return ((lane // HEAD) % 2 == which).astype(F32)


def doubled(tile, which):
    kept = tile.astype(F32) * lane_half(tile.shape, which)
    return kept + pltpu.roll(kept, HEAD, 1)


def fill_bias(bias, prefix_ref, g):
    shape = bias.shape
    key = lax.broadcasted_iota(jnp.int32, shape, 0)
    query = lax.broadcasted_iota(jnp.int32, shape, 1) % shape[0]
    seen = (key <= query) | (key + g * shape[0] < prefix_ref[0])
    bias[...] = jnp.where(seen, 0.0, MASKED)


def stacked_heads(tile):
    tile = tile.astype(F32)
    return jnp.concatenate([(tile * lane_half(tile.shape, a)).astype(BF16) for a in range(2)], 0)


def attend_kernel(g_ref, prefix_ref, q_ref, k0_ref, v0_ref, k1_ref, v1_ref, o_ref, lse_ref, bias):
    g = g_ref[0]
    which = pl.program_id(0) % 2

    @pl.when(pl.program_id(0) == 0)
    def _():
        fill_bias(bias, prefix_ref, g)

    away = jnp.where(g == 0, -MASKED, 0.0)
    tokens = q_ref.shape[0]
    q = stacked_heads(q_ref[...])
    keys = jnp.concatenate([doubled(k[...], which).astype(BF16) for k in (k0_ref, k1_ref)], 0)
    values = jnp.concatenate([doubled(v[...], which).T[:HEAD].astype(BF16) for v in (v0_ref, v1_ref)], 1)
    scores = nt(keys, q)
    own, early = scores[:tokens] + bias[...], scores[tokens:]
    peak = jnp.maximum(jnp.max(own, 0, keepdims=True), jnp.max(early, 0, keepdims=True) - away)
    own, early = jnp.exp(own - peak), jnp.exp(early - (peak + away))
    total = jnp.sum(own, 0, keepdims=True) + jnp.sum(early, 0, keepdims=True)
    out = nn(values, jnp.concatenate([own.astype(BF16), early.astype(BF16)], 0)) * (1.0 / total)
    lse = peak + jnp.log(total)
    lse_ref[0, 0:1, :] = lse[:, :tokens]
    lse_ref[0, 1:2, :] = lse[:, tokens:]
    o_ref[...] = jnp.concatenate([out[:, :tokens], out[:, tokens:]], 0).T.astype(BF16)


def attend(g, prefix, q, k0, v0, k1, v1):
    tokens = q.shape[0]
    kv = pl.BlockSpec((tokens, 128), lambda i: (0, i // 2))
    qs = pl.BlockSpec((tokens, 128), lambda i: (0, i))
    return pallas(
        attend_kernel,
        grid=(KV_HEADS,),
        in_specs=[SCALAR, SCALAR, qs, kv, kv, kv, kv],
        out_specs=[qs, pl.BlockSpec((1, 8, tokens), lambda i: (i, 0, 0))],
        out_shape=[jax.ShapeDtypeStruct(q.shape, BF16), jax.ShapeDtypeStruct((KV_HEADS, 8, tokens), F32)],
        scratch_shapes=[pltpu.VMEM((tokens, 2 * tokens), F32)],
        compiler_params=params(62),
        cost_estimate=cost(0.1),
        name="attend",
    )(g, prefix, q, k0, v0, k1, v1)


def attend_back_kernel(g_ref, prefix_ref, q_ref, k0_ref, v0_ref, k1_ref, v1_ref, do_ref, lse_ref,
                       cos_ref, sin_ref, dq_ref, own_ref, early_ref, bias):
    g = g_ref[0]
    which = pl.program_id(0) % 2

    @pl.when(pl.program_id(0) == 0)
    def _():
        fill_bias(bias, prefix_ref, g)

    away = jnp.where(g == 0, -MASKED, 0.0)
    tokens = q_ref.shape[0]
    q, do = stacked_heads(q_ref[...]), stacked_heads(do_ref[...])
    keys = [doubled(k[...], which) for k in (k0_ref, k1_ref)]
    keys_t = jnp.concatenate([k.T[:HEAD].astype(BF16) for k in keys], 1)
    keys = jnp.concatenate([k.astype(BF16) for k in keys], 0)
    values = jnp.concatenate([doubled(v[...], which).astype(BF16) for v in (v0_ref, v1_ref)], 0)
    lse = jnp.concatenate([lse_ref[0, 0:1, :], lse_ref[0, 1:2, :]], 1)
    scores = nt(keys, q)
    probs = jnp.concatenate(
        [jnp.exp(scores[:tokens] + bias[...] - lse), jnp.exp(scores[tokens:] - (lse + away))], 0)
    dprobs = nt(values, do)
    delta = jnp.sum(probs * dprobs, 0, keepdims=True)
    dscores = (probs * (dprobs - delta)).astype(BF16)
    dv = nn(probs.astype(BF16), do)
    dk = nn(dscores, q)
    dq = nn(keys_t, dscores)
    dq = jnp.concatenate([dq[:, :tokens], dq[:, tokens:]], 0).T * (1.0 / math.sqrt(HEAD))
    dq_ref[...] = rotated(dq, cos_ref[...], sin_ref[...], -1.0).astype(BF16)
    for row, grad in enumerate((dk, dv)):
        both = grad + pltpu.roll(grad, HEAD, 1)
        part = both * lane_half(both.shape, which)
        for ref, rows in ((own_ref, slice(0, tokens)), (early_ref, slice(tokens, 2 * tokens))):

            @pl.when(which == 0)
            def _():
                ref[row] = part[rows].astype(ref.dtype)

            @pl.when(which != 0)
            def _():
                ref[row] = (ref[row].astype(F32) + part[rows]).astype(ref.dtype)


def attend_back(g, prefix, q, k0, v0, k1, v1, do, lse, cosine, sine, first, count):
    tokens = q.shape[0]
    kv = pl.BlockSpec((tokens, LANES), lambda i: (0, first // 2 + i // 2))
    qs = pl.BlockSpec((tokens, LANES), lambda i: (0, first + i))
    both = pl.BlockSpec((2, tokens, LANES), lambda i: (0, 0, i // 2))
    shape = jax.ShapeDtypeStruct
    kv_shape = (2, tokens, count * HEAD)
    return pallas(
        attend_back_kernel,
        grid=(count,),
        in_specs=[SCALAR, SCALAR, qs, kv, kv, kv, kv, qs,
                  pl.BlockSpec((1, 8, tokens), lambda i: (first + i, 0, 0)),
                  whole((tokens, LANES)), whole((tokens, LANES))],
        out_specs=[pl.BlockSpec((tokens, LANES), lambda i: (0, i)), both, both],
        out_shape=[shape((tokens, count * LANES), BF16), shape(kv_shape, F32), shape(kv_shape, BF16)],
        scratch_shapes=[pltpu.VMEM((tokens, 2 * tokens), F32)],
        compiler_params=params(28),
        cost_estimate=cost(12),
        name="attend_back",
    )(g, prefix, q, k0, v0, k1, v1, do, lse, cosine, sine)


def output_kernel(where_ref, a_ref, wo0, wo1, wo2, x_ref, gain_ref, res_ref, n_ref):
    res = x_ref[...].astype(F32) + project_rows(a_ref, where_ref, (wo0, wo1, wo2))
    res_ref[...] = res
    scale = lax.rsqrt(jnp.mean(res * res, -1, keepdims=True) + EPSILON)
    n_ref[...] = (res * scale * gain_ref[...]).astype(BF16)


def halves_spec(w):
    shape = (w.shape[0] // 2, w.shape[1])
    return [pl.BlockSpec(shape, lambda *_, n=n: (n, 0), pipeline_mode=pl.Buffered(1)) for n in range(2)]


def output(where, attended, wo, x, gain):
    tokens, width = x.shape
    rows = 256
    row = pl.BlockSpec((rows, width), lambda i: (i, 0))
    return pallas(
        output_kernel,
        grid=(tokens // rows,),
        in_specs=[SCALAR, row, whole(wo[0].shape), *halves_spec(wo[1]), row, whole((1, width))],
        out_specs=[row, row],
        out_shape=[jax.ShapeDtypeStruct((tokens, width), F32), jax.ShapeDtypeStruct((tokens, width), BF16)],
        compiler_params=params(),
        cost_estimate=cost(0.1),
        name="output",
    )(where, attended, *wo, wo[1], x, gain)


def gates_of(rows, router_t, member):
    logits = jnp.where(member > 0.0, nt(rows, router_t), MASKED)
    peak = jnp.max(logits, -1, keepdims=True)
    weights = jnp.where(member > 0.0, jnp.exp(logits - peak), 0.0)
    return weights / jnp.sum(weights, -1, keepdims=True)


def experts_kernel(*refs, first, start, adding, carrying, final):
    refs = list(refs)
    take = lambda n: [refs.pop(0) for _ in range(n)]
    g_ref, x, c = take(3)
    if first:
        member, router, order_in = take(3)
    else:
        gates, xt_in, ct_in = take(3)
    win, wout = take(2)
    olds_in = [take(2) for _ in adding]
    grad_in, sum_in, gg_in = take(3) if carrying else (None, None, None)
    keep, send, grad, total = take(4)
    gg_out = None if final else take(1)[0]
    if first:
        gates, xt_out, ct_out = take(3)
    hid_scr, dgu_scr, grad_scr, sum_scr, gg_scr, xt, ct, sems = take(8)
    order = take(1)[0] if first else None
    keep_old, send_old = take(2) if adding else (None, None)
    grad_low, sum_low = take(2) if final else (grad_scr, sum_scr)
    step = pl.program_id(0)
    at_start, at_end = step == 0, step == pl.num_programs(0) - 1
    width = x.shape[1]
    column = g_ref[0] * (EXPERTS // 2) + start + step
    copy = lambda n, source, target: pltpu.make_async_copy(source, target, sems.at[n])
    loads = [copy(0, order_in, order)] if first else [copy(0, xt_in, xt), copy(1, ct_in, ct)]
    sums_in = [copy(2, grad_in, grad_scr), copy(3, sum_in, sum_scr)] if carrying else []
    olds = []
    for (keep_in, send_in), (skip, _) in zip(olds_in, adding):
        olds += [copy(4, keep_in.at[step + skip], keep_old), copy(5, send_in.at[step + skip], send_old)]
    sums_out = [copy(6, grad_low, grad), copy(7, sum_low, total)]
    turned_out = [copy(8, xt, xt_out), copy(9, ct, ct_out)] if first else []

    @pl.when(at_start)
    def _():
        for load in loads + sums_in:
            load.start()
        if first:
            gates[...] = gates_of(x[...], router[...], member[...])
        gg_scr[...] = gg_in[...] if carrying else jnp.zeros_like(gg_scr)

    for old in olds:
        old.start()
    probs = gates[...]
    mine = lax.broadcasted_iota(jnp.int32, probs.shape, 1) == column
    p = jnp.sum(jnp.where(mine, probs, 0.0), 1, keepdims=True)
    gate_up = nn(x[...], win[0])
    back = nn(c[...], wout[0])
    gate, up = gate_up[:, :FF], gate_up[:, FF:]
    sig = 1.0 / (1.0 + jnp.exp(-gate))
    act = gate * sig
    hid = act * up
    gg_scr[...] = jnp.where(mine, jnp.sum(hid * back, 1, keepdims=True), gg_scr[...])
    back = back * p
    dgate = back * up * (sig * (1.0 + gate * (1.0 - sig)))
    hid_scr[...] = (hid * p).astype(BF16)
    dgu_scr[:, :FF] = dgate.astype(BF16)
    dgu_scr[:, FF:] = (back * act).astype(BF16)

    if carrying:

        @pl.when(at_start)
        def _():
            for load in sums_in:
                load.wait()

    for scr, value in ((sum_scr, nt(hid_scr[...], wout[0])), (grad_scr, nt(dgu_scr[...], win[0]))):
        if carrying:
            scr[...] += value
        else:

            @pl.when(at_start)
            def _():
                scr[...] = value

            @pl.when(jnp.logical_not(at_start))
            def _():
                scr[...] += value

    @pl.when(at_end)
    def _():
        if final:
            sum_low[...] = sum_scr[...].astype(BF16)
            grad_low[:, :width] = grad_scr[...].astype(BF16)
            grad_low[:, width:] = gg_scr[...].astype(BF16)
        else:
            gg_out[...] = gg_scr[...]
        for store in sums_out:
            store.start()

    @pl.when(at_start)
    def _():
        for load in loads:
            load.wait()
        if first:
            xt[...] = nt(order[...], x[...]).astype(BF16)
            ct[...] = nt(order[...], c[...]).astype(BF16)
            for store in turned_out:
                store.start()

    for old in olds:
        old.wait()
    for out, old, base in ((keep, keep_old, 0), (send, send_old, width // 2)):
        rows = pl.ds(base, width // 2)
        for cols, left, right in ((slice(0, 2 * FF), xt, dgu_scr), (slice(2 * FF, 3 * FF), ct, hid_scr)):
            value = nn(left[rows], right[...])
            if adding:
                value = value + old[:, cols].astype(F32)
            out[0, :, cols] = value.astype(BF16)

    @pl.when(at_end)
    def _():
        for store in sums_out + turned_out:
            store.wait()


def experts(g, x, c, win, wout, start, count, fresh=None, known=None, adding=(), carrying=None, final=False):
    tokens, width = x.shape
    cols = 3 * FF
    shape = jax.ShapeDtypeStruct
    half = pl.BlockSpec((1, width // 2, cols), lambda i: (i, 0, 0))
    anywhere = pl.BlockSpec(memory_space=pl.ANY)
    wide, narrow, turned = (tokens, width), (tokens, LANES), (width, tokens)
    back = (tokens, width + LANES)
    args = [g, x, c, *(fresh or known), win, wout]
    specs = [SCALAR, whole(wide), whole(wide)]
    specs += [whole(narrow), whole(fresh[1].shape), anywhere] if fresh else [whole(narrow), anywhere, anywhere]
    specs += [pl.BlockSpec((1, width, 2 * FF), lambda i: (start + i, 0, 0)),
              pl.BlockSpec((1, width, FF), lambda i: (start + i, 0, 0))]
    for keep, send, _, _ in adding:
        args += [keep, send]
        specs += [anywhere, anywhere]
    if carrying:
        args += carrying
        specs += [anywhere, anywhere, whole(narrow)]
    outs = [half, half, anywhere, anywhere]
    shapes = [shape((count, width // 2, cols), BF16), shape((count, width // 2, cols), BF16)]
    if final:
        shapes += [shape(back, BF16), shape(wide, BF16)]
    else:
        outs += [whole(narrow)]
        shapes += [shape(wide, F32), shape(wide, F32), shape(narrow, F32)]
    if fresh:
        outs += [whole(narrow), anywhere, anywhere]
        shapes += [shape(narrow, F32), shape(turned, BF16), shape(turned, BF16)]
    scratch = [pltpu.VMEM((tokens, FF), BF16), pltpu.VMEM((tokens, 2 * FF), BF16),
               pltpu.VMEM(wide, F32), pltpu.VMEM(wide, F32), pltpu.VMEM(narrow, F32),
               pltpu.VMEM(turned, BF16), pltpu.VMEM(turned, BF16), pltpu.SemaphoreType.DMA((10,))]
    if fresh:
        scratch += [pltpu.VMEM((width, width), BF16)]
    if adding:
        scratch += [pltpu.VMEM((width // 2, cols), BF16)] * 2
    if final:
        scratch += [pltpu.VMEM(back, BF16), pltpu.VMEM(wide, BF16)]
    return pallas(
        functools.partial(experts_kernel, first=fresh is not None, start=start,
                          adding=tuple(entries for _, _, *entries in adding),
                          carrying=carrying is not None, final=final),
        grid=(count,),
        in_specs=specs,
        out_specs=outs,
        out_shape=shapes,
        scratch_shapes=scratch,
        compiler_params=params(62),
        cost_estimate=cost((3 if adding and carrying else 8) * count),
        name="experts",
    )(*args)


def middle_kernel(where_ref, c_ref, grad_ref, back_ref, gg_ref, p_ref, router_ref, res_ref, gain_ref,
                  wo0, wo1, wo2, dres_ref, low_ref, da_ref, dl_ref, dgain_ref):
    width = c_ref.shape[1]
    p = p_ref[...]
    gg = gg_ref[...] + back_ref[:, width:].astype(F32)
    dlogits = p * (gg - jnp.sum(p * gg, 1, keepdims=True))
    dl_ref[...] = dlogits.astype(BF16)
    high = dlogits.astype(BF16)
    rest = (dlogits - high.astype(F32)).astype(BF16)
    router = router_ref[...]
    grad = grad_ref[...] + back_ref[:, :width].astype(F32) + (nn(high, router) + nn(rest, router))
    res = res_ref[...]
    scale = lax.rsqrt(jnp.mean(res * res, -1, keepdims=True) + EPSILON)
    part = jnp.broadcast_to(jnp.sum(grad * (res * scale), 0, keepdims=True), dgain_ref.shape)

    @pl.when(pl.program_id(0) == 0)
    def _():
        dgain_ref[...] = part

    @pl.when(pl.program_id(0) != 0)
    def _():
        dgain_ref[...] += part

    w = grad * gain_ref[...]
    dres = c_ref[...].astype(F32) + (scale * w - res * (scale * scale * scale)
                                     * jnp.mean(w * res, -1, keepdims=True))
    dres_ref[...] = dres
    low = dres.astype(BF16)
    low_ref[...] = low
    for at, wo in zip(pieces(where_ref, width), (wo0, wo1, wo2)):
        da_ref[:, at] = nt(low, wo[...]).astype(BF16)


def middle(where, c, grad, back, gg, p, router_t, res, gain, wo):
    tokens, width = c.shape
    rows = 256
    row = lambda n: pl.BlockSpec((rows, n), lambda i: (i, 0))
    shape = jax.ShapeDtypeStruct
    return pallas(
        middle_kernel,
        grid=(tokens // rows,),
        in_specs=[SCALAR, row(width), row(width), row(width + LANES), row(LANES), row(LANES),
                  whole((LANES, width)), row(width), whole((1, width)), whole(wo[0].shape), *halves_spec(wo[1])],
        out_specs=[row(width), row(width), row(width), row(LANES), pl.BlockSpec((8, width), lambda i: (0, 0))],
        out_shape=[shape((tokens, width), F32), shape((tokens, width), BF16), shape((tokens, width), BF16),
                   shape((tokens, LANES), BF16), shape((8, width), F32)],
        compiler_params=params(),
        cost_estimate=cost(100),
        name="middle",
    )(where, c, grad, back, gg, p, router_t, res, gain, *wo, wo[1])


def weight_kernel(*refs, joined):
    refs = list(refs)
    take = lambda n: [refs.pop(0) for _ in range(n)]
    xt, dq, own, early, cos, sin = take(6)
    order, low, att, xt_ffn, dlogits, dgain = take(6) if joined else [None] * 6
    keep, dkv, send = take(3)
    half = keep.shape[0]
    dk = rotated(own[0] + early[0].astype(F32), cos[...], sin[...], -1.0).astype(BF16)
    dv = (own[1] + early[1].astype(F32)).astype(BF16)
    nq, nk = dq.shape[1], dk.shape[1]
    dkv[:, :nk] = dk
    dkv[:, nk:] = dv
    if joined:
        low_t, gain_rows = take(2)
        low_t[...] = nt(order[...], low[...]).astype(BF16)
        row = lax.broadcasted_iota(jnp.int32, gain_rows.shape, 0)
        gain_rows[...] = jnp.where(row == EXPERTS, dgain[0:1, :], 0.0).astype(BF16)
    def put(cols, rows, value):
        (keep if rows.start == 0 else send)[:, cols] = value.astype(BF16)

    for base in (0, half):
        rows = pl.ds(base, half)
        put(slice(0, nq), rows, nn(xt[rows], dq[...]))
        first = nq + 2 * nk
        put(slice(nq, first), rows, nn(xt[rows], dkv[...]))
        if joined:
            wide = att.shape[1]
            put(slice(first, first + wide), rows, nn(low_t[rows], att[...]))
            put(slice(first + wide, first + wide + LANES), rows,
                nn(xt_ffn[rows], dlogits[...]) + nt(order[rows], gain_rows[...]))


def weight_grads(xt, dq, own, early, cosine, sine, joined=None):
    width, tokens = xt.shape
    nq, nk = dq.shape[1], own.shape[2]
    shape = jax.ShapeDtypeStruct
    cols = nq + 2 * nk + (joined[2].shape[1] + LANES if joined else 0)
    out = shape((width // 2, cols), BF16)
    vmem = pl.BlockSpec(memory_space=pltpu.VMEM)
    args = (xt, dq, own, early, cosine, sine, *(joined or ()))
    return pallas(
        functools.partial(weight_kernel, joined=bool(joined)),
        in_specs=[vmem] * len(args),
        out_specs=[vmem] * 3,
        out_shape=[out, shape((tokens, 2 * nk), BF16), out],
        scratch_shapes=[pltpu.VMEM((width, tokens), BF16), pltpu.VMEM((LANES, width), BF16)] if joined else [],
        compiler_params=params(),
        cost_estimate=cost(0.1 if joined else 60),
        name="weight_grads",
    )(*args)


def input_kernel(where_ref, *refs, parts):
    refs = list(refs)
    take = lambda n: [refs.pop(0) for _ in range(n)]
    dqs, dkvs, wq, wk, wv = take(parts), take(parts), take(1), take(1), take(1)
    packs = take(4)
    x_ref, gain_ref, dres_ref, out_ref, grad = refs
    nq, nk = wq[0].shape[1], wk[0].shape[1]
    columns = []
    for n in range(parts):
        q0, k0 = n * nq // parts, n * nk // parts
        q1, k1 = q0 + nq // parts, k0 + nk // parts
        dkv = dkvs[n][...]
        half = dkv.shape[1] // 2
        for left, own, first, (lo, hi) in (
                (dqs[n][...], wq[0], None, (q0, q1)),
                (dkv[:, :half], wk[0], 0, (k0, k1)),
                (dkv[:, half:], wv[0], nk, (k0, k1))):
            packed = slice(lo, hi) if first is None else slice(first + lo, first + hi)
            columns.append((left, own, slice(lo, hi), (first is not None, packed)))
    at = pieces(where_ref, x_ref.shape[1])
    grad[:, at[0]] = sum(nt(left, own[:, mine]) for left, own, mine, _ in columns)
    for place, pack in zip(at[1:], (packs[0::2], packs[1::2])):
        grad[:, place] = sum(nt(left, pack[which][:, packed]) for left, _, _, (which, packed) in columns)
    x = x_ref[...].astype(F32)
    scale = lax.rsqrt(jnp.mean(x * x, -1, keepdims=True) + EPSILON)
    w = grad[...] * gain_ref[...]
    out_ref[...] = dres_ref[...] + (scale * w - x * (scale * scale * scale) * jnp.mean(w * x, -1, keepdims=True))


def input_grads(where, dqs, dkvs, wq, wk, wv, pack, x, gain, dres):
    tokens, width = x.shape
    rows = 256
    row = lambda a: pl.BlockSpec((rows, a.shape[1]), lambda i: (i, 0))
    weights = (wq, wk, wv, *pack[0], *pack[1])
    return pallas(
        functools.partial(input_kernel, parts=len(dqs)),
        grid=(tokens // rows,),
        in_specs=[SCALAR, *map(row, dqs), *map(row, dkvs), *(whole(w.shape) for w in weights), row(x),
                  whole((1, width)), row(dres)],
        out_specs=row(dres),
        out_shape=jax.ShapeDtypeStruct((tokens, width), F32),
        scratch_shapes=[pltpu.VMEM((rows, width), F32)],
        compiler_params=params(),
        cost_estimate=cost(5),
        name="input_grads",
    )(where, *dqs, *dkvs, *weights, x, gain, dres)


def exchange(value, *bits):
    count = lax.axis_size("replica")
    flip = sum(count if b == "group" else 1 << b for b in bits)
    return lax.ppermute(value, ("group", "replica"), [(i, i ^ flip) for i in range(2 * count)])


def after(value, *others):
    out = lax.optimization_barrier((value, *others))
    return out[0], list(out[1:])


def deal(out, to, entries, rows):
    def some(source, target, size):
        value = sum(p[e, pl.ds(source, size), :].astype(F32) for p, e in entries)
        out[to, pl.ds(target, size), :] = value.astype(BF16)

    at = 0
    for start, total in rows:
        step = 32
        if total % step == 0 and total > step and start % step == 0 and at % step == 0:

            @pl.loop(0, total // step)
            def _(i, start=start, at=at):
                some(pl.multiple_of(start + i * step, step), pl.multiple_of(at + i * step, step), step)

        else:
            some(start, at, total)
        at += total


def deal_entries(out, to, parts, firsts, count, rows):
    @pl.loop(0, count)
    def _(n):
        deal(out, to + n, [(p, first + n) for p, first in zip(parts, firsts)], rows)


def split_kernel(*refs, groups):
    refs = list(refs)
    parts = [[refs.pop(0) for _ in firsts] for firsts, _, _, _, _ in groups]
    for part, (firsts, count, outs, to, ranges) in zip(parts, groups):
        for out, rows in zip(outs, ranges):
            deal_entries(refs[out], to, part, firsts, count, rows)


def stream_kernel(*refs, count, pieces):
    parts, outs = refs[:count], list(refs[count:])
    for first, size, ranges in pieces:
        mine = [outs.pop(0) for _ in ranges]

        @pl.when((pl.program_id(0) >= first) & (pl.program_id(0) < first + size))
        def _():
            for out, rows in zip(mine, ranges):
                deal(out, 0, [(p, 0) for p in parts], rows)


def ranges_of(axes, chunk, bits):
    spots = np.stack(np.unravel_index(np.arange(2 ** len(axes)), (2,) * len(axes)), 1)
    at = [axes.index(b) for b in bits]
    ranges = []
    for combo in np.ndindex(*(2,) * len(bits)):
        rows = []
        for n in np.nonzero((spots[:, at] == combo).all(1))[0]:
            if rows and rows[-1][0] + rows[-1][1] == n * chunk:
                rows[-1] = (rows[-1][0], rows[-1][1] + chunk)
            else:
                rows.append((int(n) * chunk, chunk))
        ranges.append(tuple(rows))
    return tuple(ranges)


def flips_of(bits):
    return [[b for b, on in zip(bits, combo) if on] for combo in list(np.ndindex(*(2,) * len(bits)))[1:]]


class Run:
    def __init__(self, parts, axes, chunk, first=0, count=1):
        self.parts, self.axes, self.chunk, self.first, self.count = list(parts), list(axes), chunk, first, count


def firsts_of(run):
    return tuple(run.first if p.shape[0] > run.count else 0 for p in run.parts)


def split_call(groups, args, shapes):
    vmem = pl.BlockSpec(memory_space=pltpu.VMEM)
    return pallas(
        functools.partial(split_kernel, groups=tuple(groups)),
        in_specs=[vmem] * len(args),
        out_specs=[vmem] * len(shapes),
        out_shape=[jax.ShapeDtypeStruct(shape, BF16) for shape in shapes],
        compiler_params=params(),
        cost_estimate=cost(0.1),
        name="split",
    )(*args)


def split(runs, bit):
    axes, chunk = runs[0].axes, runs[0].chunk
    ranges = ranges_of(axes, chunk, (bit,))
    total, groups = 0, []
    for run in runs:
        groups.append((firsts_of(run), run.count, (0, 1), total, ranges))
        total += run.count
    shapes = [(total, sum(n for _, n in rows), runs[0].parts[0].shape[2]) for rows in ranges]
    kept, send = split_call(groups, [p for run in runs for p in run.parts], shapes)
    return Run([kept, exchange(send, bit)], [b for b in axes if b != bit], chunk, 0, total)


def split_each(*pieces):
    groups, shapes = [], []
    for run, bit in pieces:
        ranges = ranges_of(run.axes, run.chunk, (bit,))
        groups.append((firsts_of(run), run.count, (len(shapes), len(shapes) + 1), 0, ranges))
        shapes += [(run.count, sum(n for _, n in rows), run.parts[0].shape[2]) for rows in ranges]
    outs = list(split_call(groups, [p for run, _ in pieces for p in run.parts], shapes))
    made = []
    for run, bit in pieces:
        kept, send = outs.pop(0), outs.pop(0)
        made.append(Run([kept, exchange(send, bit)], [b for b in run.axes if b != bit], run.chunk, 0, run.count))
    return made


def split_apart(run, *pieces):
    rows, cols = run.parts[0].shape[1:]
    shapes, specs, plan, first = [], [], [], 0
    for bits, count in pieces:
        ranges = ranges_of(run.axes, run.chunk, bits)
        plan.append((first, count, ranges))
        for chosen in ranges:
            size = sum(n for _, n in chosen)
            shapes.append(jax.ShapeDtypeStruct((count, size, cols), BF16))
            specs.append(pl.BlockSpec(
                (1, size, cols), lambda i, first=first, count=count: (jnp.clip(i - first, 0, count - 1), 0, 0)))
        first += count
    outs = list(pallas(
        functools.partial(stream_kernel, count=len(run.parts), pieces=tuple(plan)),
        grid=(first,),
        in_specs=[pl.BlockSpec((1, rows, cols), lambda i: (i, 0, 0))] * len(run.parts),
        out_specs=specs,
        out_shape=shapes,
        compiler_params=params(62 if first > 2 else 24),
        cost_estimate=cost(0.1),
        name="split_apart",
    )(*run.parts))
    runs = []
    for bits, count in pieces:
        kept = outs.pop(0)
        received = [exchange(outs.pop(0), *flip) for flip in flips_of(bits)]
        runs.append(Run([kept, *received], [b for b in run.axes if b not in bits], run.chunk, 0, count))
    return runs


def block_sum(residual, own, other):
    def kernel(a, b, c, out):
        out[...] = (a[...] + b[...] + c[...].astype(F32)).astype(BF16)

    tokens, width = residual.shape
    row = pl.BlockSpec((tokens // 4, width), lambda i: (i, 0))
    return pallas(
        kernel,
        grid=(4,),
        in_specs=[row] * 3,
        out_specs=row,
        out_shape=jax.ShapeDtypeStruct(residual.shape, BF16),
        compiler_params=params(),
        cost_estimate=cost(0.1),
        name="block_sum",
    )(residual, own, other)


def finish_attention_kernel(*refs, counts):
    refs = list(refs)
    take = lambda n: [refs.pop(0) for _ in range(n)]
    joined, alone = take(counts[0]), take(counts[1])
    wq, wk, wv, gain = take(4)
    dq, dk, dv, do, drouter, dgain_attn, dgain_ffn = refs
    a = sum(p[0].astype(F32) for p in joined)
    b = sum(p[0].astype(F32) for p in alone)
    nq, nk = wq.shape[1] // 2, wk.shape[1] // 2
    dgain = 0.0
    for n, part in enumerate((a, b)):
        for ref, w, size, first in ((dq, wq, nq, 0), (dk, wk, nk, nq), (dv, wv, nk, nq + nk)):
            grad = part[:, first : first + size]
            ref[:, n * size : (n + 1) * size] = grad
            dgain = dgain + jnp.sum(grad * w[:, n * size : (n + 1) * size].astype(F32), 1, keepdims=True)
    dgain_attn[...] = dgain / gain[...]
    first = nq + 2 * nk
    width = do.shape[0]
    do[...] = a[:, first : first + width].T
    last = a[:, first + width :]
    drouter[...] = last[:, :EXPERTS]
    lane = lax.broadcasted_iota(jnp.int32, last.shape, 1)
    dgain_ffn[...] = jnp.sum(jnp.where(lane == EXPERTS, last, 0.0), 1, keepdims=True)


def finish_attention(joined, alone, wq, wk, wv, gain, width):
    chunk = wq.shape[0]
    shape = lambda *s: jax.ShapeDtypeStruct(s, F32)
    args = (*joined, *alone, wq, wk, wv, gain)
    vmem = pl.BlockSpec(memory_space=pltpu.VMEM)
    return pallas(
        functools.partial(finish_attention_kernel, counts=(len(joined), len(alone))),
        in_specs=[vmem] * len(args),
        out_specs=[vmem] * 7,
        out_shape=[shape(chunk, wq.shape[1]), shape(chunk, wk.shape[1]), shape(chunk, wv.shape[1]),
                   shape(width, chunk), shape(chunk, EXPERTS), shape(chunk, 1), shape(chunk, 1)],
        compiler_params=params(),
        cost_estimate=cost(0.1),
        name="finish_attention",
    )(*args)


def finish_experts_kernel(g_ref, *refs):
    own, other, (win, wout) = refs[: len(refs) // 2 - 1], refs[len(refs) // 2 - 1 : -2], refs[-2:]
    count = win.shape[0] // 2
    g = g_ref[0]
    for parts, side in ((own, g), (other, 1 - g)):
        e = 0
        for p in parts:
            for n in range(p.shape[0]):
                win[side * count + e] = p[n, :, : 2 * FF].astype(F32)
                wout[side * count + e] = p[n, :, 2 * FF :].astype(F32)
                e += 1


def finish_experts(g, own, other):
    chunk = own[0].shape[1]
    shape = lambda *s: jax.ShapeDtypeStruct(s, F32)
    vmem = pl.BlockSpec(memory_space=pltpu.VMEM)
    return pallas(
        finish_experts_kernel,
        in_specs=[SCALAR] + [vmem] * (2 * len(own)),
        out_specs=[vmem] * 2,
        out_shape=[shape(EXPERTS, chunk, 2 * FF), shape(EXPERTS, chunk, FF)],
        compiler_params=params(),
        cost_estimate=cost(0.1),
        name="finish_experts",
    )(g, *own, *other)


def on_device(
    block_in, attn_gain, query_weight, key_weight, value_weight, out_weight, ffn_gain, router_weight,
    expert_in, expert_out, routes, prefix, cotangent,
):
    FOLLOWED.clear()
    replicas = lax.axis_size("replica")
    bits = replicas.bit_length() - 1
    tokens, width = block_in.shape[1:]
    half = width // 2
    chunk = half // replicas
    group, replica = lax.axis_index("group"), lax.axis_index("replica")
    core = replica % 2
    g = group.astype(jnp.int32).reshape(1)
    where = jnp.stack([group, core]).astype(jnp.int32)
    x, cot = block_in[0], cotangent[0]
    swap = lambda v: exchange(v, "group")

    def ordered(own, other, axis):
        return jnp.where(group == 0, jnp.concatenate([own, other], axis), jnp.concatenate([other, own], axis))

    quarter = lambda w: lax.dynamic_slice_in_dim(w, core * (w.shape[0] // 2), w.shape[0] // 2, 0)
    pack_q, pack_kv = quarter(query_weight), jnp.concatenate([quarter(key_weight), quarter(value_weight)], 1)
    pack_kv, (x_send, wo_send, cot_send) = after(pack_kv, x, out_weight, cot)
    pack_q, pack_kv = swap(pack_q), swap(pack_kv)
    x_early = lax.ppermute(x_send, "group", [(0, 1)])
    wo = (out_weight, swap(wo_send))
    cot_other = swap(cot_send)
    lanes = jnp.arange(LANES, dtype=jnp.int32)
    member = (routes[0][:, :, None] == lanes[None, None, :]).any(1).astype(F32)
    member_t = (routes[0].T[:, None, :] == lanes[None, :EXPERTS, None]).any(0).astype(BF16)
    small = jnp.concatenate([attn_gain[None], ffn_gain[None], router_weight.T, member_t], 0)
    small_other = swap(small)
    vectors = ordered(small[: 2 + EXPERTS], small_other[: 2 + EXPERTS], 1)
    member_other = jnp.pad(small_other[2 + EXPERTS :].T.astype(F32), ((0, 0), (0, LANES - EXPERTS)))
    gain_attn, gain_ffn = vectors[0:1].astype(F32), vectors[1:2].astype(F32)
    router_t = jnp.concatenate([vectors[2:], jnp.zeros((LANES - EXPERTS, width), BF16)], 0)

    cosine, sine, *early_tables = tables(g, tokens)
    place = np.arange(width)
    blocks, inner = place // chunk, place % chunk
    reverse = np.zeros_like(blocks)
    for b in range(bits):
        reverse |= ((blocks >> 1 >> (bits - 1 - b)) & 1) << b
    feature = ((jnp.asarray(blocks & 1, jnp.int32) ^ group) * half
               + (jnp.asarray(reverse, jnp.int32) ^ replica) * chunk + jnp.asarray(inner, jnp.int32))
    order = (feature[:, None] == jnp.arange(width, dtype=jnp.int32)[None, :]).astype(BF16)

    mine = lambda a: lax.dynamic_slice_in_dim(a, replica * chunk, chunk, 0)
    rows = (mine(query_weight), mine(key_weight), mine(value_weight), mine(attn_gain).astype(F32)[:, None])
    pack_q, (pack_kv, cosine, sine, member, order, gain_attn, member_other, *more) = after(
        pack_q, pack_kv, cosine, sine, member, order, gain_attn, member_other, *early_tables, *rows)
    early_tables, rows = more[:2], more[2:]
    pack = (pack_q, exchange(pack_q, 0)), (pack_kv, exchange(pack_kv, 0))

    _, q, k, v, normed_t = project(
        where, x, gain_attn, query_weight, key_weight, value_weight, pack, cosine, sine, order)
    k1, v1 = project_earlier(where, x_early, gain_attn, key_weight, value_weight, pack, *early_tables)
    attended, lse = attend(g, prefix, q, k, v, k1, v1)
    whole_where = jnp.stack([group, 0 * core]).astype(jnp.int32)
    residual, normed = output(whole_where, attended, wo, x, gain_ffn)
    normed_other = swap(normed)
    count = expert_in.shape[0] // 2
    near = lambda *a, **k: experts(g, normed, cot, expert_in, expert_out, *a, **k)
    far = lambda *a, **k: experts(g, *a[0], expert_in, expert_out, *a[1:], **k)
    keep, send, grad_own, sum_own, gg_own, *known = near(0, count, fresh=(member, router_t, order))
    gates, xt_own, _ = known
    normed_other, (cot_other, keep) = after(normed_other, cot_other, keep)
    keep_a, send_a, *sums, gates_o, xt_o, ct_o = far(
        (normed_other, cot_other), 0, count, fresh=(member_other, router_t, order), adding=[(keep, send, 0, count)])
    received_a = exchange(send_a, 0)
    keep, send, back, sum_other = far(
        (normed_other, cot_other), count, count, known=(gates_o, xt_o, ct_o), carrying=sums, final=True)
    back = swap(back)
    two = count // 2
    dims = [*range(1, bits), "group"]
    first, second, *rest = [*range(1, bits)]
    run_a = Run((keep_a, received_a), dims, chunk, 0, count)
    run0, run1 = split_apart(run_a, ((first,), two), ((second,), two))
    sums, run_b = (grad_own, sum_own, gg_own), []
    for part in (0, two):
        keep_b, send_b, *sums = near(
            count + part, two, known=known, adding=[(keep, send, part, two)], carrying=sums)
        run_b.append(Run((keep_b, exchange(send_b, 0)), dims, chunk, 0, two))
    grad_own, sum_own, gg_own = sums
    back, (keep_b,) = after(back, keep_b)
    run0, run1 = split_each((run0, second), (run1, first))

    grad_res, grad_low, grad_att, grad_logits, grad_gain = middle(
        whole_where, cot, grad_own, back, gg_own, gates, router_t, residual, gain_ffn, wo)
    grad_low, (sum_send,) = after(grad_low, sum_other)
    sum_other = swap(sum_send)
    (run2,), (run3,) = (split_apart(run, ((first,), two)) for run in run_b)
    heads = KV_HEADS // 2
    attn = lambda first: attend_back(g, prefix, q, k, v, k1, v1, grad_att, lse, cosine, sine, first, heads)
    to_earlier = lambda a: lax.ppermute(a, "group", [(1, 0)])
    dq0, own0, early0 = attn(0)
    early0 = to_earlier(early0)
    run_a = run0, run1
    for bit in rest:
        run_a = [split(run_a, bit)]
    dq1, own1, early1 = attn(heads)
    early1 = to_earlier(early1)
    one = lambda keep, send: Run((keep[None], exchange(send, 0)[None]), dims, chunk)
    keep0, dkv0, send0 = weight_grads(
        normed_t, dq0, own0, early0, cosine, sine,
        joined=(order, grad_low, attended, xt_own, grad_logits, grad_gain))
    attn0 = one(keep0, send0)
    run2 = split([run2], second)
    block_out = block_sum(residual, sum_own, sum_other)
    swap_a = split(run_a, "group")
    keep1, dkv1, send1 = weight_grads(normed_t, dq1, own1, early1, cosine, sine)
    attn1 = one(keep1, send1)
    order0, order1 = ["group", first, second, *rest], [first, "group", second, *rest]
    attn0 = split([attn0], order0.pop(0))
    input_grad = input_grads(where, (dq0, dq1), (dkv0, dkv1), query_weight, key_weight, value_weight, pack,
                             x, gain_attn, grad_res)
    attn1 = split([attn1], order1.pop(0))
    run3 = split([run3], second)
    for bit in rest:
        run2 = split([run2], bit)
    for _ in range(2):
        attn0 = split([attn0], order0.pop(0))
        attn1 = split([attn1], order1.pop(0))
    for bit in rest:
        run3 = split([run3], bit)
    while order0:
        attn0 = split([attn0], order0.pop(0))
        attn1 = split([attn1], order1.pop(0))
    swap_b = split([run2, run3], "group")

    query_grad, key_grad, value_grad, out_grad, router_grad, attn_gain_grad, ffn_gain_grad = finish_attention(
        attn0.parts, attn1.parts, *rows, width)
    expert_in_grad, expert_out_grad = finish_experts(
        g, (swap_a.parts[0], swap_b.parts[0]), (swap_a.parts[1], swap_b.parts[1]))
    return (
        block_out[None], input_grad[None], attn_gain_grad[:, 0], query_grad, key_grad, value_grad, out_grad,
        ffn_gain_grad[:, 0], router_grad, expert_in_grad, expert_out_grad,
    )


def solution(mesh):
    placed = (
        P("replica", "group", None),
        P("group"),
        P("group", None),
        P("group", None),
        P("group", None),
        P("group", None),
        P("group"),
        P("group", None),
        P("group", None, None),
        P("group", None, None),
        P("replica", "group", None),
        P("replica"),
        P("replica", "group", None),
    )
    both = ("group", "replica")
    return jax.shard_map(
        on_device,
        mesh=mesh,
        in_specs=placed,
        out_specs=(
            P("replica", "group", None),
            P("replica", "group", None),
            P(both),
            P(both, None),
            P(both, None),
            P(both, None),
            P(None, both),
            P(both),
            P(both, None),
            P(None, both, None),
            P(None, both, None),
        ),
        check_vma=False,
    )
```

```python
import functools
import math

import jax
import jax.numpy as jnp
import numpy as np
from jax import lax
from jax.experimental import pallas as pl
from jax.experimental.pallas import tpu as pltpu
from jax.sharding import PartitionSpec as P

HEADS = 16
KV_HEADS = 8
HEAD = 64
FF = 512
TOP = 8
EXPERTS = 16

EPSILON = 1e-06
THETA_BASE = 10000.0
MASKED = -1e30
HIGHEST = lax.Precision.HIGHEST
F32 = jnp.float32
BF16 = jnp.bfloat16
MIB = 1 << 20


def nn(left, right):
    return lax.dot_general(left, right, (((1,), (0,)), ((), ())), preferred_element_type=F32)


def nt(left, right):
    return lax.dot_general(left, right, (((1,), (1,)), ((), ())), preferred_element_type=F32)


def params(limit=24):
    return pltpu.CompilerParams(vmem_limit_bytes=limit * MIB)


def cost(microseconds):
    return pl.CostEstimate(flops=int(microseconds * 0.9e9), bytes_accessed=int(microseconds * 1e5), transcendentals=0)


def whole(shape):
    return pl.BlockSpec(shape, lambda *_: (0,) * len(shape), pipeline_mode=pl.Buffered(1))


SCALAR = pl.BlockSpec(memory_space=pltpu.SMEM)

FOLLOWED = []


def pallas(kernel, *, in_specs, out_shape, **more):
    def call(*args):
        tokens, count = list(FOLLOWED), len(in_specs)

        def body(*refs):
            kernel(*refs[:count], *refs[count + len(tokens) :])

        out = pl.pallas_call(
            body,
            in_specs=[*in_specs, *[pl.BlockSpec(memory_space=pl.ANY)] * len(tokens)],
            out_shape=out_shape,
            **more,
        )(*args, *tokens)
        FOLLOWED[:] = [min(jax.tree.leaves(out), key=lambda a: a.size)]
        return out

    return call
LANES = 128


def pieces(where_ref, width):
    g, core = where_ref[0], where_ref[1]
    half, quarter = width // 2, width // 4
    other = (1 - g) * half
    at = lambda start, size: pl.ds(pl.multiple_of(start, size), size)
    return (at(g * half, half), at(other + core * quarter, quarter), at(other + (1 - core) * quarter, quarter))


def project_rows(ref, where_ref, weights):
    cols = pieces(where_ref, ref.shape[1])
    return sum(nn(ref[:, c], w[...]) for c, w in zip(cols, weights))


def swap_halves(tile):
    lane = lax.broadcasted_iota(jnp.int32, tile.shape, 1) % HEAD
    return jnp.where(
        lane < HEAD // 2, pltpu.roll(tile, 128 - HEAD // 2, 1), pltpu.roll(tile, HEAD // 2, 1)
    )


def rotated(values, cosine, sine, sign):
    tiles = []
    for start in range(0, values.shape[1], 128):
        tile = values[:, start : start + 128]
        tiles.append(tile * cosine + swap_halves(tile) * (sine * sign))
    return tiles[0] if len(tiles) == 1 else jnp.concatenate(tiles, 1)


def tables_kernel(g_ref, rate_ref, cos_ref, sin_ref, early_cos_ref, early_sin_ref):
    shape = cos_ref.shape
    lane = lax.broadcasted_iota(jnp.int32, shape, 1)
    row = lax.broadcasted_iota(jnp.int32, shape, 0)
    sign = jnp.where(lane % HEAD < HEAD // 2, -1.0, 1.0)
    for first, cos, sin in ((g_ref[0] * shape[0], cos_ref, sin_ref), (0, early_cos_ref, early_sin_ref)):
        angle = (row + first).astype(F32) * rate_ref[...]
        cos[...] = jnp.cos(angle)
        sin[...] = jnp.sin(angle) * sign


def tables(g, tokens):
    rate = THETA_BASE ** (-jnp.arange(HEAD // 2, dtype=F32) * 2.0 / HEAD)
    shape = jax.ShapeDtypeStruct((tokens, LANES), F32)
    vmem = pl.BlockSpec(memory_space=pltpu.VMEM)
    return pallas(
        tables_kernel,
        in_specs=[SCALAR, vmem],
        out_specs=[vmem] * 4,
        out_shape=[shape] * 4,
        compiler_params=params(),
        cost_estimate=cost(0.1),
        name="tables",
    )(g, jnp.tile(rate, LANES * 2 // HEAD)[None])


def project_kernel(where_ref, x_ref, gain_ref, wq0, wq1, wq2, wk0, wk1, wk2, wv0, wv1, wv2, cos_ref, sin_ref,
                   order_ref, n_ref, q_ref, k_ref, v_ref, nt_ref):
    @pl.when(pl.program_id(0) == 0)
    def _():
        x = x_ref[...].astype(F32)
        scale = lax.rsqrt(jnp.mean(x * x, -1, keepdims=True) + EPSILON)
        n_ref[...] = (x * scale * gain_ref[...]).astype(BF16)

    cosine, sine = cos_ref[...], sin_ref[...]
    q = rotated(project_rows(n_ref, where_ref, (wq0, wq1, wq2)), cosine, sine, 1.0)
    q_ref[...] = q.astype(BF16) * jnp.asarray(1.0 / math.sqrt(HEAD), BF16)
    k = rotated(project_rows(n_ref, where_ref, (wk0, wk1, wk2)), cosine, sine, 1.0)
    k_ref[...] = k.astype(BF16)
    v_ref[...] = project_rows(n_ref, where_ref, (wv0, wv1, wv2)).astype(BF16)
    nt_ref[...] = nt(order_ref[...], n_ref[...]).astype(BF16)


def project_earlier_kernel(where_ref, x_ref, gain_ref, wk0, wk1, wk2, wv0, wv1, wv2, cos_ref, sin_ref,
                           k_ref, v_ref, n_ref):
    @pl.when(where_ref[0] != 0)
    def _():
        @pl.when(pl.program_id(0) == 0)
        def _():
            x = x_ref[...].astype(F32)
            scale = lax.rsqrt(jnp.mean(x * x, -1, keepdims=True) + EPSILON)
            n_ref[...] = (x * scale * gain_ref[...]).astype(BF16)

        k = rotated(project_rows(n_ref, where_ref, (wk0, wk1, wk2)), cos_ref[...], sin_ref[...], 1.0)
        k_ref[...] = k.astype(BF16)
        v_ref[...] = project_rows(n_ref, where_ref, (wv0, wv1, wv2)).astype(BF16)

    @pl.when(where_ref[0] == 0)
    def _():
        k_ref[...] = jnp.zeros_like(k_ref)
        v_ref[...] = jnp.zeros_like(v_ref)


def weight_specs(rows, n, first):
    packed = pl.BlockSpec((rows // 2, n), lambda i: (0, first // n + i))
    return [pl.BlockSpec((rows, n), lambda i: (0, i)), packed, packed]


def project(where, x, gain, wq, wk, wv, pack, cosine, sine, order):
    tokens, width = x.shape
    steps = 4
    half = width // 2
    nq, nk = wq.shape[1], wk.shape[1]
    qb, kb = nq // steps, nk // steps
    o_spec = lambda n: pl.BlockSpec((tokens, n), lambda i: (0, i))
    shape = jax.ShapeDtypeStruct
    return pallas(
        project_kernel,
        grid=(steps,),
        in_specs=[SCALAR, whole((tokens, width)), whole((1, width)),
                  *weight_specs(half, qb, 0), *weight_specs(half, kb, 0), *weight_specs(half, kb, nk),
                  whole((tokens, LANES)), whole((tokens, LANES)),
                  pl.BlockSpec((width // steps, width), lambda i: (i, 0))],
        out_specs=[pl.BlockSpec((tokens, width), lambda i: (0, 0)), o_spec(qb), o_spec(kb), o_spec(kb),
                   pl.BlockSpec((width // steps, tokens), lambda i: (i, 0))],
        out_shape=[shape((tokens, width), BF16), shape((tokens, nq), BF16), shape((tokens, nk), BF16),
                   shape((tokens, nk), BF16), shape((width, tokens), BF16)],
        compiler_params=params(62),
        cost_estimate=cost(3),
        name="project",
    )(where, x, gain, wq, *pack[0], wk, *pack[1], wv, *pack[1], cosine, sine, order)


def project_earlier(where, x, gain, wk, wv, pack, cosine, sine):
    tokens, width = x.shape
    steps = 2
    half = width // 2
    nk = wk.shape[1]
    kb = nk // steps
    o_spec = pl.BlockSpec((tokens, kb), lambda i: (0, i))
    shape = jax.ShapeDtypeStruct
    return pallas(
        project_earlier_kernel,
        grid=(steps,),
        in_specs=[SCALAR, whole((tokens, width)), whole((1, width)),
                  *weight_specs(half, kb, 0), *weight_specs(half, kb, nk),
                  whole((tokens, LANES)), whole((tokens, LANES))],
        out_specs=[o_spec, o_spec],
        out_shape=[shape((tokens, nk), BF16), shape((tokens, nk), BF16)],
        scratch_shapes=[pltpu.VMEM((tokens, width), BF16)],
        compiler_params=params(62),
        cost_estimate=cost(0.1),
        name="project_earlier",
    )(where, x, gain, wk, *pack[1], wv, *pack[1], cosine, sine)


def lane_half(shape, which):
    lane = lax.broadcasted_iota(jnp.int32, shape, 1)
    return ((lane // HEAD) % 2 == which).astype(F32)


def doubled(tile, which):
    kept = tile.astype(F32) * lane_half(tile.shape, which)
    return kept + pltpu.roll(kept, HEAD, 1)


def fill_bias(bias, prefix_ref, g):
    shape = bias.shape
    key = lax.broadcasted_iota(jnp.int32, shape, 0)
    query = lax.broadcasted_iota(jnp.int32, shape, 1) % shape[0]
    seen = (key <= query) | (key + g * shape[0] < prefix_ref[0])
    bias[...] = jnp.where(seen, 0.0, MASKED)


def stacked_heads(tile):
    tile = tile.astype(F32)
    return jnp.concatenate([(tile * lane_half(tile.shape, a)).astype(BF16) for a in range(2)], 0)


def attend_kernel(g_ref, prefix_ref, q_ref, k0_ref, v0_ref, k1_ref, v1_ref, o_ref, lse_ref, bias):
    g = g_ref[0]
    which = pl.program_id(0) % 2

    @pl.when(pl.program_id(0) == 0)
    def _():
        fill_bias(bias, prefix_ref, g)

    away = jnp.where(g == 0, -MASKED, 0.0)
    tokens = q_ref.shape[0]
    q = stacked_heads(q_ref[...])
    keys = jnp.concatenate([doubled(k[...], which).astype(BF16) for k in (k0_ref, k1_ref)], 0)
    values = jnp.concatenate([doubled(v[...], which).T[:HEAD].astype(BF16) for v in (v0_ref, v1_ref)], 1)
    scores = nt(keys, q)
    own, early = scores[:tokens] + bias[...], scores[tokens:]
    peak = jnp.maximum(jnp.max(own, 0, keepdims=True), jnp.max(early, 0, keepdims=True) - away)
    own, early = jnp.exp(own - peak), jnp.exp(early - (peak + away))
    total = jnp.sum(own, 0, keepdims=True) + jnp.sum(early, 0, keepdims=True)
    out = nn(values, jnp.concatenate([own.astype(BF16), early.astype(BF16)], 0)) * (1.0 / total)
    lse = peak + jnp.log(total)
    lse_ref[0, 0:1, :] = lse[:, :tokens]
    lse_ref[0, 1:2, :] = lse[:, tokens:]
    o_ref[...] = jnp.concatenate([out[:, :tokens], out[:, tokens:]], 0).T.astype(BF16)


def attend(g, prefix, q, k0, v0, k1, v1):
    tokens = q.shape[0]
    kv = pl.BlockSpec((tokens, 128), lambda i: (0, i // 2))
    qs = pl.BlockSpec((tokens, 128), lambda i: (0, i))
    return pallas(
        attend_kernel,
        grid=(KV_HEADS,),
        in_specs=[SCALAR, SCALAR, qs, kv, kv, kv, kv],
        out_specs=[qs, pl.BlockSpec((1, 8, tokens), lambda i: (i, 0, 0))],
        out_shape=[jax.ShapeDtypeStruct(q.shape, BF16), jax.ShapeDtypeStruct((KV_HEADS, 8, tokens), F32)],
        scratch_shapes=[pltpu.VMEM((tokens, 2 * tokens), F32)],
        compiler_params=params(62),
        cost_estimate=cost(0.1),
        name="attend",
    )(g, prefix, q, k0, v0, k1, v1)


def attend_back_kernel(g_ref, prefix_ref, q_ref, k0_ref, v0_ref, k1_ref, v1_ref, do_ref, lse_ref,
                       cos_ref, sin_ref, dq_ref, own_ref, early_ref, bias):
    g = g_ref[0]
    which = pl.program_id(0) % 2

    @pl.when(pl.program_id(0) == 0)
    def _():
        fill_bias(bias, prefix_ref, g)

    away = jnp.where(g == 0, -MASKED, 0.0)
    tokens = q_ref.shape[0]
    q, do = stacked_heads(q_ref[...]), stacked_heads(do_ref[...])
    keys = [doubled(k[...], which) for k in (k0_ref, k1_ref)]
    keys_t = jnp.concatenate([k.T[:HEAD].astype(BF16) for k in keys], 1)
    keys = jnp.concatenate([k.astype(BF16) for k in keys], 0)
    values = jnp.concatenate([doubled(v[...], which).astype(BF16) for v in (v0_ref, v1_ref)], 0)
    lse = jnp.concatenate([lse_ref[0, 0:1, :], lse_ref[0, 1:2, :]], 1)
    scores = nt(keys, q)
    probs = jnp.concatenate(
        [jnp.exp(scores[:tokens] + bias[...] - lse), jnp.exp(scores[tokens:] - (lse + away))], 0)
    dprobs = nt(values, do)
    delta = jnp.sum(probs * dprobs, 0, keepdims=True)
    dscores = (probs * (dprobs - delta)).astype(BF16)
    dv = nn(probs.astype(BF16), do)
    dk = nn(dscores, q)
    dq = nn(keys_t, dscores)
    dq = jnp.concatenate([dq[:, :tokens], dq[:, tokens:]], 0).T * (1.0 / math.sqrt(HEAD))
    dq_ref[...] = rotated(dq, cos_ref[...], sin_ref[...], -1.0).astype(BF16)
    for row, grad in enumerate((dk, dv)):
        both = grad + pltpu.roll(grad, HEAD, 1)
        part = both * lane_half(both.shape, which)
        for ref, rows in ((own_ref, slice(0, tokens)), (early_ref, slice(tokens, 2 * tokens))):

            @pl.when(which == 0)
            def _():
                ref[row] = part[rows].astype(ref.dtype)

            @pl.when(which != 0)
            def _():
                ref[row] = (ref[row].astype(F32) + part[rows]).astype(ref.dtype)


def attend_back(g, prefix, q, k0, v0, k1, v1, do, lse, cosine, sine, first, count):
    tokens = q.shape[0]
    kv = pl.BlockSpec((tokens, LANES), lambda i: (0, first // 2 + i // 2))
    qs = pl.BlockSpec((tokens, LANES), lambda i: (0, first + i))
    both = pl.BlockSpec((2, tokens, LANES), lambda i: (0, 0, i // 2))
    shape = jax.ShapeDtypeStruct
    kv_shape = (2, tokens, count * HEAD)
    return pallas(
        attend_back_kernel,
        grid=(count,),
        in_specs=[SCALAR, SCALAR, qs, kv, kv, kv, kv, qs,
                  pl.BlockSpec((1, 8, tokens), lambda i: (first + i, 0, 0)),
                  whole((tokens, LANES)), whole((tokens, LANES))],
        out_specs=[pl.BlockSpec((tokens, LANES), lambda i: (0, i)), both, both],
        out_shape=[shape((tokens, count * LANES), BF16), shape(kv_shape, F32), shape(kv_shape, BF16)],
        scratch_shapes=[pltpu.VMEM((tokens, 2 * tokens), F32)],
        compiler_params=params(28),
        cost_estimate=cost(12),
        name="attend_back",
    )(g, prefix, q, k0, v0, k1, v1, do, lse, cosine, sine)


def output_kernel(where_ref, a_ref, wo0, wo1, wo2, x_ref, gain_ref, res_ref, n_ref):
    res = x_ref[...].astype(F32) + project_rows(a_ref, where_ref, (wo0, wo1, wo2))
    res_ref[...] = res
    scale = lax.rsqrt(jnp.mean(res * res, -1, keepdims=True) + EPSILON)
    n_ref[...] = (res * scale * gain_ref[...]).astype(BF16)


def halves_spec(w):
    shape = (w.shape[0] // 2, w.shape[1])
    return [pl.BlockSpec(shape, lambda *_, n=n: (n, 0), pipeline_mode=pl.Buffered(1)) for n in range(2)]


def output(where, attended, wo, x, gain):
    tokens, width = x.shape
    rows = 256
    row = pl.BlockSpec((rows, width), lambda i: (i, 0))
    return pallas(
        output_kernel,
        grid=(tokens // rows,),
        in_specs=[SCALAR, row, whole(wo[0].shape), *halves_spec(wo[1]), row, whole((1, width))],
        out_specs=[row, row],
        out_shape=[jax.ShapeDtypeStruct((tokens, width), F32), jax.ShapeDtypeStruct((tokens, width), BF16)],
        compiler_params=params(),
        cost_estimate=cost(0.1),
        name="output",
    )(where, attended, *wo, wo[1], x, gain)


def gates_of(rows, router_t, member):
    logits = jnp.where(member > 0.0, nt(rows, router_t), MASKED)
    peak = jnp.max(logits, -1, keepdims=True)
    weights = jnp.where(member > 0.0, jnp.exp(logits - peak), 0.0)
    return weights / jnp.sum(weights, -1, keepdims=True)


def experts_kernel(*refs, first, start, adding, carrying, final):
    refs = list(refs)
    take = lambda n: [refs.pop(0) for _ in range(n)]
    g_ref, x, c = take(3)
    if first:
        member, router, order_in = take(3)
    else:
        gates, xt_in, ct_in = take(3)
    win, wout = take(2)
    olds_in = [take(2) for _ in adding]
    grad_in, sum_in, gg_in = take(3) if carrying else (None, None, None)
    keep, send, grad, total = take(4)
    gg_out = None if final else take(1)[0]
    if first:
        gates, xt_out, ct_out = take(3)
    hid_scr, dgu_scr, grad_scr, sum_scr, gg_scr, xt, ct, sems = take(8)
    order = take(1)[0] if first else None
    keep_old, send_old = take(2) if adding else (None, None)
    grad_low, sum_low = take(2) if final else (grad_scr, sum_scr)
    step = pl.program_id(0)
    at_start, at_end = step == 0, step == pl.num_programs(0) - 1
    width = x.shape[1]
    column = g_ref[0] * (EXPERTS // 2) + start + step
    copy = lambda n, source, target: pltpu.make_async_copy(source, target, sems.at[n])
    loads = [copy(0, order_in, order)] if first else [copy(0, xt_in, xt), copy(1, ct_in, ct)]
    sums_in = [copy(2, grad_in, grad_scr), copy(3, sum_in, sum_scr)] if carrying else []
    olds = []
    for (keep_in, send_in), (skip, _) in zip(olds_in, adding):
        olds += [copy(4, keep_in.at[step + skip], keep_old), copy(5, send_in.at[step + skip], send_old)]
    sums_out = [copy(6, grad_low, grad), copy(7, sum_low, total)]
    turned_out = [copy(8, xt, xt_out), copy(9, ct, ct_out)] if first else []

    @pl.when(at_start)
    def _():
        for load in loads + sums_in:
            load.start()
        if first:
            gates[...] = gates_of(x[...], router[...], member[...])
        gg_scr[...] = gg_in[...] if carrying else jnp.zeros_like(gg_scr)

    for old in olds:
        old.start()
    probs = gates[...]
    mine = lax.broadcasted_iota(jnp.int32, probs.shape, 1) == column
    p = jnp.sum(jnp.where(mine, probs, 0.0), 1, keepdims=True)
    gate_up = nn(x[...], win[0])
    back = nn(c[...], wout[0])
    gate, up = gate_up[:, :FF], gate_up[:, FF:]
    sig = 1.0 / (1.0 + jnp.exp(-gate))
    act = gate * sig
    hid = act * up
    gg_scr[...] = jnp.where(mine, jnp.sum(hid * back, 1, keepdims=True), gg_scr[...])
    back = back * p
    dgate = back * up * (sig * (1.0 + gate * (1.0 - sig)))
    hid_scr[...] = (hid * p).astype(BF16)
    dgu_scr[:, :FF] = dgate.astype(BF16)
    dgu_scr[:, FF:] = (back * act).astype(BF16)

    if carrying:

        @pl.when(at_start)
        def _():
            for load in sums_in:
                load.wait()

    for scr, value in ((sum_scr, nt(hid_scr[...], wout[0])), (grad_scr, nt(dgu_scr[...], win[0]))):
        if carrying:
            scr[...] += value
        else:

            @pl.when(at_start)
            def _():
                scr[...] = value

            @pl.when(jnp.logical_not(at_start))
            def _():
                scr[...] += value

    @pl.when(at_end)
    def _():
        if final:
            sum_low[...] = sum_scr[...].astype(BF16)
            grad_low[:, :width] = grad_scr[...].astype(BF16)
            grad_low[:, width:] = gg_scr[...].astype(BF16)
        else:
            gg_out[...] = gg_scr[...]
        for store in sums_out:
            store.start()

    @pl.when(at_start)
    def _():
        for load in loads:
            load.wait()
        if first:
            xt[...] = nt(order[...], x[...]).astype(BF16)
            ct[...] = nt(order[...], c[...]).astype(BF16)
            for store in turned_out:
                store.start()

    for old in olds:
        old.wait()
    for out, old, base in ((keep, keep_old, 0), (send, send_old, width // 2)):
        rows = pl.ds(base, width // 2)
        for cols, left, right in ((slice(0, 2 * FF), xt, dgu_scr), (slice(2 * FF, 3 * FF), ct, hid_scr)):
            value = nn(left[rows], right[...])
            if adding:
                value = value + old[:, cols].astype(F32)
            out[0, :, cols] = value.astype(BF16)

    @pl.when(at_end)
    def _():
        for store in sums_out + turned_out:
            store.wait()


def experts(g, x, c, win, wout, start, count, fresh=None, known=None, adding=(), carrying=None, final=False):
    tokens, width = x.shape
    cols = 3 * FF
    shape = jax.ShapeDtypeStruct
    half = pl.BlockSpec((1, width // 2, cols), lambda i: (i, 0, 0))
    anywhere = pl.BlockSpec(memory_space=pl.ANY)
    wide, narrow, turned = (tokens, width), (tokens, LANES), (width, tokens)
    back = (tokens, width + LANES)
    args = [g, x, c, *(fresh or known), win, wout]
    specs = [SCALAR, whole(wide), whole(wide)]
    specs += [whole(narrow), whole(fresh[1].shape), anywhere] if fresh else [whole(narrow), anywhere, anywhere]
    specs += [pl.BlockSpec((1, width, 2 * FF), lambda i: (start + i, 0, 0)),
              pl.BlockSpec((1, width, FF), lambda i: (start + i, 0, 0))]
    for keep, send, _, _ in adding:
        args += [keep, send]
        specs += [anywhere, anywhere]
    if carrying:
        args += carrying
        specs += [anywhere, anywhere, whole(narrow)]
    outs = [half, half, anywhere, anywhere]
    shapes = [shape((count, width // 2, cols), BF16), shape((count, width // 2, cols), BF16)]
    if final:
        shapes += [shape(back, BF16), shape(wide, BF16)]
    else:
        outs += [whole(narrow)]
        shapes += [shape(wide, F32), shape(wide, F32), shape(narrow, F32)]
    if fresh:
        outs += [whole(narrow), anywhere, anywhere]
        shapes += [shape(narrow, F32), shape(turned, BF16), shape(turned, BF16)]
    scratch = [pltpu.VMEM((tokens, FF), BF16), pltpu.VMEM((tokens, 2 * FF), BF16),
               pltpu.VMEM(wide, F32), pltpu.VMEM(wide, F32), pltpu.VMEM(narrow, F32),
               pltpu.VMEM(turned, BF16), pltpu.VMEM(turned, BF16), pltpu.SemaphoreType.DMA((10,))]
    if fresh:
        scratch += [pltpu.VMEM((width, width), BF16)]
    if adding:
        scratch += [pltpu.VMEM((width // 2, cols), BF16)] * 2
    if final:
        scratch += [pltpu.VMEM(back, BF16), pltpu.VMEM(wide, BF16)]
    return pallas(
        functools.partial(experts_kernel, first=fresh is not None, start=start,
                          adding=tuple(entries for _, _, *entries in adding),
                          carrying=carrying is not None, final=final),
        grid=(count,),
        in_specs=specs,
        out_specs=outs,
        out_shape=shapes,
        scratch_shapes=scratch,
        compiler_params=params(62),
        cost_estimate=cost((3 if adding and carrying else 8) * count),
        name="experts",
    )(*args)


def middle_kernel(where_ref, c_ref, grad_ref, back_ref, gg_ref, p_ref, router_ref, res_ref, gain_ref,
                  wo0, wo1, wo2, dres_ref, low_ref, da_ref, dl_ref, dgain_ref):
    width = c_ref.shape[1]
    p = p_ref[...]
    gg = gg_ref[...] + back_ref[:, width:].astype(F32)
    dlogits = p * (gg - jnp.sum(p * gg, 1, keepdims=True))
    dl_ref[...] = dlogits.astype(BF16)
    high = dlogits.astype(BF16)
    rest = (dlogits - high.astype(F32)).astype(BF16)
    router = router_ref[...]
    grad = grad_ref[...] + back_ref[:, :width].astype(F32) + (nn(high, router) + nn(rest, router))
    res = res_ref[...]
    scale = lax.rsqrt(jnp.mean(res * res, -1, keepdims=True) + EPSILON)
    part = jnp.broadcast_to(jnp.sum(grad * (res * scale), 0, keepdims=True), dgain_ref.shape)

    @pl.when(pl.program_id(0) == 0)
    def _():
        dgain_ref[...] = part

    @pl.when(pl.program_id(0) != 0)
    def _():
        dgain_ref[...] += part

    w = grad * gain_ref[...]
    dres = c_ref[...].astype(F32) + (scale * w - res * (scale * scale * scale)
                                     * jnp.mean(w * res, -1, keepdims=True))
    dres_ref[...] = dres
    low = dres.astype(BF16)
    low_ref[...] = low
    for at, wo in zip(pieces(where_ref, width), (wo0, wo1, wo2)):
        da_ref[:, at] = nt(low, wo[...]).astype(BF16)


def middle(where, c, grad, back, gg, p, router_t, res, gain, wo):
    tokens, width = c.shape
    rows = 256
    row = lambda n: pl.BlockSpec((rows, n), lambda i: (i, 0))
    shape = jax.ShapeDtypeStruct
    return pallas(
        middle_kernel,
        grid=(tokens // rows,),
        in_specs=[SCALAR, row(width), row(width), row(width + LANES), row(LANES), row(LANES),
                  whole((LANES, width)), row(width), whole((1, width)), whole(wo[0].shape), *halves_spec(wo[1])],
        out_specs=[row(width), row(width), row(width), row(LANES), pl.BlockSpec((8, width), lambda i: (0, 0))],
        out_shape=[shape((tokens, width), F32), shape((tokens, width), BF16), shape((tokens, width), BF16),
                   shape((tokens, LANES), BF16), shape((8, width), F32)],
        compiler_params=params(),
        cost_estimate=cost(100),
        name="middle",
    )(where, c, grad, back, gg, p, router_t, res, gain, *wo, wo[1])


def weight_kernel(*refs, joined):
    refs = list(refs)
    take = lambda n: [refs.pop(0) for _ in range(n)]
    xt, dq, own, early, cos, sin = take(6)
    order, low, att, xt_ffn, dlogits, dgain = take(6) if joined else [None] * 6
    keep, dkv, send = take(3)
    half = keep.shape[0]
    dk = rotated(own[0] + early[0].astype(F32), cos[...], sin[...], -1.0).astype(BF16)
    dv = (own[1] + early[1].astype(F32)).astype(BF16)
    nq, nk = dq.shape[1], dk.shape[1]
    dkv[:, :nk] = dk
    dkv[:, nk:] = dv
    if joined:
        low_t, gain_rows = take(2)
        low_t[...] = nt(order[...], low[...]).astype(BF16)
        row = lax.broadcasted_iota(jnp.int32, gain_rows.shape, 0)
        gain_rows[...] = jnp.where(row == EXPERTS, dgain[0:1, :], 0.0).astype(BF16)
    def put(cols, rows, value):
        (keep if rows.start == 0 else send)[:, cols] = value.astype(BF16)

    for base in (0, half):
        rows = pl.ds(base, half)
        put(slice(0, nq), rows, nn(xt[rows], dq[...]))
        first = nq + 2 * nk
        put(slice(nq, first), rows, nn(xt[rows], dkv[...]))
        if joined:
            wide = att.shape[1]
            put(slice(first, first + wide), rows, nn(low_t[rows], att[...]))
            put(slice(first + wide, first + wide + LANES), rows,
                nn(xt_ffn[rows], dlogits[...]) + nt(order[rows], gain_rows[...]))


def weight_grads(xt, dq, own, early, cosine, sine, joined=None):
    width, tokens = xt.shape
    nq, nk = dq.shape[1], own.shape[2]
    shape = jax.ShapeDtypeStruct
    cols = nq + 2 * nk + (joined[2].shape[1] + LANES if joined else 0)
    out = shape((width // 2, cols), BF16)
    vmem = pl.BlockSpec(memory_space=pltpu.VMEM)
    args = (xt, dq, own, early, cosine, sine, *(joined or ()))
    return pallas(
        functools.partial(weight_kernel, joined=bool(joined)),
        in_specs=[vmem] * len(args),
        out_specs=[vmem] * 3,
        out_shape=[out, shape((tokens, 2 * nk), BF16), out],
        scratch_shapes=[pltpu.VMEM((width, tokens), BF16), pltpu.VMEM((LANES, width), BF16)] if joined else [],
        compiler_params=params(),
        cost_estimate=cost(0.1 if joined else 60),
        name="weight_grads",
    )(*args)


def input_kernel(where_ref, *refs, parts):
    refs = list(refs)
    take = lambda n: [refs.pop(0) for _ in range(n)]
    dqs, dkvs, wq, wk, wv = take(parts), take(parts), take(1), take(1), take(1)
    packs = take(4)
    x_ref, gain_ref, dres_ref, out_ref, grad = refs
    nq, nk = wq[0].shape[1], wk[0].shape[1]
    columns = []
    for n in range(parts):
        q0, k0 = n * nq // parts, n * nk // parts
        q1, k1 = q0 + nq // parts, k0 + nk // parts
        dkv = dkvs[n][...]
        half = dkv.shape[1] // 2
        for left, own, first, (lo, hi) in (
                (dqs[n][...], wq[0], None, (q0, q1)),
                (dkv[:, :half], wk[0], 0, (k0, k1)),
                (dkv[:, half:], wv[0], nk, (k0, k1))):
            packed = slice(lo, hi) if first is None else slice(first + lo, first + hi)
            columns.append((left, own, slice(lo, hi), (first is not None, packed)))
    at = pieces(where_ref, x_ref.shape[1])
    grad[:, at[0]] = sum(nt(left, own[:, mine]) for left, own, mine, _ in columns)
    for place, pack in zip(at[1:], (packs[0::2], packs[1::2])):
        grad[:, place] = sum(nt(left, pack[which][:, packed]) for left, _, _, (which, packed) in columns)
    x = x_ref[...].astype(F32)
    scale = lax.rsqrt(jnp.mean(x * x, -1, keepdims=True) + EPSILON)
    w = grad[...] * gain_ref[...]
    out_ref[...] = dres_ref[...] + (scale * w - x * (scale * scale * scale) * jnp.mean(w * x, -1, keepdims=True))


def input_grads(where, dqs, dkvs, wq, wk, wv, pack, x, gain, dres):
    tokens, width = x.shape
    rows = 256
    row = lambda a: pl.BlockSpec((rows, a.shape[1]), lambda i: (i, 0))
    weights = (wq, wk, wv, *pack[0], *pack[1])
    return pallas(
        functools.partial(input_kernel, parts=len(dqs)),
        grid=(tokens // rows,),
        in_specs=[SCALAR, *map(row, dqs), *map(row, dkvs), *(whole(w.shape) for w in weights), row(x),
                  whole((1, width)), row(dres)],
        out_specs=row(dres),
        out_shape=jax.ShapeDtypeStruct((tokens, width), F32),
        scratch_shapes=[pltpu.VMEM((rows, width), F32)],
        compiler_params=params(),
        cost_estimate=cost(5),
        name="input_grads",
    )(where, *dqs, *dkvs, *weights, x, gain, dres)


def exchange(value, *bits):
    count = lax.axis_size("replica")
    flip = sum(count if b == "group" else 1 << b for b in bits)
    return lax.ppermute(value, ("group", "replica"), [(i, i ^ flip) for i in range(2 * count)])


def after(value, *others):
    out = lax.optimization_barrier((value, *others))
    return out[0], list(out[1:])


def deal(out, to, entries, rows):
    def some(source, target, size):
        value = sum(p[e, pl.ds(source, size), :].astype(F32) for p, e in entries)
        out[to, pl.ds(target, size), :] = value.astype(BF16)

    at = 0
    for start, total in rows:
        step = 32
        if total % step == 0 and total > step and start % step == 0 and at % step == 0:

            @pl.loop(0, total // step)
            def _(i, start=start, at=at):
                some(pl.multiple_of(start + i * step, step), pl.multiple_of(at + i * step, step), step)

        else:
            some(start, at, total)
        at += total


def deal_entries(out, to, parts, firsts, count, rows):
    @pl.loop(0, count)
    def _(n):
        deal(out, to + n, [(p, first + n) for p, first in zip(parts, firsts)], rows)


def split_kernel(*refs, groups):
    refs = list(refs)
    parts = [[refs.pop(0) for _ in firsts] for firsts, _, _, _, _ in groups]
    for part, (firsts, count, outs, to, ranges) in zip(parts, groups):
        for out, rows in zip(outs, ranges):
            deal_entries(refs[out], to, part, firsts, count, rows)


def stream_kernel(*refs, count, pieces):
    parts, outs = refs[:count], list(refs[count:])
    for first, size, ranges in pieces:
        mine = [outs.pop(0) for _ in ranges]

        @pl.when((pl.program_id(0) >= first) & (pl.program_id(0) < first + size))
        def _():
            for out, rows in zip(mine, ranges):
                deal(out, 0, [(p, 0) for p in parts], rows)


def ranges_of(axes, chunk, bits):
    spots = np.stack(np.unravel_index(np.arange(2 ** len(axes)), (2,) * len(axes)), 1)
    at = [axes.index(b) for b in bits]
    ranges = []
    for combo in np.ndindex(*(2,) * len(bits)):
        rows = []
        for n in np.nonzero((spots[:, at] == combo).all(1))[0]:
            if rows and rows[-1][0] + rows[-1][1] == n * chunk:
                rows[-1] = (rows[-1][0], rows[-1][1] + chunk)
            else:
                rows.append((int(n) * chunk, chunk))
        ranges.append(tuple(rows))
    return tuple(ranges)


def flips_of(bits):
    return [[b for b, on in zip(bits, combo) if on] for combo in list(np.ndindex(*(2,) * len(bits)))[1:]]


class Run:
    def __init__(self, parts, axes, chunk, first=0, count=1):
        self.parts, self.axes, self.chunk, self.first, self.count = list(parts), list(axes), chunk, first, count


def firsts_of(run):
    return tuple(run.first if p.shape[0] > run.count else 0 for p in run.parts)


def split_call(groups, args, shapes):
    vmem = pl.BlockSpec(memory_space=pltpu.VMEM)
    return pallas(
        functools.partial(split_kernel, groups=tuple(groups)),
        in_specs=[vmem] * len(args),
        out_specs=[vmem] * len(shapes),
        out_shape=[jax.ShapeDtypeStruct(shape, BF16) for shape in shapes],
        compiler_params=params(),
        cost_estimate=cost(0.1),
        name="split",
    )(*args)


def split(runs, bit):
    axes, chunk = runs[0].axes, runs[0].chunk
    ranges = ranges_of(axes, chunk, (bit,))
    total, groups = 0, []
    for run in runs:
        groups.append((firsts_of(run), run.count, (0, 1), total, ranges))
        total += run.count
    shapes = [(total, sum(n for _, n in rows), runs[0].parts[0].shape[2]) for rows in ranges]
    kept, send = split_call(groups, [p for run in runs for p in run.parts], shapes)
    return Run([kept, exchange(send, bit)], [b for b in axes if b != bit], chunk, 0, total)


def split_each(*pieces):
    groups, shapes = [], []
    for run, bit in pieces:
        ranges = ranges_of(run.axes, run.chunk, (bit,))
        groups.append((firsts_of(run), run.count, (len(shapes), len(shapes) + 1), 0, ranges))
        shapes += [(run.count, sum(n for _, n in rows), run.parts[0].shape[2]) for rows in ranges]
    outs = list(split_call(groups, [p for run, _ in pieces for p in run.parts], shapes))
    made = []
    for run, bit in pieces:
        kept, send = outs.pop(0), outs.pop(0)
        made.append(Run([kept, exchange(send, bit)], [b for b in run.axes if b != bit], run.chunk, 0, run.count))
    return made


def split_apart(run, *pieces):
    rows, cols = run.parts[0].shape[1:]
    blocks = 2 if run.count > 2 and cols % (2 * LANES) == 0 else 1
    wide = cols // blocks
    shapes, specs, plan, first = [], [], [], 0
    for bits, count in pieces:
        ranges = ranges_of(run.axes, run.chunk, bits)
        plan.append((first, count, ranges))
        for chosen in ranges:
            size = sum(n for _, n in chosen)
            shapes.append(jax.ShapeDtypeStruct((count, size, cols), BF16))

            def place(i, j, first=first, count=count):
                column = jnp.where(i < first, 0, jnp.where(i >= first + count, blocks - 1, j))
                return jnp.clip(i - first, 0, count - 1), 0, column

            specs.append(pl.BlockSpec((1, size, wide), place))
        first += count
    outs = list(pallas(
        functools.partial(stream_kernel, count=len(run.parts), pieces=tuple(plan)),
        grid=(first, blocks),
        in_specs=[pl.BlockSpec((1, rows, wide), lambda i, j: (i, 0, j))] * len(run.parts),
        out_specs=specs,
        out_shape=shapes,
        compiler_params=params(62 if first > 2 else 24),
        cost_estimate=cost(0.1),
        name="split_apart",
    )(*run.parts))
    runs = []
    for bits, count in pieces:
        kept = outs.pop(0)
        received = [exchange(outs.pop(0), *flip) for flip in flips_of(bits)]
        runs.append(Run([kept, *received], [b for b in run.axes if b not in bits], run.chunk, 0, count))
    return runs


def block_sum(residual, own, other):
    def kernel(a, b, c, out):
        out[...] = (a[...] + b[...] + c[...].astype(F32)).astype(BF16)

    tokens, width = residual.shape
    row = pl.BlockSpec((tokens // 4, width), lambda i: (i, 0))
    return pallas(
        kernel,
        grid=(4,),
        in_specs=[row] * 3,
        out_specs=row,
        out_shape=jax.ShapeDtypeStruct(residual.shape, BF16),
        compiler_params=params(),
        cost_estimate=cost(0.1),
        name="block_sum",
    )(residual, own, other)


def finish_attention_kernel(*refs, counts):
    refs = list(refs)
    take = lambda n: [refs.pop(0) for _ in range(n)]
    joined, alone = take(counts[0]), take(counts[1])
    wq, wk, wv, gain = take(4)
    dq, dk, dv, do, drouter, dgain_attn, dgain_ffn = refs
    a = sum(p[0].astype(F32) for p in joined)
    b = sum(p[0].astype(F32) for p in alone)
    nq, nk = wq.shape[1] // 2, wk.shape[1] // 2
    dgain = 0.0
    for n, part in enumerate((a, b)):
        for ref, w, size, first in ((dq, wq, nq, 0), (dk, wk, nk, nq), (dv, wv, nk, nq + nk)):
            grad = part[:, first : first + size]
            ref[:, n * size : (n + 1) * size] = grad
            dgain = dgain + jnp.sum(grad * w[:, n * size : (n + 1) * size].astype(F32), 1, keepdims=True)
    dgain_attn[...] = dgain / gain[...]
    first = nq + 2 * nk
    width = do.shape[0]
    do[...] = a[:, first : first + width].T
    last = a[:, first + width :]
    drouter[...] = last[:, :EXPERTS]
    lane = lax.broadcasted_iota(jnp.int32, last.shape, 1)
    dgain_ffn[...] = jnp.sum(jnp.where(lane == EXPERTS, last, 0.0), 1, keepdims=True)


def finish_attention(joined, alone, wq, wk, wv, gain, width):
    chunk = wq.shape[0]
    shape = lambda *s: jax.ShapeDtypeStruct(s, F32)
    args = (*joined, *alone, wq, wk, wv, gain)
    vmem = pl.BlockSpec(memory_space=pltpu.VMEM)
    return pallas(
        functools.partial(finish_attention_kernel, counts=(len(joined), len(alone))),
        in_specs=[vmem] * len(args),
        out_specs=[vmem] * 7,
        out_shape=[shape(chunk, wq.shape[1]), shape(chunk, wk.shape[1]), shape(chunk, wv.shape[1]),
                   shape(width, chunk), shape(chunk, EXPERTS), shape(chunk, 1), shape(chunk, 1)],
        compiler_params=params(),
        cost_estimate=cost(0.1),
        name="finish_attention",
    )(*args)


def finish_experts_kernel(g_ref, *refs):
    own, other, (win, wout) = refs[: len(refs) // 2 - 1], refs[len(refs) // 2 - 1 : -2], refs[-2:]
    count = win.shape[0] // 2
    g = g_ref[0]
    for parts, side in ((own, g), (other, 1 - g)):
        e = 0
        for p in parts:
            for n in range(p.shape[0]):
                win[side * count + e] = p[n, :, : 2 * FF].astype(F32)
                wout[side * count + e] = p[n, :, 2 * FF :].astype(F32)
                e += 1


def finish_experts(g, own, other):
    chunk = own[0].shape[1]
    shape = lambda *s: jax.ShapeDtypeStruct(s, F32)
    vmem = pl.BlockSpec(memory_space=pltpu.VMEM)
    return pallas(
        finish_experts_kernel,
        in_specs=[SCALAR] + [vmem] * (2 * len(own)),
        out_specs=[vmem] * 2,
        out_shape=[shape(EXPERTS, chunk, 2 * FF), shape(EXPERTS, chunk, FF)],
        compiler_params=params(),
        cost_estimate=cost(0.1),
        name="finish_experts",
    )(g, *own, *other)


def on_device(
    block_in, attn_gain, query_weight, key_weight, value_weight, out_weight, ffn_gain, router_weight,
    expert_in, expert_out, routes, prefix, cotangent,
):
    FOLLOWED.clear()
    replicas = lax.axis_size("replica")
    bits = replicas.bit_length() - 1
    tokens, width = block_in.shape[1:]
    half = width // 2
    chunk = half // replicas
    group, replica = lax.axis_index("group"), lax.axis_index("replica")
    core = replica % 2
    g = group.astype(jnp.int32).reshape(1)
    where = jnp.stack([group, core]).astype(jnp.int32)
    x, cot = block_in[0], cotangent[0]
    swap = lambda v: exchange(v, "group")

    def ordered(own, other, axis):
        return jnp.where(group == 0, jnp.concatenate([own, other], axis), jnp.concatenate([other, own], axis))

    quarter = lambda w: lax.dynamic_slice_in_dim(w, core * (w.shape[0] // 2), w.shape[0] // 2, 0)
    pack_q, pack_kv = quarter(query_weight), jnp.concatenate([quarter(key_weight), quarter(value_weight)], 1)
    pack_kv, (x_send, wo_send, cot_send) = after(pack_kv, x, out_weight, cot)
    pack_q, pack_kv = swap(pack_q), swap(pack_kv)
    x_early = lax.ppermute(x_send, "group", [(0, 1)])
    wo = (out_weight, swap(wo_send))
    cot_other = swap(cot_send)
    lanes = jnp.arange(LANES, dtype=jnp.int32)
    member = (routes[0][:, :, None] == lanes[None, None, :]).any(1).astype(F32)
    member_t = (routes[0].T[:, None, :] == lanes[None, :EXPERTS, None]).any(0).astype(BF16)
    small = jnp.concatenate([attn_gain[None], ffn_gain[None], router_weight.T, member_t], 0)
    small_other = swap(small)
    vectors = ordered(small[: 2 + EXPERTS], small_other[: 2 + EXPERTS], 1)
    member_other = jnp.pad(small_other[2 + EXPERTS :].T.astype(F32), ((0, 0), (0, LANES - EXPERTS)))
    gain_attn, gain_ffn = vectors[0:1].astype(F32), vectors[1:2].astype(F32)
    router_t = jnp.concatenate([vectors[2:], jnp.zeros((LANES - EXPERTS, width), BF16)], 0)

    cosine, sine, *early_tables = tables(g, tokens)
    place = np.arange(width)
    blocks, inner = place // chunk, place % chunk
    reverse = np.zeros_like(blocks)
    for b in range(bits):
        reverse |= ((blocks >> 1 >> (bits - 1 - b)) & 1) << b
    feature = ((jnp.asarray(blocks & 1, jnp.int32) ^ group) * half
               + (jnp.asarray(reverse, jnp.int32) ^ replica) * chunk + jnp.asarray(inner, jnp.int32))
    order = (feature[:, None] == jnp.arange(width, dtype=jnp.int32)[None, :]).astype(BF16)

    mine = lambda a: lax.dynamic_slice_in_dim(a, replica * chunk, chunk, 0)
    rows = (mine(query_weight), mine(key_weight), mine(value_weight), mine(attn_gain).astype(F32)[:, None])
    pack_q, (pack_kv, cosine, sine, member, order, gain_attn, member_other, *more) = after(
        pack_q, pack_kv, cosine, sine, member, order, gain_attn, member_other, *early_tables, *rows)
    early_tables, rows = more[:2], more[2:]
    pack = (pack_q, exchange(pack_q, 0)), (pack_kv, exchange(pack_kv, 0))

    _, q, k, v, normed_t = project(
        where, x, gain_attn, query_weight, key_weight, value_weight, pack, cosine, sine, order)
    k1, v1 = project_earlier(where, x_early, gain_attn, key_weight, value_weight, pack, *early_tables)
    attended, lse = attend(g, prefix, q, k, v, k1, v1)
    whole_where = jnp.stack([group, 0 * core]).astype(jnp.int32)
    residual, normed = output(whole_where, attended, wo, x, gain_ffn)
    normed_other = swap(normed)
    count = expert_in.shape[0] // 2
    near = lambda *a, **k: experts(g, normed, cot, expert_in, expert_out, *a, **k)
    far = lambda *a, **k: experts(g, *a[0], expert_in, expert_out, *a[1:], **k)
    keep, send, grad_own, sum_own, gg_own, *known = near(0, count, fresh=(member, router_t, order))
    gates, xt_own, _ = known
    normed_other, (cot_other, keep) = after(normed_other, cot_other, keep)
    keep_a, send_a, *sums, gates_o, xt_o, ct_o = far(
        (normed_other, cot_other), 0, count, fresh=(member_other, router_t, order), adding=[(keep, send, 0, count)])
    received_a = exchange(send_a, 0)
    keep, send, back, sum_other = far(
        (normed_other, cot_other), count, count, known=(gates_o, xt_o, ct_o), carrying=sums, final=True)
    back = swap(back)
    two = count // 2
    dims = [*range(1, bits), "group"]
    first, second, *rest = [*range(1, bits)]
    run_a = Run((keep_a, received_a), dims, chunk, 0, count)
    run0, run1 = split_apart(run_a, ((first,), two), ((second,), two))
    sums, run_b = (grad_own, sum_own, gg_own), []
    for part in (0, two):
        keep_b, send_b, *sums = near(
            count + part, two, known=known, adding=[(keep, send, part, two)], carrying=sums)
        run_b.append(Run((keep_b, exchange(send_b, 0)), dims, chunk, 0, two))
    grad_own, sum_own, gg_own = sums
    back, (keep_b,) = after(back, keep_b)
    run0, run1 = split_each((run0, second), (run1, first))

    grad_res, grad_low, grad_att, grad_logits, grad_gain = middle(
        whole_where, cot, grad_own, back, gg_own, gates, router_t, residual, gain_ffn, wo)
    grad_low, (sum_send,) = after(grad_low, sum_other)
    sum_other = swap(sum_send)
    (run2,), (run3,) = (split_apart(run, ((first,), two)) for run in run_b)
    heads = KV_HEADS // 2
    attn = lambda first: attend_back(g, prefix, q, k, v, k1, v1, grad_att, lse, cosine, sine, first, heads)
    to_earlier = lambda a: lax.ppermute(a, "group", [(1, 0)])
    dq0, own0, early0 = attn(0)
    early0 = to_earlier(early0)
    run_a = run0, run1
    for bit in rest:
        run_a = [split(run_a, bit)]
    dq1, own1, early1 = attn(heads)
    early1 = to_earlier(early1)
    one = lambda keep, send: Run((keep[None], exchange(send, 0)[None]), dims, chunk)
    keep0, dkv0, send0 = weight_grads(
        normed_t, dq0, own0, early0, cosine, sine,
        joined=(order, grad_low, attended, xt_own, grad_logits, grad_gain))
    attn0 = one(keep0, send0)
    run2 = split([run2], second)
    block_out = block_sum(residual, sum_own, sum_other)
    swap_a = split(run_a, "group")
    keep1, dkv1, send1 = weight_grads(normed_t, dq1, own1, early1, cosine, sine)
    attn1 = one(keep1, send1)
    order0, order1 = ["group", first, second, *rest], [first, "group", second, *rest]
    attn0 = split([attn0], order0.pop(0))
    input_grad = input_grads(where, (dq0, dq1), (dkv0, dkv1), query_weight, key_weight, value_weight, pack,
                             x, gain_attn, grad_res)
    attn1 = split([attn1], order1.pop(0))
    run3 = split([run3], second)
    for bit in rest:
        run2 = split([run2], bit)
    for _ in range(2):
        attn0 = split([attn0], order0.pop(0))
        attn1 = split([attn1], order1.pop(0))
    for bit in rest:
        run3 = split([run3], bit)
    while order0:
        attn0 = split([attn0], order0.pop(0))
        attn1 = split([attn1], order1.pop(0))
    swap_b = split([run2, run3], "group")

    query_grad, key_grad, value_grad, out_grad, router_grad, attn_gain_grad, ffn_gain_grad = finish_attention(
        attn0.parts, attn1.parts, *rows, width)
    expert_in_grad, expert_out_grad = finish_experts(
        g, (swap_a.parts[0], swap_b.parts[0]), (swap_a.parts[1], swap_b.parts[1]))
    return (
        block_out[None], input_grad[None], attn_gain_grad[:, 0], query_grad, key_grad, value_grad, out_grad,
        ffn_gain_grad[:, 0], router_grad, expert_in_grad, expert_out_grad,
    )


def solution(mesh):
    placed = (
        P("replica", "group", None),
        P("group"),
        P("group", None),
        P("group", None),
        P("group", None),
        P("group", None),
        P("group"),
        P("group", None),
        P("group", None, None),
        P("group", None, None),
        P("replica", "group", None),
        P("replica"),
        P("replica", "group", None),
    )
    both = ("group", "replica")
    return jax.shard_map(
        on_device,
        mesh=mesh,
        in_specs=placed,
        out_specs=(
            P("replica", "group", None),
            P("replica", "group", None),
            P(both),
            P(both, None),
            P(both, None),
            P(both, None),
            P(None, both),
            P(both),
            P(both, None),
            P(None, both, None),
            P(None, both, None),
        ),
        check_vma=False,
    )
```
